32 devices in a mesh: fsdp: 32 (over z, y, x, core).
Axes of the slice: x: 2, y: 2, z: 4, core: 2. Of those that a mesh axis runs over, the one named last changes fastest.
Arguments:
- hidden_in: bfloat16 [4096, 1024], P('fsdp'), may hold values from -6 to 6
- out_grad: bfloat16 [4096, 1024], P('fsdp'), may hold values from -6 to 6
- doc_ids: int32 [32, 128], P('fsdp'), may hold values from 0 to 3, never falling along the last dimension, each value on 1 to 64 neighbouring positions
- routes: int32 [4096, 6], P('fsdp'), may hold values from 0 to 63, all different within a row; in each aligned block of 128 rows (0 to 127, 128 to 255, ...) at most 16 rows name the same one
- gate_values: float32 [4096, 6], P('fsdp'), may hold values from 0.05 to 0.5
- attn_gain: bfloat16 [1024], P('fsdp'), may hold values from 0.5 to 1.5
- query_proj: bfloat16 [1024, 1536], P('fsdp'), may hold values from -0.1875 to 0.1875
- latent_proj: bfloat16 [1024, 576], P('fsdp'), may hold values from -0.1875 to 0.1875
- latent_gain: bfloat16 [512], P('fsdp'), may hold values from 0.5 to 1.5
- latent_up: bfloat16 [512, 2048], P('fsdp'), may hold values from -0.25 to 0.25
- output_proj: bfloat16 [1024, 1024], P('fsdp'), may hold values from -0.75 to 0.75
- ffn_gain: bfloat16 [1024], P('fsdp'), may hold values from 0.5 to 1.5
- shared_in: bfloat16 [1024, 2816], P('fsdp'), may hold values from -0.1875 to 0.1875
- shared_out: bfloat16 [1024, 1408], P('fsdp'), may hold values from -0.15625 to 0.15625
- expert_in: bfloat16 [128, 1024, 1408], P('fsdp'), may hold values from -0.1875 to 0.1875
- expert_out: bfloat16 [128, 704, 1024], P('fsdp'), may hold values from -0.21875 to 0.21875
Outputs:
- layer_out: bfloat16 [4096, 1024], P('fsdp')
- input_grad: float32 [4096, 1024], P('fsdp')
- grad_attn_gain: float32 [1024], P('fsdp')
- grad_query_proj: float32 [1024, 1536], P('fsdp')
- grad_latent_proj: float32 [1024, 576], P('fsdp')
- grad_latent_gain: float32 [512], P('fsdp')
- grad_latent_up: float32 [512, 2048], P('fsdp')
- grad_output_proj: float32 [1024, 1024], P('fsdp')
- grad_ffn_gain: float32 [1024], P('fsdp')
- grad_shared_in: float32 [1024, 2816], P('fsdp')
- grad_shared_out: float32 [1024, 1408], P('fsdp')
- grad_expert_in: float32 [128, 1024, 1408], P('fsdp')
- grad_expert_out: float32 [128, 704, 1024], P('fsdp')
The draws below stay inside these ranges and needn't reach their ends.
Inputs may be any that keep to these rules, and one draw needn't show every extreme that they name: `doc_ids`: each row holds document numbers that never fall; each document is 1 to 64 positions long and one is exactly 64. `routes`: A token names 6 different experts. Among the tokens of one device no expert is named more than 16 times, a bound that some block reaches; every expert is named by some token.
All inputs are finite; a program needn't handle non-finite values.
Results may differ from the reference program's by a relative error of at most 0.014.
Values may be sent and summed in bfloat16 or wider, within the bound.
No kernel may reach another device: no remote copies, remote signals or barrier semaphores. Data moves between devices by JAX's collectives and lax.ppermute only.
A program may use at most 256 MiB of HBM per device.

```python
import math
import jax
import jax.numpy as jnp
import numpy as np
from jax import lax

D = 1024
H = 8
NOPE = 128
ROPE = 64
VDIM = 128
RANK = 512
EXPERTS = 64
FF = 1408
FS = 1408
TOP = 6
TOK_DEV = 128
DOCS = 4
CAP = 16
DOC_MOST = 64
TOKENS = 4096
N_FSDP = 32


def raised(drawn, own_key, source, target, blocks, factor):
    owner, partner = [(jnp.arange(drawn.shape[dim]) // (drawn.shape[dim] // blocks)).reshape([-1 if axis == dim else 1 for axis in range(drawn.ndim)]) for dim in (source, target)]
    chosen = jax.random.permutation(own_key, blocks)[partner]
    strong = (owner == chosen) | (owner == (partner + blocks // 2) % blocks)
    return jnp.where(strong, factor * drawn, drawn)


def levels(key, extent, split, low, largest):
    factor_of, own = 1.0, jax.random.fold_in(key, 6)
    for axis_at, parts in split:
        heights = jnp.exp(jax.random.uniform(jax.random.fold_in(own, axis_at), (parts,), jnp.float32, low / len(split), largest / len(split)))
        factor_of = factor_of * jnp.repeat(heights, extent[axis_at] // parts).reshape([-1 if axis == axis_at else 1 for axis in range(len(extent))])
    return factor_of


def profile(amount, total, bound, skew):
    weights = [(1 << 20) // math.isqrt(grade ** skew) + 1 for grade in range(2, amount + 1)]
    spare, holding = total - bound - (amount - 1), [1] * (amount - 1)
    while spare > 0:
        movable = [i for i in range(amount - 1) if holding[i] < bound]
        whole, remaining = sum([weights[i] for i in movable]), spare
        for i in movable:
            addition = min(bound - holding[i], max(1, remaining * weights[i] // whole), spare)
            holding[i] = holding[i] + addition
            spare = spare - addition
    return np.array([bound] + holding)


def ragged_sizes(rng, number_of, total, bound, skew):
    if number_of == 2:
        one = jax.random.randint(rng, (), max(1, total - bound), min(bound, total - 1) + 1)
        return jnp.stack([one, total - one])
    sizes = jnp.asarray(profile(number_of, total, bound, skew), jnp.int32)
    pairs = (number_of - 1) // 2
    giver, receiver = sizes[1:1 + 2 * pairs:2], sizes[2:2 + 2 * pairs:2]
    margin = jnp.minimum(giver - 1, bound - receiver)
    passed = jax.random.randint(jax.random.fold_in(rng, 1), (pairs,), 0, 1 << 20) % (margin + 1)
    sizes = sizes.at[1:1 + 2 * pairs:2].set(giver - passed).at[2:2 + 2 * pairs:2].set(receiver + passed)
    return sizes[jax.random.permutation(jax.random.fold_in(rng, 2), number_of)]


def deal_out(stream_key, own, number, rows, count, top, bound, skew):
    sequence = jax.random.permutation(stream_key, count)
    crowded, ordinary = portions_of(count, rows * top, bound, skew, True), portions_of(count, rows * top, bound, skew, False)
    places = jnp.arange(count)

    def named(lengths, turn):
        used = int((lengths > 0).sum())
        fixed = max(1, used // 4)
        moved = fixed + (places - fixed + turn * (used - fixed)) % max(1, count - fixed)
        return jnp.zeros((count,), jnp.int32).at[sequence[jnp.where(places < fixed, places, moved)]].set(jnp.asarray(lengths, jnp.int32))

    lengths = jnp.where(number % 4 == 0, named(crowded, number // 4), named(ordinary, number - number // 4 - 1))
    mixed = jax.random.permutation(jax.random.fold_in(own, 3), count)
    donor, taker = mixed[0:count // 2 * 2:2], mixed[1:count // 2 * 2:2]
    margin = jnp.minimum(lengths[donor] - 1, bound - lengths[taker]) // 2
    margin = jnp.where((donor == sequence[0]) | (taker == sequence[0]) | (lengths[taker] == 0), 0, jnp.maximum(margin, 0))
    moved = jax.random.randint(jax.random.fold_in(own, 4), (count // 2,), 0, 1 << 20) % (margin + 1)
    lengths = lengths.at[donor].add(-moved).at[taker].add(moved)
    labels = jnp.searchsorted(jnp.cumsum(lengths), jnp.arange(rows * top), side="right").astype(jnp.int32)
    table = labels.reshape(top, rows).T
    table = table[jax.random.permutation(jax.random.fold_in(own, 1), rows)]
    turn = jax.random.randint(jax.random.fold_in(own, 2), (rows, 1), 0, top)
    return jnp.take_along_axis(table, (jnp.arange(top)[None, :] + turn) % top, axis=1)


def portions_of(number_of, total, reach, lean, full):
    portions = [(1 << 20) // math.isqrt(grade ** lean) + 1 for grade in range(1, number_of + 1)]
    largest = reach if full else min(reach, max(-(-total // number_of), total * portions[0] // sum(portions)))
    least = 1 if total - largest >= number_of - 1 else 0
    counts, spare = [largest] + [least] * (number_of - 1), total - largest - least * (number_of - 1)
    while spare > 0:
        movable = [i for i in range(1, number_of) if counts[i] < largest] or [i for i in range(1, number_of) if counts[i] < reach]
        whole, left = sum([portions[i] for i in movable]), spare
        for i in movable:
            addition = min(reach - counts[i], max(1, left * portions[i] // whole), spare)
            counts[i] = counts[i] + addition
            spare = spare - addition
    return np.array(counts)


def gaussian(stream_key, extent, scale, limit, pieces=(), held_as=jnp.bfloat16):
    loudness = levels(stream_key, extent, pieces, -0.22, 0.18) if pieces else 1.0
    drawn = jax.random.normal(stream_key, extent, jnp.float32) * scale * loudness
    return jnp.minimum(jnp.maximum(drawn, -limit), limit).astype(held_as)


def noise_with(stream_key, shape, spread, bound, split, heavy, kind=jnp.bfloat16):
    entries = spread * jax.random.normal(stream_key, shape, jnp.float32)
    if split:
        entries = entries * levels(stream_key, shape, split, -0.22, 0.18)
    return jnp.clip(raised(entries, jax.random.fold_in(stream_key, 3), *heavy), -bound, bound).astype(kind)


def setup_inputs(seed: int = 0) -> dict:
    seeds = jax.random.split(jax.random.key(seed), 17)
    hidden_in = noise_with(seeds[0], (TOKENS, D), 1.0, 6.0, ((0, 32),), (0, 1, 32, 2.75))
    out_grad = noise_with(seeds[1], (TOKENS, D), 1.0, 6.0, ((0, 32),), (0, 1, 32, 2.75))
    doc_ids = jax.vmap(lambda own: jnp.searchsorted(jnp.cumsum(ragged_sizes(own, DOCS, TOK_DEV, DOC_MOST, 2)), jnp.arange(TOK_DEV), side="right"))(jax.random.split(seeds[2], N_FSDP)).reshape((N_FSDP, TOK_DEV)).astype(jnp.int32)
    routes_keys = jax.random.split(jax.random.fold_in(seeds[3], 1), TOKENS // TOK_DEV)
    routes_turns = jax.random.permutation(jax.random.fold_in(seeds[3], 3), TOKENS // TOK_DEV)
    routes = jax.vmap(lambda own, number: deal_out(jax.random.fold_in(seeds[3], 2), own, number, TOK_DEV, EXPERTS, TOP, CAP, 2))(routes_keys, routes_turns).reshape((TOKENS, TOP))
    gate_values = jnp.clip(0.05 + 0.45 * jax.random.uniform(seeds[4], (TOKENS, TOP), jnp.float32) ** levels(seeds[4], (TOKENS, TOP), ((0, 32),), -0.2, 0.2), 0.05, 0.5)
    attn_gain = jnp.clip(1.0 + 0.1 * jax.random.normal(seeds[5], (D,), jnp.float32), 0.5, 1.5).astype(jnp.bfloat16)
    query_proj = gaussian(seeds[6], (D, H * (NOPE + ROPE)), D ** -0.5, 0.1875, ((0, 32),))
    latent_proj = gaussian(seeds[7], (D, RANK + ROPE), D ** -0.5, 0.1875, ((0, 32),))
    latent_gain = jnp.clip(1.0 + 0.1 * jax.random.normal(seeds[8], (RANK,), jnp.float32), 0.5, 1.5).astype(jnp.bfloat16)
    latent_up = gaussian(seeds[9], (RANK, H * (NOPE + VDIM)), RANK ** -0.5, 0.25, ((0, 32),))
    output_proj = gaussian(seeds[10], (D, H * VDIM), (H * VDIM // 16) ** -0.5, 0.75, ((0, 32),))
    ffn_gain = jnp.clip(1.0 + 0.1 * jax.random.normal(seeds[11], (D,), jnp.float32), 0.5, 1.5).astype(jnp.bfloat16)
    shared_in = gaussian(seeds[12], (D, 2 * FS), D ** -0.5, 0.1875, ((0, 32),))
    shared_out = gaussian(seeds[13], (D, FS), FS ** -0.5, 0.15625, ((0, 32),))
    expert_in = gaussian(seeds[14], (2 * EXPERTS, D, FF), D ** -0.5, 0.1875, ((0, 32),))
    expert_out = gaussian(seeds[15], (2 * EXPERTS, FF // 2, D), (FF // 2) ** -0.5, 0.21875, ((0, 32),))
    return {"hidden_in": hidden_in, "out_grad": out_grad, "doc_ids": doc_ids, "routes": routes, "gate_values": gate_values, "attn_gain": attn_gain, "query_proj": query_proj, "latent_proj": latent_proj, "latent_gain": latent_gain, "latent_up": latent_up, "output_proj": output_proj, "ffn_gain": ffn_gain, "shared_in": shared_in, "shared_out": shared_out, "expert_in": expert_in, "expert_out": expert_out}


EPSILON = 1e-06

def matmul(left_side, right_side):
    return jnp.dot(left_side, right_side, preferred_element_type=jnp.float32)

def product(pattern, left_side, right_side):
    return jnp.einsum(pattern, left_side.astype(jnp.float32), right_side.astype(jnp.float32))

def inverse_rms(values):
    return lax.rsqrt(lax.optimization_barrier(jnp.mean(values * values, axis=-1, keepdims=True)) + EPSILON)

def rotate(values, cosine_table, sine_table):
    middle = values.shape[-1] // 2
    first_half = values[..., :middle]
    second_half = values[..., middle:]
    return jnp.concatenate([first_half * cosine_table - second_half * sine_table, second_half * cosine_table + first_half * sine_table], axis=-1)

def unrotate(values, cosine_table, sine_table):
    middle = values.shape[-1] // 2
    first_half = values[..., :middle]
    second_half = values[..., middle:]
    return jnp.concatenate([first_half * cosine_table + second_half * sine_table, second_half * cosine_table - first_half * sine_table], axis=-1)

def swiglu_parts(pre_act):
    middle = pre_act.shape[-1] // 2
    gate_pre = pre_act[..., :middle]
    up_pre = pre_act[..., middle:]
    return (gate_pre, up_pre, jax.nn.sigmoid(gate_pre))

def swiglu_forward(pre_act):
    gate_pre, up_pre, sigmoid_gate = swiglu_parts(pre_act)
    return (gate_pre * sigmoid_gate * up_pre).astype(jnp.bfloat16)

def swiglu_backward(pre_act, grad_act):
    gate_pre, up_pre, sigmoid_gate = swiglu_parts(pre_act)
    silu_value = gate_pre * sigmoid_gate
    slope = sigmoid_gate * (1.0 + gate_pre * (1.0 - sigmoid_gate))
    return jnp.concatenate([grad_act * up_pre * slope, grad_act * silu_value], axis=-1).astype(jnp.bfloat16)

def prepare(query_raw, kv_raw, rope_key, documents):
    rows_here = query_raw.shape[0]
    indices = jnp.arange(rows_here, dtype=jnp.int32)
    same_doc = documents[:, None] == documents[None, :]
    starts = lax.optimization_barrier(jnp.min(jnp.where(same_doc, indices[None, :], rows_here), axis=1))
    allowed = same_doc & (indices[None, :] <= indices[:, None])
    position = (indices - starts).astype(jnp.float32)
    frequency = jnp.exp(jnp.arange(ROPE // 2, dtype=jnp.float32) * (-2.0 * math.log(10000.0) / ROPE))
    angles = position[:, None] * frequency[None, :]
    cosine_table = jnp.cos(angles)
    sine_table = jnp.sin(angles)
    query_heads = query_raw.reshape(rows_here, H, NOPE + ROPE)
    queries = jnp.concatenate([query_heads[..., :NOPE], rotate(query_heads[..., NOPE:], cosine_table[:, None, :], sine_table[:, None, :])], axis=-1).astype(jnp.bfloat16)
    kv_heads = kv_raw.reshape(rows_here, H, NOPE + VDIM)
    turned = rotate(rope_key, cosine_table, sine_table)
    key_rows = jnp.concatenate([kv_heads[..., :NOPE], jnp.broadcast_to(turned[:, None, :], (rows_here, H, ROPE))], axis=-1).astype(jnp.bfloat16)
    value_rows = kv_heads[..., NOPE:].astype(jnp.bfloat16)
    return (queries, key_rows, value_rows, allowed, cosine_table, sine_table)

def attend(query_raw, kv_raw, rope_key, documents):
    queries, key_rows, value_rows, allowed, cosine_table, sine_table = prepare(query_raw, kv_raw, rope_key, documents)
    scaling = (NOPE + ROPE) ** (-0.5)
    scores = product('ihd,jhd->hij', queries, key_rows) * scaling
    log_total = jnp.log(lax.optimization_barrier(jnp.sum(jnp.where(allowed[None], jnp.exp(scores), 0.0), axis=-1)))
    rounded_probs = jnp.where(allowed[None], jnp.exp(scores - log_total[..., None]), 0.0).astype(jnp.bfloat16)
    head_out = product('hij,jhd->ihd', rounded_probs, value_rows).astype(jnp.bfloat16)
    return (head_out.reshape(head_out.shape[0], H * VDIM), log_total)

def attend_back(query_raw, kv_raw, rope_key, documents, log_total, head_out, grad_heads):
    queries, key_rows, value_rows, allowed, cosine_table, sine_table = prepare(query_raw, kv_raw, rope_key, documents)
    rows_here = query_raw.shape[0]
    scaling = (NOPE + ROPE) ** (-0.5)
    scores = product('ihd,jhd->hij', queries, key_rows) * scaling
    weights = jnp.where(allowed[None], jnp.exp(scores - log_total[..., None]), 0.0)
    rounded_probs = weights.astype(jnp.bfloat16)
    grad_three = grad_heads.reshape(rows_here, H, VDIM)
    heads_three = head_out.reshape(rows_here, H, VDIM)
    grad_probs = product('ihd,jhd->hij', grad_three, value_rows)
    deltas = lax.optimization_barrier(jnp.sum(grad_three.astype(jnp.float32) * heads_three.astype(jnp.float32), axis=-1)).T
    grad_scores = (weights * (grad_probs - deltas[..., None]) * scaling).astype(jnp.bfloat16)
    grad_queries = product('hij,jhd->ihd', grad_scores, key_rows)
    grad_keys = product('hij,ihd->jhd', grad_scores, queries)
    grad_values = product('hij,ihd->jhd', rounded_probs, grad_three)
    grad_query_raw = jnp.concatenate([grad_queries[..., :NOPE], unrotate(grad_queries[..., NOPE:], cosine_table[:, None, :], sine_table[:, None, :])], axis=-1).reshape(rows_here, H * (NOPE + ROPE))
    grad_rope = unrotate(lax.optimization_barrier(jnp.sum(grad_keys[..., NOPE:], axis=1)), cosine_table, sine_table)
    grad_kv = jnp.concatenate([grad_keys[..., :NOPE], grad_values], axis=-1).reshape(rows_here, H * (NOPE + VDIM))
    return (grad_query_raw, grad_kv, grad_rope)

def reference(hidden_in, out_grad, doc_ids, routes, gate_values, attn_gain, query_proj, latent_proj, latent_gain, latent_up, output_proj, ffn_gain, shared_in, shared_out, expert_in, expert_out):
    hidden_wide = hidden_in.astype(jnp.float32)
    scale_one = inverse_rms(hidden_wide)
    norm_one = hidden_wide * scale_one
    normed_one = (norm_one * attn_gain.astype(jnp.float32)).astype(jnp.bfloat16)
    query_raw = matmul(normed_one, query_proj)
    latent_all = matmul(normed_one, latent_proj)
    latent_part = latent_all[:, :RANK]
    rope_key = latent_all[:, RANK:]
    scale_latent = inverse_rms(latent_part)
    latent_norm = latent_part * scale_latent
    latent_in = (latent_norm * latent_gain.astype(jnp.float32)).astype(jnp.bfloat16)
    kv_raw = matmul(latent_in, latent_up)

    def block_view(values):
        return values.reshape(N_FSDP, TOK_DEV, values.shape[-1])

    def forward_block(packed):
        return attend(packed[0], packed[1], packed[2], packed[3])
    head_blocks, log_blocks = lax.map(forward_block, (block_view(query_raw), block_view(kv_raw), block_view(rope_key), doc_ids))
    head_out = head_blocks.reshape(TOKENS, H * VDIM)
    mixed = hidden_wide + matmul(head_out, output_proj.T)
    scale_two = inverse_rms(mixed)
    norm_two = mixed * scale_two
    normed_two = (norm_two * ffn_gain.astype(jnp.float32)).astype(jnp.bfloat16)
    shared_pre = matmul(normed_two, shared_in)
    shared_act = swiglu_forward(shared_pre)
    shared_y = matmul(shared_act, shared_out.T)
    assigned = routes.reshape(N_FSDP, TOK_DEV * TOP)
    chosen = (assigned[..., None] == jnp.arange(EXPERTS, dtype=jnp.int32)).astype(jnp.int32)
    slot_index = lax.optimization_barrier(jnp.sum((jnp.cumsum(chosen, axis=1) - chosen) * chosen, axis=-1))
    device_ids = jnp.arange(N_FSDP, dtype=jnp.int32)[:, None]
    local_ids = jnp.arange(TOK_DEV * TOP, dtype=jnp.int32)[None, :]
    token_ids = device_ids * TOK_DEV + local_ids // TOP
    row_ids = device_ids * CAP + slot_index
    table = jnp.full((EXPERTS, N_FSDP * CAP), TOKENS, dtype=jnp.int32).at[assigned, row_ids].set(token_ids)
    gate_table = jnp.zeros((EXPERTS, N_FSDP * CAP), jnp.float32).at[assigned, row_ids].set(gate_values.reshape(N_FSDP, TOK_DEV * TOP))
    padded_in = jnp.concatenate([normed_two, jnp.zeros((1, D), jnp.bfloat16)], axis=0)
    padded_grad = jnp.concatenate([out_grad.astype(jnp.float32), jnp.zeros((1, D), jnp.float32)], axis=0)

    def expert_piece(carry, inputs):
        routed_sum, routed_grad = carry
        weight_in, weight_out, piece_id = inputs
        expert_id = piece_id // 2
        rows_used = table[expert_id]
        gate_rows = gate_table[expert_id]
        piece_rows = padded_in[rows_used]
        grad_rows = (gate_rows[:, None] * padded_grad[rows_used]).astype(jnp.bfloat16)
        pre_act = matmul(piece_rows, weight_in)
        activation = swiglu_forward(pre_act)
        piece_out = matmul(activation, weight_out).astype(jnp.bfloat16)
        grad_act = matmul(grad_rows, weight_out.T)
        grad_out = matmul(activation.T, grad_rows)
        grad_pre = swiglu_backward(pre_act, grad_act)
        grad_in = matmul(piece_rows.T, grad_pre)
        piece_dx = matmul(grad_pre, weight_in.T).astype(jnp.bfloat16)
        routed_sum = routed_sum.at[rows_used].add(gate_rows[:, None] * piece_out.astype(jnp.float32))
        routed_grad = routed_grad.at[rows_used].add(piece_dx.astype(jnp.float32))
        return ((routed_sum, routed_grad), (grad_in, grad_out))
    start_carry = (jnp.zeros((TOKENS + 1, D), jnp.float32), jnp.zeros((TOKENS + 1, D), jnp.float32))
    (routed_sum, routed_grad), (grad_expert_in, grad_expert_out) = lax.scan(expert_piece, start_carry, (expert_in, expert_out, jnp.arange(2 * EXPERTS, dtype=jnp.int32)))
    routed_y = routed_sum[:TOKENS]
    routed_dx = routed_grad[:TOKENS]
    layer_out = (mixed + shared_y + routed_y).astype(jnp.bfloat16)
    grad_shared_out = matmul(out_grad.T, shared_act)
    grad_shared_act = matmul(out_grad, shared_out)
    grad_shared_pre = swiglu_backward(shared_pre, grad_shared_act)
    grad_shared_in = matmul(normed_two.T, grad_shared_pre)
    grad_normed_two = matmul(grad_shared_pre, shared_in.T) + routed_dx
    grad_ffn_gain = lax.optimization_barrier(jnp.sum(grad_normed_two * norm_two, axis=0))
    grad_norm_two = grad_normed_two * ffn_gain.astype(jnp.float32)
    grad_mixed = out_grad.astype(jnp.float32) + scale_two * (grad_norm_two - norm_two * lax.optimization_barrier(jnp.mean(grad_norm_two * norm_two, axis=-1, keepdims=True)))
    mixed_low = grad_mixed.astype(jnp.bfloat16)
    grad_output_proj = matmul(mixed_low.T, head_out)
    grad_heads = matmul(mixed_low, output_proj).astype(jnp.bfloat16)

    def backward_block(packed):
        return attend_back(packed[0], packed[1], packed[2], packed[3], packed[4], packed[5], packed[6])
    grad_query_blocks, grad_kv_blocks, grad_rope_blocks = lax.map(backward_block, (block_view(query_raw), block_view(kv_raw), block_view(rope_key), doc_ids, log_blocks, head_blocks, block_view(grad_heads)))
    grad_query_raw = grad_query_blocks.reshape(TOKENS, H * (NOPE + ROPE)).astype(jnp.bfloat16)
    grad_kv = grad_kv_blocks.reshape(TOKENS, H * (NOPE + VDIM)).astype(jnp.bfloat16)
    grad_rope = grad_rope_blocks.reshape(TOKENS, ROPE)
    grad_latent_up = matmul(latent_in.T, grad_kv)
    grad_latent_in = matmul(grad_kv, latent_up.T)
    grad_latent_gain = lax.optimization_barrier(jnp.sum(grad_latent_in * latent_norm, axis=0))
    grad_norm_latent = grad_latent_in * latent_gain.astype(jnp.float32)
    grad_latent = scale_latent * (grad_norm_latent - latent_norm * lax.optimization_barrier(jnp.mean(grad_norm_latent * latent_norm, axis=-1, keepdims=True)))
    grad_latent_all = jnp.concatenate([grad_latent, grad_rope], axis=-1).astype(jnp.bfloat16)
    grad_query_proj = matmul(normed_one.T, grad_query_raw)
    grad_latent_proj = matmul(normed_one.T, grad_latent_all)
    grad_normed_one = matmul(grad_query_raw, query_proj.T) + matmul(grad_latent_all, latent_proj.T)
    grad_attn_gain = lax.optimization_barrier(jnp.sum(grad_normed_one * norm_one, axis=0))
    grad_norm_one = grad_normed_one * attn_gain.astype(jnp.float32)
    input_grad = grad_mixed + scale_one * (grad_norm_one - norm_one * lax.optimization_barrier(jnp.mean(grad_norm_one * norm_one, axis=-1, keepdims=True)))
    return (layer_out, input_grad, grad_attn_gain, grad_query_proj, grad_latent_proj, grad_latent_gain, grad_latent_up, grad_output_proj, grad_ffn_gain, grad_shared_in, grad_shared_out, grad_expert_in, grad_expert_out)
```

```python
import math

import jax
import jax.numpy as jnp
from jax import lax
from jax.sharding import PartitionSpec as P

D = 1024
H = 8
NOPE = 128
ROPE = 64
VDIM = 128
RANK = 512
EXPERTS = 64
TOP = 6
CAP = 16
QW = H * (NOPE + ROPE)
OW = H * VDIM
UW = H * (NOPE + VDIM) // 2
LW = RANK + ROPE
ATT_W = 4224

EPSILON = 1e-06
F32 = jnp.float32
BF16 = jnp.bfloat16


def matmul(left_side, right_side):
    return jnp.dot(left_side, right_side, preferred_element_type=F32)


def product(pattern, left_side, right_side):
    return jnp.einsum(pattern, left_side, right_side, preferred_element_type=F32)


def inverse_rms(values):
    return lax.rsqrt(jnp.mean(values * values, axis=-1, keepdims=True) + EPSILON)


def rotate(values, cosine_table, sine_table):
    middle = values.shape[-1] // 2
    first_half = values[..., :middle]
    second_half = values[..., middle:]
    return jnp.concatenate(
        [
            first_half * cosine_table - second_half * sine_table,
            second_half * cosine_table + first_half * sine_table,
        ],
        axis=-1,
    )


def unrotate(values, cosine_table, sine_table):
    return rotate(values, cosine_table, -sine_table)


def swiglu_parts(pre_act):
    middle = pre_act.shape[-1] // 2
    gate_pre = pre_act[..., :middle]
    up_pre = pre_act[..., middle:]
    return (gate_pre, up_pre, jax.nn.sigmoid(gate_pre))


def swiglu_forward(pre_act):
    gate_pre, up_pre, sigmoid_gate = swiglu_parts(pre_act)
    return (gate_pre * sigmoid_gate * up_pre).astype(BF16)


def swiglu_backward(pre_act, grad_act):
    gate_pre, up_pre, sigmoid_gate = swiglu_parts(pre_act)
    silu_value = gate_pre * sigmoid_gate
    slope = sigmoid_gate * (1.0 + gate_pre * (1.0 - sigmoid_gate))
    return jnp.concatenate([grad_act * up_pre * slope, grad_act * silu_value], axis=-1).astype(BF16)


def tables(documents):
    rows_here = documents.shape[0]
    indices = jnp.arange(rows_here, dtype=jnp.int32)
    same_doc = documents[:, None] == documents[None, :]
    starts = jnp.min(jnp.where(same_doc, indices[None, :], rows_here), axis=1)
    allowed = same_doc & (indices[None, :] <= indices[:, None])
    position = (indices - starts).astype(F32)
    frequency = jnp.exp(jnp.arange(ROPE // 2, dtype=F32) * (-2.0 * math.log(10000.0) / ROPE))
    angles = position[:, None] * frequency[None, :]
    return (allowed, jnp.cos(angles), jnp.sin(angles))


def prepare(query_raw, kv_raw, rope_key, cosine_table, sine_table):
    rows_here = query_raw.shape[0]
    query_heads = query_raw.reshape(rows_here, H, NOPE + ROPE)
    queries = jnp.concatenate(
        [
            query_heads[..., :NOPE],
            rotate(query_heads[..., NOPE:], cosine_table[:, None, :], sine_table[:, None, :]),
        ],
        axis=-1,
    ).astype(BF16)
    kv_heads = kv_raw.reshape(rows_here, H, NOPE + VDIM)
    turned = rotate(rope_key, cosine_table, sine_table)
    key_rows = jnp.concatenate(
        [kv_heads[..., :NOPE], jnp.broadcast_to(turned[:, None, :], (rows_here, H, ROPE))], axis=-1
    ).astype(BF16)
    value_rows = kv_heads[..., NOPE:].astype(BF16)
    return (queries, key_rows, value_rows)


def attend(queries, key_rows, value_rows, allowed):
    scaling = (NOPE + ROPE) ** (-0.5)
    scores = product("ihd,jhd->hij", queries, key_rows) * scaling
    log_total = jnp.log(jnp.sum(jnp.where(allowed[None], jnp.exp(scores), 0.0), axis=-1))
    weights = jnp.where(allowed[None], jnp.exp(scores - log_total[..., None]), 0.0)
    head_out = product("hij,jhd->ihd", weights.astype(BF16), value_rows).astype(BF16)
    return (head_out.reshape(head_out.shape[0], H * VDIM), weights)


def attend_back(queries, key_rows, value_rows, weights, cosine_table, sine_table, head_out, grad_heads):
    rows_here = queries.shape[0]
    scaling = (NOPE + ROPE) ** (-0.5)
    rounded_probs = weights.astype(BF16)
    grad_three = grad_heads.reshape(rows_here, H, VDIM)
    heads_three = head_out.reshape(rows_here, H, VDIM)
    grad_probs = product("ihd,jhd->hij", grad_three, value_rows)
    deltas = jnp.sum(grad_three.astype(F32) * heads_three.astype(F32), axis=-1).T
    grad_scores = (weights * (grad_probs - deltas[..., None]) * scaling).astype(BF16)
    grad_queries = product("hij,jhd->ihd", grad_scores, key_rows)
    grad_keys = product("hij,ihd->jhd", grad_scores, queries)
    grad_values = product("hij,ihd->jhd", rounded_probs, grad_three)
    grad_query_raw = jnp.concatenate(
        [
            grad_queries[..., :NOPE],
            unrotate(grad_queries[..., NOPE:], cosine_table[:, None, :], sine_table[:, None, :]),
        ],
        axis=-1,
    ).reshape(rows_here, H * (NOPE + ROPE))
    grad_rope = unrotate(jnp.sum(grad_keys[..., NOPE:], axis=1), cosine_table, sine_table)
    grad_kv = jnp.concatenate([grad_keys[..., :NOPE], grad_values], axis=-1).reshape(
        rows_here, H * (NOPE + VDIM)
    )
    return (grad_query_raw, grad_kv, grad_rope)


def body(
    hidden_in,
    out_grad,
    doc_ids,
    routes,
    gate_values,
    attn_gain,
    query_proj,
    latent_proj,
    latent_gain,
    latent_up,
    output_proj,
    ffn_gain,
    shared_in,
    shared_out,
    expert_in,
    expert_out,
):
    devices = lax.axis_size("fsdp")
    rows_here = hidden_in.shape[0]
    own = D // devices
    half = own // 2

    gains = jnp.concatenate(
        [
            attn_gain[:, None],
            ffn_gain[:, None],
            jnp.concatenate([latent_gain, jnp.zeros_like(latent_gain)])[:, None],
            jnp.zeros((own, ATT_W - QW - OW - UW - LW - 3), BF16),
        ],
        axis=1,
    )
    packed = jnp.concatenate(
        [
            query_proj,
            output_proj,
            jnp.concatenate([latent_up[:, :UW], latent_up[:, UW:]], axis=0),
            latent_proj,
            gains,
        ],
        axis=1,
    )
    gathered = lax.all_gather(packed, "fsdp", axis=0, tiled=True)
    gathered_shared = lax.all_gather(
        jnp.concatenate([shared_in, shared_out], axis=1), "fsdp", axis=0, tiled=True
    )

    per_device = expert_in.shape[0]
    pieces = 2 if per_device % 2 == 0 else 1
    units = 2 * EXPERTS // pieces
    local_units = units // devices
    unit_expert = jnp.arange(units, dtype=jnp.int32) // (2 // pieces)
    named = routes[:, :, None] == unit_expert[None, None, :]
    hits = jnp.any(named, axis=1)
    gates = jnp.sum(jnp.where(named, gate_values[:, :, None], 0.0), axis=1)
    token = jnp.arange(rows_here, dtype=jnp.int32)
    earlier = (token[None, :] < token[:, None]).astype(BF16)
    slots = matmul(earlier, hits.astype(BF16)).astype(jnp.int32)
    slots = jnp.where(hits, slots, CAP)
    by_row = lambda table: table.T.reshape(devices, local_units, rows_here).transpose(1, 0, 2)
    row_slots = by_row(slots)
    row_gates = by_row(gates)
    chosen = row_slots[:, :, None, :] == jnp.arange(CAP, dtype=jnp.int32)[None, None, :, None]
    selector = chosen.astype(BF16).reshape(local_units, devices * CAP, rows_here)
    gate_wide = jnp.where(chosen, row_gates[:, :, None, :], 0.0).reshape(
        local_units, devices * CAP, rows_here
    )
    gate_rows = jnp.sum(gate_wide, axis=-1, keepdims=True)

    def exchange(rows):
        return lax.all_to_all(
            rows.reshape(devices, CAP, D), "fsdp", split_axis=0, concat_axis=0, tiled=True
        ).reshape(devices * CAP, D)

    grad_rows = [
        exchange((gate_rows[u] * matmul(selector[u], out_grad)).astype(BF16))
        for u in range(local_units)
    ]

    full_query = gathered[:, :QW]
    full_output = gathered[:, QW : QW + OW]
    ups = gathered[:, QW + OW : QW + OW + UW].reshape(devices, 2, half, UW)
    up_left = ups[:, 0].reshape(RANK, UW)
    up_right = ups[:, 1].reshape(RANK, UW)
    full_latent = gathered[:, QW + OW + UW : QW + OW + UW + LW]
    gain_at = QW + OW + UW + LW
    full_attn_gain = gathered[:, gain_at].astype(F32)
    full_ffn_gain = gathered[:, gain_at + 1].astype(F32)
    full_latent_gain = (
        gathered[:, gain_at + 2].reshape(devices, own)[:, :half].reshape(RANK).astype(F32)
    )

    hidden_wide = hidden_in.astype(F32)
    scale_one = inverse_rms(hidden_wide)
    norm_one = hidden_wide * scale_one
    normed_one = (norm_one * full_attn_gain).astype(BF16)
    query_raw = matmul(normed_one, full_query)
    latent_all = matmul(normed_one, full_latent)
    latent_part = latent_all[:, :RANK]
    rope_key = latent_all[:, RANK:]
    scale_latent = inverse_rms(latent_part)
    latent_norm = latent_part * scale_latent
    latent_in = (latent_norm * full_latent_gain).astype(BF16)
    kv_raw = jnp.concatenate([matmul(latent_in, up_left), matmul(latent_in, up_right)], axis=1)
    allowed, cosine_table, sine_table = tables(doc_ids[0])
    queries, key_rows, value_rows = prepare(query_raw, kv_raw, rope_key, cosine_table, sine_table)
    head_out, weights = attend(queries, key_rows, value_rows, allowed)
    mixed = hidden_wide + product("tv,dv->td", head_out, full_output)
    scale_two = inverse_rms(mixed)
    norm_two = mixed * scale_two
    normed_two = (norm_two * full_ffn_gain).astype(BF16)

    rows_in = [exchange(matmul(selector[u], normed_two).astype(BF16)) for u in range(local_units)]

    shared_width = shared_in.shape[1]
    full_shared_in = gathered_shared[:, :shared_width]
    full_shared_out = gathered_shared[:, shared_width:]
    shared_pre = matmul(normed_two, full_shared_in)
    shared_act = swiglu_forward(shared_pre)
    grad_shared_act = matmul(out_grad, full_shared_out)
    grad_shared_pre = swiglu_backward(shared_pre, grad_shared_act)
    grad_shared = jnp.concatenate(
        [
            product("td,tf->df", normed_two, grad_shared_pre).astype(BF16),
            product("td,tf->df", out_grad, shared_act).astype(BF16),
        ],
        axis=1,
    )
    owned_shared = lax.psum_scatter(grad_shared, "fsdp", scatter_dimension=0, tiled=True)
    shared_y = product("tf,df->td", shared_act, full_shared_out)
    shared_dx = product("tf,df->td", grad_shared_pre, full_shared_in)

    back_dx, back_out, grads_in, grads_out = [], [], [], []
    for u in range(local_units):
        weight_in = expert_in[u * pieces : (u + 1) * pieces]
        weight_out = expert_out[u * pieces : (u + 1) * pieces]
        pre_act = product("rd,pdf->prf", rows_in[u], weight_in)
        activation = swiglu_forward(pre_act)
        grad_act = product("rd,pfd->prf", grad_rows[u], weight_out)
        grad_pre = swiglu_backward(pre_act, grad_act)
        back_dx.append(exchange(product("prf,pdf->rd", grad_pre, weight_in).astype(BF16)))
        back_out.append(exchange(product("prf,pfd->rd", activation, weight_out).astype(BF16)))
        grads_out.append(product("prf,rd->pfd", activation, grad_rows[u]))
        grads_in.append(product("rd,prf->pdf", rows_in[u], grad_pre))
    grad_expert_in = jnp.concatenate(grads_in, axis=0)
    grad_expert_out = jnp.concatenate(grads_out, axis=0)

    routed_dx = sum(product("rt,rd->td", selector[u], back_dx[u]) for u in range(local_units))
    gate_high = lax.reduce_precision(gate_wide, 8, 7)
    gate_low = (gate_wide - gate_high).astype(BF16)
    gate_high = gate_high.astype(BF16)
    routed_y = sum(
        product("rt,rd->td", gate_high[u], back_out[u])
        + product("rt,rd->td", gate_low[u], back_out[u])
        for u in range(local_units)
    )
    layer_out = (mixed + shared_y + routed_y).astype(BF16)

    grad_normed_two = shared_dx + routed_dx
    grad_ffn_gain = jnp.sum(grad_normed_two * norm_two, axis=0)
    grad_norm_two = grad_normed_two * full_ffn_gain
    grad_mixed = out_grad.astype(F32) + scale_two * (
        grad_norm_two - norm_two * jnp.mean(grad_norm_two * norm_two, axis=-1, keepdims=True)
    )
    mixed_low = grad_mixed.astype(BF16)
    grad_output_proj = product("td,tv->dv", mixed_low, head_out)
    grad_heads = matmul(mixed_low, full_output).astype(BF16)
    grad_query_wide, grad_kv_wide, grad_rope = attend_back(
        queries, key_rows, value_rows, weights, cosine_table, sine_table, head_out, grad_heads
    )
    grad_query_raw = grad_query_wide.astype(BF16)
    grad_kv = grad_kv_wide.astype(BF16)
    kv_left, kv_right = grad_kv[:, :UW], grad_kv[:, UW:]
    grad_up = jnp.stack(
        [
            product("tr,tk->rk", latent_in, kv_left).astype(BF16).reshape(devices, half, UW),
            product("tr,tk->rk", latent_in, kv_right).astype(BF16).reshape(devices, half, UW),
        ],
        axis=1,
    ).reshape(D, UW)
    grad_latent_in = product("tk,rk->tr", kv_left, up_left) + product("tk,rk->tr", kv_right, up_right)
    grad_latent_gain = jnp.sum(grad_latent_in * latent_norm, axis=0)
    grad_norm_latent = grad_latent_in * full_latent_gain
    grad_latent = scale_latent * (
        grad_norm_latent
        - latent_norm * jnp.mean(grad_norm_latent * latent_norm, axis=-1, keepdims=True)
    )
    grad_latent_all = jnp.concatenate([grad_latent, grad_rope], axis=-1).astype(BF16)
    grad_query_proj = product("td,tq->dq", normed_one, grad_query_raw)
    grad_latent_proj = product("td,tq->dq", normed_one, grad_latent_all)
    grad_normed_one = product("tq,dq->td", grad_query_raw, full_query) + product(
        "tq,dq->td", grad_latent_all, full_latent
    )
    grad_attn_gain = jnp.sum(grad_normed_one * norm_one, axis=0)
    grad_norm_one = grad_normed_one * full_attn_gain
    input_grad = grad_mixed + scale_one * (
        grad_norm_one - norm_one * jnp.mean(grad_norm_one * norm_one, axis=-1, keepdims=True)
    )
    latent_gain_column = jnp.concatenate(
        [grad_latent_gain.reshape(devices, half), jnp.zeros((devices, own - half), F32)], axis=1
    ).reshape(D)
    grad_gains = jnp.concatenate(
        [
            jnp.stack([grad_attn_gain, grad_ffn_gain, latent_gain_column], axis=1),
            jnp.zeros((D, ATT_W - gain_at - 3), F32),
        ],
        axis=1,
    ).astype(BF16)
    grad_packed = jnp.concatenate(
        [
            grad_query_proj.astype(BF16),
            grad_output_proj.astype(BF16),
            grad_up,
            grad_latent_proj.astype(BF16),
            grad_gains,
        ],
        axis=1,
    )
    owned = lax.psum_scatter(grad_packed, "fsdp", scatter_dimension=0, tiled=True).astype(F32)
    owned_shared = owned_shared.astype(F32)
    owned_up = owned[:, QW + OW : QW + OW + UW]
    return (
        layer_out,
        input_grad,
        owned[:, gain_at],
        owned[:, :QW],
        owned[:, QW + OW + UW : gain_at],
        owned[:half, gain_at + 2],
        jnp.concatenate([owned_up[:half], owned_up[half:]], axis=1),
        owned[:, QW : QW + OW],
        owned[:, gain_at + 1],
        owned_shared[:, :shared_width],
        owned_shared[:, shared_width:],
        grad_expert_in,
        grad_expert_out,
    )


def solution(mesh):
    rows = P("fsdp", None)
    flat = P("fsdp")
    cube = P("fsdp", None, None)
    in_specs = (rows,) * 5 + (flat, rows, rows, flat, rows, rows, flat, rows, rows, cube, cube)
    out_specs = (rows, rows, flat, rows, rows, flat, rows, rows, flat, rows, rows, cube, cube)
    return jax.shard_map(body, mesh=mesh, in_specs=in_specs, out_specs=out_specs, check_vma=False)
```

```python
import functools
import math

import jax
import jax.numpy as jnp
from jax import lax
from jax.experimental import pallas as pl
from jax.experimental.pallas import tpu as pltpu
from jax.sharding import PartitionSpec as P


D = 1024
H = 8
NOPE = 128
ROPE = 64
VDIM = 128
RANK = 512
EXPERTS = 64
CAP = 16
UW = H * (NOPE + VDIM) // 2
LW = RANK + ROPE

EPSILON = 1e-06
F32 = jnp.float32
BF16 = jnp.bfloat16


def matmul(left_side, right_side):
    return jnp.dot(left_side, right_side, preferred_element_type=F32)


def product(pattern, left_side, right_side):
    return jnp.einsum(pattern, left_side, right_side, preferred_element_type=F32)


def inverse_rms(values):
    return lax.rsqrt(jnp.mean(values * values, axis=-1, keepdims=True) + EPSILON)


def swiglu_parts(pre_act):
    middle = pre_act.shape[-1] // 2
    gate_pre = pre_act[..., :middle]
    up_pre = pre_act[..., middle:]
    return (gate_pre, up_pre, jax.nn.sigmoid(gate_pre))


def swiglu_forward(pre_act):
    gate_pre, up_pre, sigmoid_gate = swiglu_parts(pre_act)
    return (gate_pre * sigmoid_gate * up_pre).astype(BF16)


def swiglu_backward(pre_act, grad_act):
    gate_pre, up_pre, sigmoid_gate = swiglu_parts(pre_act)
    silu_value = gate_pre * sigmoid_gate
    slope = sigmoid_gate * (1.0 + gate_pre * (1.0 - sigmoid_gate))
    return jnp.concatenate([grad_act * up_pre * slope, grad_act * silu_value], axis=-1).astype(BF16)


def tables(documents):
    rows_here = documents.shape[0]
    indices = jnp.arange(rows_here, dtype=jnp.int32)
    same_doc = documents[:, None] == documents[None, :]
    starts = jnp.min(jnp.where(same_doc, indices[None, :], rows_here), axis=1)
    allowed = same_doc & (indices[None, :] <= indices[:, None])
    position = (indices - starts).astype(F32)
    frequency = jnp.exp(jnp.arange(ROPE // 2, dtype=F32) * (-2.0 * math.log(10000.0) / ROPE))
    angles = position[:, None] * frequency[None, :]
    return (allowed, jnp.cos(angles), jnp.sin(angles))


def nn(left_side, right_side):
    return lax.dot_general(
        left_side, right_side, (((1,), (0,)), ((), ())), preferred_element_type=F32
    )


def nt(left_side, right_side):
    return lax.dot_general(
        left_side, right_side, (((1,), (1,)), ((), ())), preferred_element_type=F32
    )


def tn(left_side, right_side):
    return lax.dot_general(
        left_side, right_side, (((0,), (0,)), ((), ())), preferred_element_type=F32
    )


def experts_kernel(rows, grads, w_in, w_out, dx, y, act, dpre, dx_sum, y_sum):
    piece = pl.program_id(1)
    middle = w_out.shape[1]
    pre_act = nn(rows[...], w_in[0])
    gate_pre = pre_act[:, :middle]
    up_pre = pre_act[:, middle:]
    sigmoid_gate = jax.nn.sigmoid(gate_pre)
    silu_value = gate_pre * sigmoid_gate
    act_low = (silu_value * up_pre).astype(BF16)
    act[0] = act_low
    grad_act = nt(grads[...], w_out[0])
    slope = sigmoid_gate * (1.0 + gate_pre * (1.0 - sigmoid_gate))
    dpre_low = jnp.concatenate([grad_act * up_pre * slope, grad_act * silu_value], axis=1).astype(BF16)
    dpre[0] = dpre_low
    dx_part = nt(dpre_low, w_in[0])
    y_part = nn(act_low, w_out[0])

    @pl.when(piece == 0)
    def _():
        dx_sum[...] = dx_part
        y_sum[...] = y_part

    @pl.when(piece > 0)
    def _():
        dx_sum[...] += dx_part
        y_sum[...] += y_part

    @pl.when(piece == pl.num_programs(1) - 1)
    def _():
        dx[...] = dx_sum[...].astype(BF16)
        y[...] = y_sum[...].astype(BF16)


def experts(rows, grads, w_in, w_out, unit, pieces):
    count, width = rows.shape
    first = unit * pieces
    double, middle = w_in.shape[2], w_out.shape[1]
    block = min(512, count)
    row_spec = pl.BlockSpec((block, width), lambda r, p: (r, 0))
    return pl.pallas_call(
        experts_kernel,
        grid=(count // block, pieces),
        in_specs=[
            row_spec,
            row_spec,
            pl.BlockSpec((1, width, double), lambda r, p: (first + p, 0, 0)),
            pl.BlockSpec((1, middle, width), lambda r, p: (first + p, 0, 0)),
        ],
        out_specs=[
            row_spec,
            row_spec,
            pl.BlockSpec((1, block, middle), lambda r, p: (p, r, 0)),
            pl.BlockSpec((1, block, double), lambda r, p: (p, r, 0)),
        ],
        out_shape=[
            jax.ShapeDtypeStruct((count, width), BF16),
            jax.ShapeDtypeStruct((count, width), BF16),
            jax.ShapeDtypeStruct((pieces, count, middle), BF16),
            jax.ShapeDtypeStruct((pieces, count, double), BF16),
        ],
        scratch_shapes=[pltpu.VMEM((block, width), F32), pltpu.VMEM((block, width), F32)],
        compiler_params=pltpu.CompilerParams(vmem_limit_bytes=60 * 2**20),
        cost_estimate=pl.CostEstimate(
            flops=2 * count * width * pieces * (2 * double + 2 * middle),
            bytes_accessed=pieces * (width + count) * (double + middle) * 2 + count * width * 8,
            transcendentals=count * middle * pieces,
        ),
        name="experts",
    )(rows, grads, w_in, w_out)


def expert_grads_kernel(rows, grads, act, dpre, *refs):
    grad_in, grad_out = refs[-2:]
    grad_in[0] = tn(rows[...], dpre[0])
    grad_out[0] = tn(act[0], grads[...])


def expert_grads(rows, grads, act, dpre, total, unit, late, held=None, chunk=256):
    count, width = rows.shape
    pieces, _, middle = act.shape
    first = unit * pieces
    double = dpre.shape[2]
    row_spec = pl.BlockSpec((count, chunk), lambda p, k: (0, k))
    operands = [rows, grads, act, dpre]
    in_specs = [
        row_spec,
        row_spec,
        pl.BlockSpec((1, count, middle), lambda p, k: (p, 0, 0)),
        pl.BlockSpec((1, count, double), lambda p, k: (p, 0, 0)),
    ]
    if late is not None:
        operands.append(late)
        in_specs.append(pl.BlockSpec(memory_space=pl.ANY))
    aliases = {}
    if held is not None:
        operands += list(held)
        in_specs += [pl.BlockSpec(memory_space=pl.ANY)] * 2
        aliases = {len(operands) - 2: 0, len(operands) - 1: 1}
    return pl.pallas_call(
        expert_grads_kernel,
        grid=(pieces, width // chunk),
        in_specs=in_specs,
        out_specs=[
            pl.BlockSpec((1, chunk, double), lambda p, k: (first + p, k, 0)),
            pl.BlockSpec((1, middle, chunk), lambda p, k: (first + p, 0, k)),
        ],
        out_shape=[
            jax.ShapeDtypeStruct((total, width, double), F32),
            jax.ShapeDtypeStruct((total, middle, width), F32),
        ],
        input_output_aliases=aliases,
        compiler_params=pltpu.CompilerParams(vmem_limit_bytes=60 * 2**20),
        cost_estimate=pl.CostEstimate(
            flops=2 * count * width * pieces * (double + middle),
            bytes_accessed=pieces * width * (double + middle) * 4 + count * width * 8,
            transcendentals=0,
        ),
        name="expert_grads",
    )(*operands)


def grads_kernel(*refs, plan, count):
    inputs, outs = refs[:-count], refs[-count:]
    rows = outs[0].shape[0]
    at = 0
    for width, starts in plan:
        left, right = [], []
        for start in starts:
            pair, inputs = inputs[:4], inputs[4:]
            left += [pair[0][...], pair[1][...]]
            right += [values[:, start : start + width] for values in pair[2:]]
        total = tn(jnp.concatenate(left, axis=0), jnp.concatenate(right, axis=0))
        for k, out in enumerate(outs):
            out[:, at : at + width] = total[k * rows : (k + 1) * rows].astype(BF16)
        at += width


def grads_of(segments, count):
    plan, operands, specs = [], [], []
    rows = segments[0][1][0][0].shape[1]

    def block(values, at, width):
        return pl.BlockSpec((values.shape[0], width), lambda _: (0, at // width))

    flops = 0
    for width, products in segments:
        starts = []
        for left_mine, left_other, right_mine, right_other, at in products:
            operands += [left_mine, left_other, right_mine, right_other]
            whole = at % width > 0
            starts.append(at if whole else 0)
            specs += [block(left_mine, 0, rows)] * 2
            specs += [block(right_mine, 0 if whole else at, right_mine.shape[1] if whole else width)] * 2
            flops += 4 * rows * width * left_mine.shape[0]
        plan.append((width, tuple(starts)))
    total = sum(width for width, _ in segments)
    return pl.pallas_call(
        functools.partial(grads_kernel, plan=tuple(plan), count=count),
        grid=(1,),
        in_specs=specs,
        out_specs=[pl.BlockSpec((rows // count, total), lambda _: (0, 0))] * count,
        out_shape=[jax.ShapeDtypeStruct((rows // count, total), BF16)] * count,
        compiler_params=pltpu.CompilerParams(vmem_limit_bytes=60 * 2**20),
        cost_estimate=pl.CostEstimate(
            flops=flops, bytes_accessed=4 * rows * total, transcendentals=0
        ),
    )(*operands)


def swap_halves(values):
    width = values.shape[1]
    lane = lax.broadcasted_iota(jnp.int32, values.shape, 1)
    return jnp.where(
        lane % ROPE < ROPE // 2,
        pltpu.roll(values, width - ROPE // 2, 1),
        pltpu.roll(values, ROPE // 2, 1),
    )


def repeated(table, times):
    return jnp.concatenate([table] * times, axis=1)


def upper_lanes(shape, head):
    return lax.broadcasted_iota(jnp.int32, shape, 1) // ROPE == head % 2


def lefts_and_rights(block, half, into):
    rows, width = block.shape
    if half % 16 == 0:
        cut = block.reshape(rows // (2 * half), 2 * half, width)
        return [
            cut[:, side * half : (side + 1) * half].reshape(rows // 2, width) for side in range(into)
        ]
    out = []
    for side in range(into):
        shape = (rows // 2, rows)
        row = lax.broadcasted_iota(jnp.int32, shape, 0)
        column = lax.broadcasted_iota(jnp.int32, shape, 1)
        wanted = row // half * (2 * half) + side * half + row % half
        out.append(nn((column == wanted).astype(BF16), block).astype(BF16))
    return out


def attention_kernel(
    hidden,
    mask,
    cosine,
    sine,
    weights,
    normed_two,
    mixed_out,
    normed_one_out,
    latent_norm_out,
    latent_in_out,
    latent_scale_out,
    query_out,
    key_value_out,
    rope_key_out,
    probs_out,
    head_out,
    gains_out,
    ups_out,
    first,
    output,
    up,
    sems,
    *,
    half,
):
    first_width, output_width = first.shape[1], output.shape[1]
    copies = [
        pltpu.make_async_copy(weights.at[:, pl.ds(at, target.shape[1])], target, sems.at[i])
        for i, (at, target) in enumerate(
            ((0, first), (first_width + output_width, up), (first_width, output))
        )
    ]
    for copy in copies:
        copy.start()
    hidden_wide = hidden[...].astype(F32)
    norm_one = hidden_wide * inverse_rms(hidden_wide)
    copies[0].wait()
    tail = first[:, first_width - 128 :]
    picked = lax.broadcasted_iota(jnp.int32, (16, 128), 1) == ROPE + lax.broadcasted_iota(
        jnp.int32, (16, 128), 0
    )
    picked = picked.astype(BF16)
    gains = nt(picked, tail)
    latent_gains = nt(picked, lefts_and_rights(tail, half, 1)[0])
    gains_out[...] = jnp.concatenate(
        [gains[:2], jnp.concatenate([latent_gains[2:3], jnp.zeros((1, D - RANK), F32)], axis=1),
         jnp.zeros((5, D), F32)], axis=0
    )
    normed_one = (norm_one * gains[0:1]).astype(BF16)
    normed_one_out[...] = normed_one
    projected = nn(normed_one, first[...])
    nope_width = H * NOPE
    query_width = H * (NOPE + ROPE)
    latent_part = projected[:, query_width : query_width + RANK]
    latent_scale = inverse_rms(latent_part)
    latent_norm = latent_part * latent_scale
    latent_in = (latent_norm * latent_gains[2:3]).astype(BF16)
    latent_norm_out[...] = latent_norm
    latent_in_out[...] = latent_in
    latent_scale_out[...] = jnp.broadcast_to(latent_scale, latent_scale_out.shape)
    cos, sin = cosine[...], sine[...]
    rope = projected[:, nope_width:query_width]
    rope = rope * repeated(cos, H // 2) + swap_halves(rope) * repeated(sin, H // 2)
    query_out[:, :nope_width] = projected[:, :nope_width].astype(BF16)
    query_out[:, nope_width:] = rope.astype(BF16)
    key = projected[:, query_width + RANK : query_width + RANK + 128]
    key = jnp.where(upper_lanes(key.shape, 0), key, 0.0)
    key = key + pltpu.roll(key, ROPE, 1)
    rope_key = (key * cos + swap_halves(key) * sin).astype(BF16)
    rope_key_out[...] = rope_key
    copies[1].wait()
    for side, part in enumerate(lefts_and_rights(up[...], half, 2)):
        ups_out[side] = part
        key_value_out[:, side * UW : (side + 1) * UW] = nn(latent_in, part).astype(BF16)
    scaling = (NOPE + ROPE) ** (-0.5)
    allowed = mask[...]
    for head in range(H):
        pair = query_out[:, nope_width + head // 2 * 128 : nope_width + head // 2 * 128 + 128]
        pair = jnp.where(upper_lanes(pair.shape, head), pair, jnp.zeros_like(pair))
        query = jnp.concatenate([query_out[:, head * NOPE : (head + 1) * NOPE], pair], axis=1)
        at = head * (NOPE + VDIM)
        keys = jnp.concatenate([key_value_out[:, at : at + NOPE], rope_key], axis=1)
        scores = nt(query, keys) * scaling
        raised = jnp.exp(scores) * allowed
        probs = raised / jnp.sum(raised, axis=-1, keepdims=True)
        probs_out[head] = probs
        head_out[:, head * VDIM : (head + 1) * VDIM] = nn(
            probs.astype(BF16), key_value_out[:, at + NOPE : at + NOPE + VDIM]
        ).astype(BF16)
    copies[2].wait()
    mixed = hidden_wide + nt(head_out[...], output[...])
    mixed_out[...] = mixed
    normed_two[...] = (mixed * inverse_rms(mixed) * gains[1:2]).astype(BF16)


def attention(hidden, mask, cosine, sine, weights, half):
    rows, width = hidden.shape
    query_width = H * (NOPE + ROPE)
    first_width = query_width + RANK + 128
    vmem = pl.BlockSpec(memory_space=pltpu.VMEM)
    shapes = [
        ((rows, width), BF16),
        ((rows, width), F32),
        ((rows, width), BF16),
        ((rows, RANK), F32),
        ((rows, RANK), BF16),
        ((rows, 128), F32),
        ((rows, query_width), BF16),
        ((rows, 2 * UW), BF16),
        ((rows, 128), BF16),
        ((H, rows, rows), F32),
        ((rows, H * VDIM), BF16),
        ((8, width), F32),
        ((2, RANK, UW), BF16),
    ]
    return pl.pallas_call(
        functools.partial(attention_kernel, half=half),
        in_specs=[vmem] * 4 + [pl.BlockSpec(memory_space=pl.ANY)],
        out_specs=[vmem] * len(shapes),
        out_shape=[jax.ShapeDtypeStruct(shape, dtype) for shape, dtype in shapes],
        scratch_shapes=[
            pltpu.VMEM((width, first_width), BF16),
            pltpu.VMEM((width, H * VDIM), BF16),
            pltpu.VMEM((width, UW), BF16),
            pltpu.SemaphoreType.DMA((3,)),
        ],
        compiler_params=pltpu.CompilerParams(vmem_limit_bytes=60 * 2**20),
        cost_estimate=pl.CostEstimate(
            flops=2 * rows * width * (first_width + 3 * width),
            bytes_accessed=2 * width * (first_width + 2 * width) + 8 * rows * width,
            transcendentals=H * rows * rows,
        ),
        name="attention",
    )(hidden, mask, cosine, sine, weights)


def mixed_back_kernel(*refs):
    count = (len(refs) - 7) // 2
    shared_dx, out_grad, mixed, gains = refs[:4]
    selectors, back = refs[4 : 4 + count], refs[4 + count : 4 + 2 * count]
    grad_mixed_out, mixed_low, gain_out = refs[4 + 2 * count :]
    grad = shared_dx[...]
    for selector, rows in zip(selectors, back):
        grad = grad + tn(selector[...], rows[...])
    scale = inverse_rms(mixed[...])
    norm_two = mixed[...] * scale
    gain_out[...] = jnp.broadcast_to(jnp.sum(grad * norm_two, axis=0, keepdims=True), gain_out.shape)
    grad_norm = grad * gains[1:2]
    grad_mixed = out_grad[...].astype(F32) + scale * (
        grad_norm - norm_two * jnp.mean(grad_norm * norm_two, axis=-1, keepdims=True)
    )
    grad_mixed_out[...] = grad_mixed
    mixed_low[...] = grad_mixed.astype(BF16)


def mixed_back(shared_dx, out_grad, mixed, gains, selectors, back):
    rows, width = mixed.shape
    vmem = pl.BlockSpec(memory_space=pltpu.VMEM)
    total = sum(values.shape[0] for values in back)
    return pl.pallas_call(
        mixed_back_kernel,
        in_specs=[vmem] * (4 + 2 * len(back)),
        out_specs=[vmem] * 3,
        out_shape=[
            jax.ShapeDtypeStruct((rows, width), F32),
            jax.ShapeDtypeStruct((rows, width), BF16),
            jax.ShapeDtypeStruct((8, width), F32),
        ],
        compiler_params=pltpu.CompilerParams(vmem_limit_bytes=60 * 2**20),
        cost_estimate=pl.CostEstimate(
            flops=2 * rows * width * total, bytes_accessed=2 * total * width, transcendentals=0
        ),
        name="mixed_back",
    )(shared_dx, out_grad, mixed, gains, *selectors, *back)


def attention_back_kernel(
    hidden,
    grad_mixed,
    mixed_low,
    cosine,
    sine,
    latent_norm,
    latent_scale,
    query,
    key_value,
    rope_key,
    probs,
    head_out,
    gains,
    ups,
    weights,
    back,
    input_grad,
    gain_out,
    first,
    output,
    sems,
):
    first_width = first.shape[1]
    grad_projected = back.at[:, 2 * UW :]
    grad_key_value = back.at[:, : 2 * UW]
    copies = [
        pltpu.make_async_copy(weights.at[:, pl.ds(at, target.shape[1])], target, sems.at[i])
        for i, (at, target) in enumerate(((first_width, output), (0, first)))
    ]
    for copy in copies:
        copy.start()
    copies[0].wait()
    rows = hidden.shape[0]
    nope_width = H * NOPE
    query_width = H * (NOPE + ROPE)
    scaling = (NOPE + ROPE) ** (-0.5)
    heads = nn(mixed_low[...], output[...]).astype(BF16)
    rope_sum = jnp.zeros((rows, 128), F32)
    rope_grads = []
    for head in range(H):
        grad_head = heads[:, head * VDIM : (head + 1) * VDIM]
        at = head * (NOPE + VDIM)
        weights_here = probs[head]
        own_lanes = upper_lanes((rows, 128), head)
        pair = query[:, nope_width + head // 2 * 128 : nope_width + head // 2 * 128 + 128]
        pair = jnp.where(own_lanes, pair, jnp.zeros_like(pair))
        query_here = jnp.concatenate([query[:, head * NOPE : (head + 1) * NOPE], pair], axis=1)
        keys = jnp.concatenate([key_value[:, at : at + NOPE], rope_key[...]], axis=1)
        grad_probs = nt(grad_head, key_value[:, at + NOPE : at + NOPE + VDIM])
        delta = jnp.sum(
            grad_head.astype(F32) * head_out[:, head * VDIM : (head + 1) * VDIM].astype(F32),
            axis=-1,
            keepdims=True,
        )
        grad_scores = (weights_here * (grad_probs - delta) * scaling).astype(BF16)
        grad_query = nn(grad_scores, keys)
        grad_projected[:, head * NOPE : (head + 1) * NOPE] = grad_query[:, :NOPE].astype(BF16)
        rope_grads.append(jnp.where(own_lanes, grad_query[:, NOPE:], 0.0))
        grad_keys = tn(grad_scores, query_here)
        rope_sum = rope_sum + grad_keys[:, NOPE:]
        grad_key_value[:, at : at + NOPE] = grad_keys[:, :NOPE].astype(BF16)
        grad_key_value[:, at + NOPE : at + NOPE + VDIM] = tn(
            weights_here.astype(BF16), grad_head
        ).astype(BF16)
    cos, sin = cosine[...], sine[...]
    rope = jnp.concatenate(
        [rope_grads[2 * pair] + rope_grads[2 * pair + 1] for pair in range(H // 2)], axis=1
    )
    rope = rope * repeated(cos, H // 2) - swap_halves(rope) * repeated(sin, H // 2)
    grad_projected[:, nope_width:query_width] = rope.astype(BF16)
    key = rope_sum + pltpu.roll(rope_sum, ROPE, 1)
    key = key * cos - swap_halves(key) * sin
    key = jnp.where(upper_lanes(key.shape, 0), key, 0.0)
    grad_projected[:, query_width + RANK :] = key.astype(BF16)
    grad_latent_in = nt(grad_key_value[:, :UW], ups[0]) + nt(grad_key_value[:, UW:], ups[1])
    norm = latent_norm[...]
    latent_gain_grad = jnp.sum(grad_latent_in * norm, axis=0, keepdims=True)
    grad_norm = grad_latent_in * gains[2:3, :RANK]
    grad_latent = latent_scale[:, 0:1] * (
        grad_norm - norm * jnp.mean(grad_norm * norm, axis=-1, keepdims=True)
    )
    grad_projected[:, query_width : query_width + RANK] = grad_latent.astype(BF16)
    copies[1].wait()
    grad_normed = nt(grad_projected[...], first[...])
    hidden_wide = hidden[...].astype(F32)
    scale = inverse_rms(hidden_wide)
    norm_one = hidden_wide * scale
    gain_out[...] = jnp.concatenate(
        [
            jnp.sum(grad_normed * norm_one, axis=0, keepdims=True),
            jnp.concatenate([latent_gain_grad, jnp.zeros((1, D - RANK), F32)], axis=1),
            jnp.zeros((6, D), F32),
        ],
        axis=0,
    )
    grad_norm = grad_normed * gains[0:1]
    input_grad[...] = grad_mixed[...] + scale * (
        grad_norm - norm_one * jnp.mean(grad_norm * norm_one, axis=-1, keepdims=True)
    )


def attention_back(operands, weights):
    hidden = operands[0]
    rows, width = hidden.shape
    first_width = H * (NOPE + ROPE) + RANK + 128
    vmem = pl.BlockSpec(memory_space=pltpu.VMEM)
    return pl.pallas_call(
        attention_back_kernel,
        in_specs=[vmem] * len(operands) + [pl.BlockSpec(memory_space=pl.ANY)],
        out_specs=[vmem] * 3,
        out_shape=[
            jax.ShapeDtypeStruct((rows, first_width + 2 * UW), BF16),
            jax.ShapeDtypeStruct((rows, width), F32),
            jax.ShapeDtypeStruct((8, width), F32),
        ],
        scratch_shapes=[
            pltpu.VMEM((width, first_width), BF16),
            pltpu.VMEM((width, H * VDIM), BF16),
            pltpu.SemaphoreType.DMA((2,)),
        ],
        compiler_params=pltpu.CompilerParams(vmem_limit_bytes=60 * 2**20),
        cost_estimate=pl.CostEstimate(
            flops=2 * rows * width * (first_width + 3 * width),
            bytes_accessed=2 * width * (first_width + 2 * width) + 8 * rows * width,
            transcendentals=0,
        ),
        name="attention_back",
    )(*operands, weights)


def after_kernel(values, late, out):
    pass


def after(values, late):
    anywhere = pl.BlockSpec(memory_space=pl.ANY)
    return pl.pallas_call(
        after_kernel,
        in_specs=[anywhere, anywhere],
        out_specs=anywhere,
        out_shape=jax.ShapeDtypeStruct(values.shape, values.dtype),
        input_output_aliases={0: 0},
        cost_estimate=pl.CostEstimate(flops=0, bytes_accessed=0, transcendentals=0),
        name="after",
    )(values, late)


def axes_of(devices):
    return {32: ((8, 4), (4, 2), (2, 2)), 128: ((32, 4), (8, 4), (2, 4))}[devices]


def swap_with(values, devices, offset):
    return lax.ppermute(values, "fsdp", [(i, i ^ offset) for i in range(devices)])


def pick(values, index, axis):
    return lax.dynamic_index_in_dim(values, index, axis, keepdims=False)


def row_order(devices, axis, half=None):
    me = lax.axis_index("fsdp")
    own = D // devices
    axes = axes_of(devices)
    to = jnp.arange(D, dtype=jnp.int32)
    chip_row = to % (D // 2)
    stride, size = axes[axis]
    block = chip_row // (D // 2 // size)
    rest = chip_row % (D // 2 // size) // own
    device = (me % 2) ^ (to // (D // 2))
    device = device + (((me // stride) % size) ^ block) * stride
    for other in (2, 1, 0):
        if other != axis:
            device = device + rest % axes[other][1] * axes[other][0]
            rest = rest // axes[other][1]
    row = to % own
    if half is None:
        source = device * own + row
        return (jnp.arange(D, dtype=jnp.int32)[:, None] == source[None, :]).astype(BF16)
    source = device * half + row % half
    hit = jnp.arange(D // 2, dtype=jnp.int32)[:, None] == source[None, :]
    return [(hit & (row // half == side)[None, :]).astype(BF16) for side in range(2)]


def scatter_sum(blocks, devices, order, late=None):
    me = lax.axis_index("fsdp")
    axes = axes_of(devices)
    left = [0, 1, 2]
    values = None
    for axis in order:
        stride, size = axes[axis]
        at = left.index(axis)
        left.remove(axis)
        mine = (me // stride) % size
        if values is not None:
            blocks = [pick(values, mine ^ k, at) for k in range(size)]
        total = blocks[0] if late is None or values is not None else after(blocks[0], late)
        total = total.astype(F32)
        parts = [swap_with(blocks[k], devices, k * stride) for k in range(1, size)]
        for part in parts:
            total = total + part.astype(F32)
        values = total if not left else total.astype(BF16)
        if values.ndim == 2 and left:
            values = values.reshape(
                *(axes[other][1] for other in left), D // devices, values.shape[-1]
            )
    return values


def body(
    hidden_in,
    out_grad,
    doc_ids,
    routes,
    gate_values,
    attn_gain,
    query_proj,
    latent_proj,
    latent_gain,
    latent_up,
    output_proj,
    ffn_gain,
    shared_in,
    shared_out,
    expert_in,
    expert_out,
):
    devices = lax.axis_size("fsdp")
    rows_here = hidden_in.shape[0]
    own = D // devices
    half = own // 2

    along_x, along_y = row_order(devices, 2), row_order(devices, 1)
    sides_x, sides_y = row_order(devices, 2, half), row_order(devices, 1, half)

    def mine_and_other(columns, order):
        placed = matmul(columns, order).astype(BF16)
        return (placed[:, : D // 2], swap_with(placed[:, D // 2 :], devices, 1))

    spare = 128 - LW % 128
    query_width, output_width = query_proj.shape[1], output_proj.shape[1]
    gain_at = query_width + LW
    output_at = gain_at + spare
    by_head = query_proj.reshape(own, H, NOPE + ROPE)
    gathered = lax.all_gather(
        jnp.concatenate(
            [
                by_head[:, :, :NOPE].reshape(own, H * NOPE),
                by_head[:, :, NOPE:].reshape(own, H * ROPE),
                latent_proj,
                attn_gain[:, None],
                ffn_gain[:, None],
                jnp.concatenate([latent_gain, jnp.zeros_like(latent_gain)])[:, None],
                jnp.zeros((own, spare - 3), BF16),
                output_proj,
                jnp.concatenate([latent_up[:, :UW], latent_up[:, UW:]], axis=0),
            ],
            axis=1,
        ),
        "fsdp",
        axis=0,
        tiled=True,
    )
    gathered_shared = lax.all_gather(
        jnp.concatenate([shared_in, shared_out], axis=1), "fsdp", axis=0, tiled=True
    )

    per_device = expert_in.shape[0]
    pieces = 2 if per_device % 2 == 0 else 1
    units = 2 * EXPERTS // pieces
    local_units = units // devices
    token = jnp.arange(rows_here, dtype=jnp.int32)
    earlier = (token[None, :] < token[:, None]).astype(BF16)

    def routing(names, values, base, count):
        unit_expert = (base + jnp.arange(count, dtype=jnp.int32)) // (2 // pieces)
        named = names[:, :, None] == unit_expert[None, None, :]
        hits = jnp.any(named, axis=1)
        gates = jnp.sum(jnp.where(named, values[:, :, None], 0.0), axis=1)
        slots = matmul(earlier, hits.astype(BF16)).astype(jnp.int32)
        return (jnp.where(hits, slots, CAP).T, gates.T)

    slots, gates = routing(routes, gate_values, 0, units)
    chosen = slots[:, None, :] == jnp.arange(CAP, dtype=jnp.int32)[None, :, None]
    gate_wide = jnp.where(chosen, gates[:, None, :], 0.0).reshape(units * CAP, rows_here)
    gate_rows = jnp.sum(gate_wide, axis=-1, keepdims=True)
    selector = chosen.astype(BF16)
    unit_selector = selector.reshape(devices, local_units, CAP, rows_here)
    unit_selector = [
        unit_selector[:, u].reshape(devices * CAP, rows_here) for u in range(local_units)
    ]
    selector = selector.reshape(units * CAP, rows_here)

    def exchange(rows):
        return lax.all_to_all(rows, "fsdp", split_axis=0, concat_axis=0, tiled=True)

    def exchange_unit(rows):
        return exchange(rows.reshape(devices, CAP, D)).reshape(devices * CAP, D)

    grad_rows = exchange(
        (gate_rows * matmul(selector, out_grad)).astype(BF16).reshape(devices, local_units * CAP, D)
    ).reshape(devices, local_units, CAP, D)
    grad_rows = [grad_rows[:, u].reshape(devices * CAP, D) for u in range(local_units)]

    allowed, cosine_table, sine_table = tables(doc_ids[0])
    cosine_lanes = jnp.concatenate([cosine_table] * 4, axis=1)
    sine_lanes = jnp.concatenate([-sine_table, sine_table] * 2, axis=1)
    (
        normed_two,
        mixed,
        normed_one,
        latent_norm,
        latent_in,
        latent_scale,
        queries,
        key_values,
        rope_key,
        probs,
        head_out,
        gain_rows,
        ups,
    ) = attention(hidden_in, allowed.astype(F32), cosine_lanes, sine_lanes, gathered, half)

    rows_out = [matmul(unit_selector[u], normed_two).astype(BF16) for u in range(local_units)]
    rows_in = []
    for rows in rows_out:
        rows_in.append(exchange_unit(rows))

    sent_dx, back_dx, back_out, saved = [], [], [], []
    for u in range(local_units):
        dx_rows, y_rows, activation, grad_pre = experts(
            rows_in[u], grad_rows[u], expert_in, expert_out, u, pieces
        )
        sent_dx.append(dx_rows)
        back_dx.append(exchange_unit(dx_rows))
        back_out.append(y_rows.reshape(devices, CAP, D))
        saved.append((activation, grad_pre))
    shared_rows = normed_two
    for rows in sent_dx:
        shared_rows = after(shared_rows, rows)
    shared_width = shared_in.shape[1]
    full_shared_in = gathered_shared[:, :shared_width]
    full_shared_out = gathered_shared[:, shared_width:]
    shared_pre = matmul(shared_rows, full_shared_in)
    shared_act = swiglu_forward(shared_pre)
    grad_shared_act = matmul(out_grad, full_shared_out)
    grad_shared_pre = swiglu_backward(shared_pre, grad_shared_act)
    middle = shared_out.shape[1]
    dpre_pair = (grad_shared_pre, swap_with(grad_shared_pre, devices, 1))
    act_pair = (shared_act, swap_with(shared_act, devices, 1))
    size_x, size_y = axes_of(devices)[2][1], axes_of(devices)[1][1]
    blocks_x = grads_of(
        (
            (middle, ((*mine_and_other(normed_two, along_x), *dpre_pair, 0),)),
            (middle, ((*mine_and_other(out_grad, along_x), *act_pair, 0),)),
        ),
        size_x,
    )
    blocks_y = grads_of(
        ((middle, ((*mine_and_other(normed_two, along_y), *dpre_pair, middle),)),), size_y
    )
    shared_blocks = (blocks_x, blocks_y)
    shared_y = product("tf,df->td", shared_act, full_shared_out)
    shared_dx = product("tf,df->td", grad_shared_pre, full_shared_in)

    back_out = jnp.concatenate(back_out, axis=1)
    for rows in back_dx:
        back_out = after(back_out, rows)
    back_out = exchange(back_out).reshape(units * CAP, D)

    grad_mixed, mixed_low, ffn_gain_grad = mixed_back(
        shared_dx, out_grad, mixed, gain_rows, unit_selector, back_dx
    )

    heads_pair = (head_out, swap_with(head_out, devices, 1))
    first_left = mine_and_other(normed_one, along_y)
    up_left = [mine_and_other(latent_in, side) for side in sides_x]
    output_left = mine_and_other(mixed_low, along_x)
    back, input_grad, other_gain_grads = attention_back(
        (
            hidden_in,
            grad_mixed,
            mixed_low,
            cosine_lanes,
            sine_lanes,
            latent_norm,
            latent_scale,
            queries,
            key_values,
            rope_key,
            probs,
            head_out,
            gain_rows,
            ups,
        ),
        gathered,
    )
    back_pair = (back, swap_with(back, devices, 1))
    gain_grads = jnp.concatenate(
        [other_gain_grads[:1], ffn_gain_grad[:1], jnp.zeros((6, D), F32)], axis=0
    ).astype(BF16)
    placed = matmul(gain_grads, along_y) + jnp.pad(
        matmul(other_gain_grads[1:7, :RANK].astype(BF16), sides_y[0]), ((2, 0), (0, 0))
    )
    placed = placed.astype(BF16)
    gain_left = (placed[:, : D // 2], swap_with(placed[:, D // 2 :], devices, 1))
    row = jnp.arange(8, dtype=jnp.int32)[:, None]
    lane = jnp.arange(output_at, dtype=jnp.int32)[None, :]
    gain_right = ((row < 3) & (lane == gain_at + row)).astype(BF16)
    blocks_y = grads_of(
        (
            (
                output_at,
                ((*first_left, *back_pair, 2 * UW), (*gain_left, gain_right, gain_right, 0)),
            ),
        ),
        size_y,
    )
    owned_first = scatter_sum(blocks_y, devices, (1, 2, 0))
    blocks_x = grads_of(
        (
            (output_width, ((*output_left, *heads_pair, 0),)),
            (UW, tuple((*up_left[i], *back_pair, i * UW) for i in range(2))),
        ),
        size_x,
    )
    owned_second = scatter_sum(blocks_x, devices, (2, 1, 0))
    owned_gate_out = scatter_sum(shared_blocks[0], devices, (2, 1, 0), blocks_x[0])
    owned_up_in = scatter_sum(shared_blocks[1], devices, (1, 2, 0), blocks_x[0])
    owned_output, owned_up = owned_second[:, :output_width], owned_second[:, output_width:]
    gates_high = lax.reduce_precision(gate_wide, 8, 7)
    gates_low = (gate_wide - gates_high).astype(BF16)
    back_out = after(back_out, blocks_x[0])
    routed_y = product("rt,rd->td", gates_high.astype(BF16), back_out) + product(
        "rt,rd->td", gates_low, back_out
    )
    layer_out = (mixed + shared_y + routed_y).astype(BF16)
    held = None
    for u in range(local_units):
        held = expert_grads(
            rows_in[u], grad_rows[u], *saved[u], per_device, u, blocks_x[-1] if u else None, held
        )
    owned_query = jnp.concatenate(
        [
            owned_first[:, : H * NOPE].reshape(own, H, NOPE),
            owned_first[:, H * NOPE : query_width].reshape(own, H, ROPE),
        ],
        axis=2,
    ).reshape(own, query_width)
    return (
        layer_out,
        input_grad,
        owned_first[:, gain_at],
        owned_query,
        owned_first[:, query_width:gain_at],
        owned_first[:half, gain_at + 2],
        jnp.concatenate([owned_up[:half], owned_up[half:]], axis=1),
        owned_output,
        owned_first[:, gain_at + 1],
        jnp.concatenate([owned_gate_out[:, :middle], owned_up_in], axis=1),
        owned_gate_out[:, middle:],
        held[0],
        held[1],
    )


def solution(mesh):
    rows = P("fsdp", None)
    flat = P("fsdp")
    cube = P("fsdp", None, None)
    in_specs = (rows,) * 5 + (flat, rows, rows, flat, rows, rows, flat, rows, rows, cube, cube)
    out_specs = (rows, rows, flat, rows, rows, flat, rows, rows, flat, rows, rows, cube, cube)
    return jax.shard_map(body, mesh=mesh, in_specs=in_specs, out_specs=out_specs, check_vma=False)
```

```python
import functools
import math

import jax
import jax.numpy as jnp
from jax import lax
from jax.experimental import pallas as pl
from jax.experimental.pallas import tpu as pltpu
from jax.sharding import PartitionSpec as P


D = 1024
H = 8
NOPE = 128
ROPE = 64
VDIM = 128
RANK = 512
EXPERTS = 64
CAP = 16
UW = H * (NOPE + VDIM) // 2
LW = RANK + ROPE

EPSILON = 1e-06
F32 = jnp.float32
BF16 = jnp.bfloat16


def matmul(left_side, right_side):
    return jnp.dot(left_side, right_side, preferred_element_type=F32)


def product(pattern, left_side, right_side):
    return jnp.einsum(pattern, left_side, right_side, preferred_element_type=F32)


def inverse_rms(values):
    return lax.rsqrt(jnp.mean(values * values, axis=-1, keepdims=True) + EPSILON)


def swiglu_parts(pre_act):
    middle = pre_act.shape[-1] // 2
    gate_pre = pre_act[..., :middle]
    up_pre = pre_act[..., middle:]
    return (gate_pre, up_pre, jax.nn.sigmoid(gate_pre))


def swiglu_forward(pre_act):
    gate_pre, up_pre, sigmoid_gate = swiglu_parts(pre_act)
    return (gate_pre * sigmoid_gate * up_pre).astype(BF16)


def swiglu_backward(pre_act, grad_act):
    gate_pre, up_pre, sigmoid_gate = swiglu_parts(pre_act)
    silu_value = gate_pre * sigmoid_gate
    slope = sigmoid_gate * (1.0 + gate_pre * (1.0 - sigmoid_gate))
    return jnp.concatenate([grad_act * up_pre * slope, grad_act * silu_value], axis=-1).astype(BF16)


def tables(documents):
    rows_here = documents.shape[0]
    indices = jnp.arange(rows_here, dtype=jnp.int32)
    same_doc = documents[:, None] == documents[None, :]
    starts = jnp.min(jnp.where(same_doc, indices[None, :], rows_here), axis=1)
    allowed = same_doc & (indices[None, :] <= indices[:, None])
    position = (indices - starts).astype(F32)
    frequency = jnp.exp(jnp.arange(ROPE // 2, dtype=F32) * (-2.0 * math.log(10000.0) / ROPE))
    angles = position[:, None] * frequency[None, :]
    return (allowed, jnp.cos(angles), jnp.sin(angles))


def nn(left_side, right_side):
    return lax.dot_general(
        left_side, right_side, (((1,), (0,)), ((), ())), preferred_element_type=F32
    )


def nt(left_side, right_side):
    return lax.dot_general(
        left_side, right_side, (((1,), (1,)), ((), ())), preferred_element_type=F32
    )


def tn(left_side, right_side):
    return lax.dot_general(
        left_side, right_side, (((0,), (0,)), ((), ())), preferred_element_type=F32
    )


def experts_kernel(rows, grads, w_in, w_out, dx, y, act, dpre, dx_sum, y_sum):
    piece = pl.program_id(1)
    middle = w_out.shape[1]
    pre_act = nn(rows[...], w_in[0])
    gate_pre = pre_act[:, :middle]
    up_pre = pre_act[:, middle:]
    sigmoid_gate = jax.nn.sigmoid(gate_pre)
    silu_value = gate_pre * sigmoid_gate
    act_low = (silu_value * up_pre).astype(BF16)
    act[0] = act_low
    grad_act = nt(grads[...], w_out[0])
    slope = sigmoid_gate * (1.0 + gate_pre * (1.0 - sigmoid_gate))
    dpre_low = jnp.concatenate([grad_act * up_pre * slope, grad_act * silu_value], axis=1).astype(BF16)
    dpre[0] = dpre_low
    dx_part = nt(dpre_low, w_in[0])
    y_part = nn(act_low, w_out[0])

    @pl.when(piece == 0)
    def _():
        dx_sum[...] = dx_part
        y_sum[...] = y_part

    @pl.when(piece > 0)
    def _():
        dx_sum[...] += dx_part
        y_sum[...] += y_part

    @pl.when(piece == pl.num_programs(1) - 1)
    def _():
        dx[...] = dx_sum[...].astype(BF16)
        y[...] = y_sum[...].astype(BF16)


def experts(rows, grads, w_in, w_out, unit, pieces):
    count, width = rows.shape
    first = unit * pieces
    double, middle = w_in.shape[2], w_out.shape[1]
    block = min(512, count)
    row_spec = pl.BlockSpec((block, width), lambda r, p: (r, 0))
    return pl.pallas_call(
        experts_kernel,
        grid=(count // block, pieces),
        in_specs=[
            row_spec,
            row_spec,
            pl.BlockSpec((1, width, double), lambda r, p: (first + p, 0, 0)),
            pl.BlockSpec((1, middle, width), lambda r, p: (first + p, 0, 0)),
        ],
        out_specs=[
            row_spec,
            row_spec,
            pl.BlockSpec((1, block, middle), lambda r, p: (p, r, 0)),
            pl.BlockSpec((1, block, double), lambda r, p: (p, r, 0)),
        ],
        out_shape=[
            jax.ShapeDtypeStruct((count, width), BF16),
            jax.ShapeDtypeStruct((count, width), BF16),
            jax.ShapeDtypeStruct((pieces, count, middle), BF16),
            jax.ShapeDtypeStruct((pieces, count, double), BF16),
        ],
        scratch_shapes=[pltpu.VMEM((block, width), F32), pltpu.VMEM((block, width), F32)],
        compiler_params=pltpu.CompilerParams(vmem_limit_bytes=60 * 2**20),
        cost_estimate=pl.CostEstimate(
            flops=2 * count * width * pieces * (2 * double + 2 * middle),
            bytes_accessed=pieces * (width + count) * (double + middle) * 2 + count * width * 8,
            transcendentals=count * middle * pieces,
        ),
        name="experts",
    )(rows, grads, w_in, w_out)


def expert_grads_kernel(rows, grads, act, dpre, *refs):
    grad_in, grad_out = refs[-2:]
    grad_in[0] = tn(rows[...], dpre[0])
    grad_out[0] = tn(act[0], grads[...])


def expert_grads(rows, grads, act, dpre, total, unit, late, held=None, chunk=256):
    count, width = rows.shape
    pieces, _, middle = act.shape
    first = unit * pieces
    double = dpre.shape[2]
    row_spec = pl.BlockSpec((count, chunk), lambda p, k: (0, k))
    operands = [rows, grads, act, dpre]
    in_specs = [
        row_spec,
        row_spec,
        pl.BlockSpec((1, count, middle), lambda p, k: (p, 0, 0)),
        pl.BlockSpec((1, count, double), lambda p, k: (p, 0, 0)),
    ]
    if late is not None:
        operands.append(late)
        in_specs.append(pl.BlockSpec(memory_space=pl.ANY))
    aliases = {}
    if held is not None:
        operands += list(held)
        in_specs += [pl.BlockSpec(memory_space=pl.ANY)] * 2
        aliases = {len(operands) - 2: 0, len(operands) - 1: 1}
    return pl.pallas_call(
        expert_grads_kernel,
        grid=(pieces, width // chunk),
        in_specs=in_specs,
        out_specs=[
            pl.BlockSpec((1, chunk, double), lambda p, k: (first + p, k, 0)),
            pl.BlockSpec((1, middle, chunk), lambda p, k: (first + p, 0, k)),
        ],
        out_shape=[
            jax.ShapeDtypeStruct((total, width, double), F32),
            jax.ShapeDtypeStruct((total, middle, width), F32),
        ],
        input_output_aliases=aliases,
        compiler_params=pltpu.CompilerParams(vmem_limit_bytes=60 * 2**20),
        cost_estimate=pl.CostEstimate(
            flops=2 * count * width * pieces * (double + middle),
            bytes_accessed=pieces * width * (double + middle) * 4 + count * width * 8,
            transcendentals=0,
        ),
        name="expert_grads",
    )(*operands)


def grads_kernel(*refs, plan, count):
    inputs, outs = refs[:-count], refs[-count:]
    rows = outs[0].shape[0]
    at = 0
    for width, starts in plan:
        left, right = [], []
        for start in starts:
            pair, inputs = inputs[:4], inputs[4:]
            left += [pair[0][...], pair[1][...]]
            right += [values[:, start : start + width] for values in pair[2:]]
        total = tn(jnp.concatenate(left, axis=0), jnp.concatenate(right, axis=0))
        for k, out in enumerate(outs):
            out[:, at : at + width] = total[k * rows : (k + 1) * rows].astype(BF16)
        at += width


def grads_of(segments, count):
    plan, operands, specs = [], [], []
    rows = segments[0][1][0][0].shape[1]

    def block(values, at, width):
        return pl.BlockSpec((values.shape[0], width), lambda _: (0, at // width))

    flops = 0
    for width, products in segments:
        starts = []
        for left_mine, left_other, right_mine, right_other, at in products:
            operands += [left_mine, left_other, right_mine, right_other]
            whole = at % width > 0
            starts.append(at if whole else 0)
            specs += [block(left_mine, 0, rows)] * 2
            specs += [block(right_mine, 0 if whole else at, right_mine.shape[1] if whole else width)] * 2
            flops += 4 * rows * width * left_mine.shape[0]
        plan.append((width, tuple(starts)))
    total = sum(width for width, _ in segments)
    return pl.pallas_call(
        functools.partial(grads_kernel, plan=tuple(plan), count=count),
        grid=(1,),
        in_specs=specs,
        out_specs=[pl.BlockSpec((rows // count, total), lambda _: (0, 0))] * count,
        out_shape=[jax.ShapeDtypeStruct((rows // count, total), BF16)] * count,
        compiler_params=pltpu.CompilerParams(vmem_limit_bytes=60 * 2**20),
        cost_estimate=pl.CostEstimate(
            flops=flops, bytes_accessed=4 * rows * total, transcendentals=0
        ),
    )(*operands)


def swap_halves(values):
    width = values.shape[1]
    lane = lax.broadcasted_iota(jnp.int32, values.shape, 1)
    return jnp.where(
        lane % ROPE < ROPE // 2,
        pltpu.roll(values, width - ROPE // 2, 1),
        pltpu.roll(values, ROPE // 2, 1),
    )


def repeated(table, times):
    return jnp.concatenate([table] * times, axis=1)


def upper_lanes(shape, head):
    return lax.broadcasted_iota(jnp.int32, shape, 1) // ROPE == head % 2


def lefts_and_rights(block, half, into):
    rows, width = block.shape
    if half % 16 == 0:
        cut = block.reshape(rows // (2 * half), 2 * half, width)
        return [
            cut[:, side * half : (side + 1) * half].reshape(rows // 2, width) for side in range(into)
        ]
    out = []
    for side in range(into):
        shape = (rows // 2, rows)
        row = lax.broadcasted_iota(jnp.int32, shape, 0)
        column = lax.broadcasted_iota(jnp.int32, shape, 1)
        wanted = row // half * (2 * half) + side * half + row % half
        out.append(nn((column == wanted).astype(BF16), block).astype(BF16))
    return out


def assemble(place, refs, targets, sems, size):
    if size is None:
        return [[pltpu.make_async_copy(ref, target, sems.at[i])] for i, (ref, target) in enumerate(zip(refs, targets))]
    core, spots = place[0], (place[1], place[2])
    out = []
    for i, target in enumerate(targets):
        copies = []
        for j in range(2 * size):
            spot = spots[i] ^ (j % size)
            here = core ^ (j // size)
            view = target.at[:, spot, :, here] if i == 0 else target.at[:, :, spot, here]
            at = 2 * size * i + j
            copies.append(pltpu.make_async_copy(refs[at], view, sems.at[at]))
        out.append(copies)
    return out


def flat(target):
    values = target[...]
    return values.reshape(D, values.shape[-1])


def attention_kernel(
    hidden,
    mask,
    cosine,
    sine,
    place,
    *refs,
    half,
    size,
):
    weights, refs = refs[:-16], refs[-16:]
    (
    normed_two,
    mixed_out,
    normed_one_out,
    latent_norm_out,
    latent_in_out,
    latent_scale_out,
    query_out,
    key_value_out,
    rope_key_out,
    probs_out,
    head_out,
    gains_out,
    ups_out,
    first_ref,
    second_ref,
    sems,
    ) = refs
    copies = assemble(place, weights, (first_ref, second_ref), sems, size)
    for copy in copies[0] + copies[1]:
        copy.start()
    hidden_wide = hidden[...].astype(F32)
    norm_one = hidden_wide * inverse_rms(hidden_wide)
    for copy in copies[0]:
        copy.wait()
    first = flat(first_ref)
    tail = first[:, first.shape[1] - 128 :]
    picked = lax.broadcasted_iota(jnp.int32, (16, 128), 1) == ROPE + lax.broadcasted_iota(
        jnp.int32, (16, 128), 0
    )
    picked = picked.astype(BF16)
    gains = nt(picked, tail)
    latent_gains = nt(picked, lefts_and_rights(tail, half, 1)[0])
    gains_out[...] = jnp.concatenate(
        [gains[:2], jnp.concatenate([latent_gains[2:3], jnp.zeros((1, D - RANK), F32)], axis=1),
         jnp.zeros((5, D), F32)], axis=0
    )
    normed_one = (norm_one * gains[0:1]).astype(BF16)
    normed_one_out[...] = normed_one
    projected = nn(normed_one, first)
    nope_width = H * NOPE
    query_width = H * (NOPE + ROPE)
    latent_part = projected[:, query_width : query_width + RANK]
    latent_scale = inverse_rms(latent_part)
    latent_norm = latent_part * latent_scale
    latent_in = (latent_norm * latent_gains[2:3]).astype(BF16)
    latent_norm_out[...] = latent_norm
    latent_in_out[...] = latent_in
    latent_scale_out[...] = jnp.broadcast_to(latent_scale, latent_scale_out.shape)
    cos, sin = cosine[...], sine[...]
    rope = projected[:, nope_width:query_width]
    rope = rope * repeated(cos, H // 2) + swap_halves(rope) * repeated(sin, H // 2)
    query_out[:, :nope_width] = projected[:, :nope_width].astype(BF16)
    query_out[:, nope_width:] = rope.astype(BF16)
    key = projected[:, query_width + RANK : query_width + RANK + 128]
    key = jnp.where(upper_lanes(key.shape, 0), key, 0.0)
    key = key + pltpu.roll(key, ROPE, 1)
    rope_key = (key * cos + swap_halves(key) * sin).astype(BF16)
    rope_key_out[...] = rope_key
    for copy in copies[1]:
        copy.wait()
    second = flat(second_ref)
    for side, part in enumerate(lefts_and_rights(second[:, H * VDIM :], half, 2)):
        ups_out[side] = part
        key_value_out[:, side * UW : (side + 1) * UW] = nn(latent_in, part).astype(BF16)
    scaling = (NOPE + ROPE) ** (-0.5)
    allowed = mask[...]
    for head in range(H):
        pair = query_out[:, nope_width + head // 2 * 128 : nope_width + head // 2 * 128 + 128]
        pair = jnp.where(upper_lanes(pair.shape, head), pair, jnp.zeros_like(pair))
        query = jnp.concatenate([query_out[:, head * NOPE : (head + 1) * NOPE], pair], axis=1)
        at = head * (NOPE + VDIM)
        keys = jnp.concatenate([key_value_out[:, at : at + NOPE], rope_key], axis=1)
        scores = nt(query, keys) * scaling
        raised = jnp.exp(scores) * allowed
        probs = raised / jnp.sum(raised, axis=-1, keepdims=True)
        probs_out[head] = probs
        head_out[:, head * VDIM : (head + 1) * VDIM] = nn(
            probs.astype(BF16), key_value_out[:, at + NOPE : at + NOPE + VDIM]
        ).astype(BF16)
    mixed = hidden_wide + nt(head_out[...], second[:, : H * VDIM])
    mixed_out[...] = mixed
    normed_two[...] = (mixed * inverse_rms(mixed) * gains[1:2]).astype(BF16)


def weight_scratch(weights, size):
    if size is None:
        return [pltpu.VMEM(values.shape, BF16) for values in weights] + [
            pltpu.SemaphoreType.DMA((len(weights),))
        ]
    out = []
    for i in range(2):
        part = weights[2 * size * i].shape
        shape = (part[0], size, part[1], 2) if i == 0 else (part[0], part[1], size, 2)
        out.append(pltpu.VMEM(shape + part[2:], BF16))
    return out + [pltpu.SemaphoreType.DMA((len(weights),))]


def attention(hidden, mask, cosine, sine, place, weights, half, size):
    rows, width = hidden.shape
    query_width = H * (NOPE + ROPE)
    first_width = query_width + RANK + 128
    vmem = pl.BlockSpec(memory_space=pltpu.VMEM)
    smem = pl.BlockSpec(memory_space=pltpu.SMEM)
    shapes = [
        ((rows, width), BF16),
        ((rows, width), F32),
        ((rows, width), BF16),
        ((rows, RANK), F32),
        ((rows, RANK), BF16),
        ((rows, 128), F32),
        ((rows, query_width), BF16),
        ((rows, 2 * UW), BF16),
        ((rows, 128), BF16),
        ((H, rows, rows), F32),
        ((rows, H * VDIM), BF16),
        ((8, width), F32),
        ((2, RANK, UW), BF16),
    ]
    return pl.pallas_call(
        functools.partial(attention_kernel, half=half, size=size),
        in_specs=[vmem] * 4 + [smem] + [pl.BlockSpec(memory_space=pl.ANY)] * len(weights),
        out_specs=[vmem] * len(shapes),
        out_shape=[jax.ShapeDtypeStruct(shape, dtype) for shape, dtype in shapes],
        scratch_shapes=weight_scratch(weights, size),
        compiler_params=pltpu.CompilerParams(vmem_limit_bytes=60 * 2**20),
        cost_estimate=pl.CostEstimate(
            flops=2 * rows * width * (first_width + 3 * width),
            bytes_accessed=2 * width * (first_width + 2 * width) + 8 * rows * width,
            transcendentals=H * rows * rows,
        ),
        name="attention",
    )(hidden, mask, cosine, sine, place, *weights)


def combined_kernel(mixed, shared_y, gates_high, gates_low, rows, out):
    routed = tn(gates_high[...], rows[...]) + tn(gates_low[...], rows[...])
    out[...] = (mixed[...] + shared_y[...] + routed).astype(BF16)


def combined(mixed, shared_y, gates_high, gates_low, rows):
    vmem = pl.BlockSpec(memory_space=pltpu.VMEM)
    return pl.pallas_call(
        combined_kernel,
        in_specs=[vmem] * 5,
        out_specs=vmem,
        out_shape=jax.ShapeDtypeStruct(mixed.shape, BF16),
        compiler_params=pltpu.CompilerParams(vmem_limit_bytes=60 * 2**20),
        cost_estimate=pl.CostEstimate(
            flops=4 * rows.size * mixed.shape[0], bytes_accessed=2 * rows.size, transcendentals=0
        ),
        name="combined",
    )(mixed, shared_y, gates_high, gates_low, rows)


def mixed_back_kernel(*refs):
    count = (len(refs) - 7) // 2
    shared_dx, out_grad, mixed, gains = refs[:4]
    selectors, back = refs[4 : 4 + count], refs[4 + count : 4 + 2 * count]
    grad_mixed_out, mixed_low, gain_out = refs[4 + 2 * count :]
    grad = shared_dx[...]
    for selector, rows in zip(selectors, back):
        grad = grad + tn(selector[...], rows[...])
    scale = inverse_rms(mixed[...])
    norm_two = mixed[...] * scale
    gain_out[...] = jnp.broadcast_to(jnp.sum(grad * norm_two, axis=0, keepdims=True), gain_out.shape)
    grad_norm = grad * gains[1:2]
    grad_mixed = out_grad[...].astype(F32) + scale * (
        grad_norm - norm_two * jnp.mean(grad_norm * norm_two, axis=-1, keepdims=True)
    )
    grad_mixed_out[...] = grad_mixed
    mixed_low[...] = grad_mixed.astype(BF16)


def mixed_back(shared_dx, out_grad, mixed, gains, selectors, back):
    rows, width = mixed.shape
    vmem = pl.BlockSpec(memory_space=pltpu.VMEM)
    total = sum(values.shape[0] for values in back)
    return pl.pallas_call(
        mixed_back_kernel,
        in_specs=[vmem] * (4 + 2 * len(back)),
        out_specs=[vmem] * 3,
        out_shape=[
            jax.ShapeDtypeStruct((rows, width), F32),
            jax.ShapeDtypeStruct((rows, width), BF16),
            jax.ShapeDtypeStruct((8, width), F32),
        ],
        compiler_params=pltpu.CompilerParams(vmem_limit_bytes=60 * 2**20),
        cost_estimate=pl.CostEstimate(
            flops=2 * rows * width * total, bytes_accessed=2 * total * width, transcendentals=0
        ),
        name="mixed_back",
    )(shared_dx, out_grad, mixed, gains, *selectors, *back)


def attention_back_kernel(
    hidden,
    grad_mixed,
    mixed_low,
    cosine,
    sine,
    latent_norm,
    latent_scale,
    query,
    key_value,
    rope_key,
    probs,
    head_out,
    gains,
    ups,
    place,
    *refs,
    size,
):
    weights, refs = refs[:-6], refs[-6:]
    back, input_grad, gain_out, first_ref, second_ref, sems = refs
    copies = assemble(place, weights, (first_ref, second_ref), sems, size)
    for copy in copies[1] + copies[0]:
        copy.start()
    grad_projected = back.at[:, 2 * UW :]
    grad_key_value = back.at[:, : 2 * UW]
    for copy in copies[1]:
        copy.wait()
    output = flat(second_ref)[:, : H * VDIM]
    rows = hidden.shape[0]
    nope_width = H * NOPE
    query_width = H * (NOPE + ROPE)
    scaling = (NOPE + ROPE) ** (-0.5)
    heads = nn(mixed_low[...], output).astype(BF16)
    rope_sum = jnp.zeros((rows, 128), F32)
    rope_grads = []
    for head in range(H):
        grad_head = heads[:, head * VDIM : (head + 1) * VDIM]
        at = head * (NOPE + VDIM)
        weights_here = probs[head]
        own_lanes = upper_lanes((rows, 128), head)
        pair = query[:, nope_width + head // 2 * 128 : nope_width + head // 2 * 128 + 128]
        pair = jnp.where(own_lanes, pair, jnp.zeros_like(pair))
        query_here = jnp.concatenate([query[:, head * NOPE : (head + 1) * NOPE], pair], axis=1)
        keys = jnp.concatenate([key_value[:, at : at + NOPE], rope_key[...]], axis=1)
        grad_probs = nt(grad_head, key_value[:, at + NOPE : at + NOPE + VDIM])
        delta = jnp.sum(
            grad_head.astype(F32) * head_out[:, head * VDIM : (head + 1) * VDIM].astype(F32),
            axis=-1,
            keepdims=True,
        )
        grad_scores = (weights_here * (grad_probs - delta) * scaling).astype(BF16)
        grad_query = nn(grad_scores, keys)
        grad_projected[:, head * NOPE : (head + 1) * NOPE] = grad_query[:, :NOPE].astype(BF16)
        rope_grads.append(jnp.where(own_lanes, grad_query[:, NOPE:], 0.0))
        grad_keys = tn(grad_scores, query_here)
        rope_sum = rope_sum + grad_keys[:, NOPE:]
        grad_key_value[:, at : at + NOPE] = grad_keys[:, :NOPE].astype(BF16)
        grad_key_value[:, at + NOPE : at + NOPE + VDIM] = tn(
            weights_here.astype(BF16), grad_head
        ).astype(BF16)
    cos, sin = cosine[...], sine[...]
    rope = jnp.concatenate(
        [rope_grads[2 * pair] + rope_grads[2 * pair + 1] for pair in range(H // 2)], axis=1
    )
    rope = rope * repeated(cos, H // 2) - swap_halves(rope) * repeated(sin, H // 2)
    grad_projected[:, nope_width:query_width] = rope.astype(BF16)
    key = rope_sum + pltpu.roll(rope_sum, ROPE, 1)
    key = key * cos - swap_halves(key) * sin
    key = jnp.where(upper_lanes(key.shape, 0), key, 0.0)
    grad_projected[:, query_width + RANK :] = key.astype(BF16)
    grad_latent_in = nt(grad_key_value[:, :UW], ups[0]) + nt(grad_key_value[:, UW:], ups[1])
    norm = latent_norm[...]
    latent_gain_grad = jnp.sum(grad_latent_in * norm, axis=0, keepdims=True)
    grad_norm = grad_latent_in * gains[2:3, :RANK]
    grad_latent = latent_scale[:, 0:1] * (
        grad_norm - norm * jnp.mean(grad_norm * norm, axis=-1, keepdims=True)
    )
    grad_projected[:, query_width : query_width + RANK] = grad_latent.astype(BF16)
    for copy in copies[0]:
        copy.wait()
    grad_normed = nt(grad_projected[...], flat(first_ref))
    hidden_wide = hidden[...].astype(F32)
    scale = inverse_rms(hidden_wide)
    norm_one = hidden_wide * scale
    gain_out[...] = jnp.concatenate(
        [
            jnp.sum(grad_normed * norm_one, axis=0, keepdims=True),
            jnp.concatenate([latent_gain_grad, jnp.zeros((1, D - RANK), F32)], axis=1),
            jnp.zeros((6, D), F32),
        ],
        axis=0,
    )
    grad_norm = grad_normed * gains[0:1]
    input_grad[...] = grad_mixed[...] + scale * (
        grad_norm - norm_one * jnp.mean(grad_norm * norm_one, axis=-1, keepdims=True)
    )


def attention_back(operands, place, weights, size):
    hidden = operands[0]
    rows, width = hidden.shape
    first_width = H * (NOPE + ROPE) + RANK + 128
    vmem = pl.BlockSpec(memory_space=pltpu.VMEM)
    return pl.pallas_call(
        functools.partial(attention_back_kernel, size=size),
        in_specs=[vmem] * len(operands)
        + [pl.BlockSpec(memory_space=pltpu.SMEM)]
        + [pl.BlockSpec(memory_space=pl.ANY)] * len(weights),
        out_specs=[vmem] * 3,
        out_shape=[
            jax.ShapeDtypeStruct((rows, first_width + 2 * UW), BF16),
            jax.ShapeDtypeStruct((rows, width), F32),
            jax.ShapeDtypeStruct((8, width), F32),
        ],
        scratch_shapes=weight_scratch(weights, size),
        compiler_params=pltpu.CompilerParams(vmem_limit_bytes=60 * 2**20),
        cost_estimate=pl.CostEstimate(
            flops=2 * rows * width * (first_width + 3 * width),
            bytes_accessed=2 * width * (first_width + 2 * width) + 8 * rows * width,
            transcendentals=0,
        ),
        name="attention_back",
    )(*operands, place, *weights)


def after_kernel(values, late, out):
    pass


def after(values, late):
    anywhere = pl.BlockSpec(memory_space=pl.ANY)
    return pl.pallas_call(
        after_kernel,
        in_specs=[anywhere, anywhere],
        out_specs=anywhere,
        out_shape=jax.ShapeDtypeStruct(values.shape, values.dtype),
        input_output_aliases={0: 0},
        cost_estimate=pl.CostEstimate(flops=0, bytes_accessed=0, transcendentals=0),
        name="after",
    )(values, late)


def axes_of(devices):
    return {32: ((8, 4), (4, 2), (2, 2)), 128: ((32, 4), (8, 4), (2, 4))}[devices]


def swap_with(values, devices, offset):
    return lax.ppermute(values, "fsdp", [(i, i ^ offset) for i in range(devices)])


def pick(values, index, axis):
    return lax.dynamic_index_in_dim(values, index, axis, keepdims=False)


def row_order(devices, axis, half=None):
    me = lax.axis_index("fsdp")
    own = D // devices
    axes = axes_of(devices)
    to = jnp.arange(D, dtype=jnp.int32)
    chip_row = to % (D // 2)
    stride, size = axes[axis]
    block = chip_row // (D // 2 // size)
    rest = chip_row % (D // 2 // size) // own
    device = (me % 2) ^ (to // (D // 2))
    device = device + (((me // stride) % size) ^ block) * stride
    for other in (2, 1, 0):
        if other != axis:
            device = device + rest % axes[other][1] * axes[other][0]
            rest = rest // axes[other][1]
    row = to % own
    if half is None:
        source = device * own + row
        return (jnp.arange(D, dtype=jnp.int32)[:, None] == source[None, :]).astype(BF16)
    source = device * half + row % half
    hit = jnp.arange(D // 2, dtype=jnp.int32)[:, None] == source[None, :]
    return [(hit & (row // half == side)[None, :]).astype(BF16) for side in range(2)]


def scatter_sum(blocks, devices, order, late=()):
    me = lax.axis_index("fsdp")
    axes = axes_of(devices)
    left = [0, 1, 2]
    values = None
    for axis in order:
        stride, size = axes[axis]
        at = left.index(axis)
        left.remove(axis)
        mine = (me // stride) % size
        if values is not None:
            blocks = [pick(values, mine ^ k, at) for k in range(size)]
        total = blocks[0]
        if late:
            for values in late[0]:
                total = after(total, values)
            late = late[1:]
        total = total.astype(F32)
        parts = [swap_with(blocks[k], devices, k * stride) for k in range(1, size)]
        for part in parts:
            total = total + part.astype(F32)
        values = total if not left else total.astype(BF16)
        if values.ndim == 2 and left:
            values = values.reshape(
                *(axes[other][1] for other in left), D // devices, values.shape[-1]
            )
    return values


def gather_start(shard, devices, order):
    me = lax.axis_index("fsdp")
    axes = axes_of(devices)
    have = []
    values = shard
    for axis in order:
        stride, size = axes[axis]
        mine = (me // stride) % size
        at = sum(other < axis for other in have)
        have.append(axis)
        parts = [values] + [swap_with(values, devices, k * stride) for k in range(1, size)]
        if len(have) < 3:
            values = placed_along(parts, mine, at)
    return (parts, mine, at)


def placed_along(parts, mine, at):
    if len(parts) == 2:
        return jnp.where(mine == 0, jnp.stack(parts, at), jnp.stack(parts[::-1], at))
    shape = parts[0].shape
    values = jnp.zeros(shape[:at] + (len(parts),) + shape[at:], parts[0].dtype)
    for k, part in enumerate(parts):
        values = lax.dynamic_update_index_in_dim(values, part, mine ^ k, at)
    return values


def gather_finish(started, devices):
    parts, mine, at = started
    values = placed_along(parts, mine, at)
    other = swap_with(values, devices, 1)
    first = lax.axis_index("fsdp") % 2 == 0
    pair = jnp.where(first, jnp.stack([values, other], 3), jnp.stack([other, values], 3))
    return pair.reshape(-1, values.shape[-1])


def body(
    hidden_in,
    out_grad,
    doc_ids,
    routes,
    gate_values,
    attn_gain,
    query_proj,
    latent_proj,
    latent_gain,
    latent_up,
    output_proj,
    ffn_gain,
    shared_in,
    shared_out,
    expert_in,
    expert_out,
):
    devices = lax.axis_size("fsdp")
    rows_here = hidden_in.shape[0]
    own = D // devices
    half = own // 2
    me = lax.axis_index("fsdp")

    along_x, along_y = row_order(devices, 2), row_order(devices, 1)
    sides_x, sides_y = row_order(devices, 2, half), row_order(devices, 1, half)

    def mine_and_other(columns, order):
        placed = matmul(columns, order).astype(BF16)
        return (placed[:, : D // 2], swap_with(placed[:, D // 2 :], devices, 1))

    spare = 128 - LW % 128
    query_width, output_width = query_proj.shape[1], output_proj.shape[1]
    gain_at = query_width + LW
    output_at = gain_at + spare
    by_head = query_proj.reshape(own, H, NOPE + ROPE)
    started = [
        gather_start(
            jnp.concatenate(
                [
                    by_head[:, :, :NOPE].reshape(own, H * NOPE),
                    by_head[:, :, NOPE:].reshape(own, H * ROPE),
                    latent_proj,
                    attn_gain[:, None],
                    ffn_gain[:, None],
                    jnp.concatenate([latent_gain, jnp.zeros_like(latent_gain)])[:, None],
                    jnp.zeros((own, spare - 3), BF16),
                ],
                axis=1,
            ),
            devices,
            (0, 2, 1),
        ),
        gather_start(
            jnp.concatenate(
                [output_proj, jnp.concatenate([latent_up[:, :UW], latent_up[:, UW:]], axis=0)],
                axis=1,
            ),
            devices,
            (0, 1, 2),
        ),
    ]
    place = jnp.stack([me % 2, started[0][1], started[1][1]]).astype(jnp.int32)
    if own % 16 == 0:
        size = len(started[0][0])
        attention_weights = []
        for parts, _, _ in started:
            attention_weights += parts + [swap_with(part, devices, 1) for part in parts]
    else:
        size = None
        attention_weights = [gather_finish(begun, devices) for begun in started]

    per_device = expert_in.shape[0]
    pieces = 2 if per_device % 2 == 0 else 1
    units = 2 * EXPERTS // pieces
    local_units = units // devices
    token = jnp.arange(rows_here, dtype=jnp.int32)
    earlier = (token[None, :] < token[:, None]).astype(BF16)

    def routing(names, values, base, count):
        unit_expert = (base + jnp.arange(count, dtype=jnp.int32)) // (2 // pieces)
        named = names[:, :, None] == unit_expert[None, None, :]
        hits = jnp.any(named, axis=1)
        gates = jnp.sum(jnp.where(named, values[:, :, None], 0.0), axis=1)
        slots = matmul(earlier, hits.astype(BF16)).astype(jnp.int32)
        return (jnp.where(hits, slots, CAP).T, gates.T)

    slots, gates = routing(routes, gate_values, 0, units)
    chosen = slots[:, None, :] == jnp.arange(CAP, dtype=jnp.int32)[None, :, None]
    gate_wide = jnp.where(chosen, gates[:, None, :], 0.0).reshape(units * CAP, rows_here)
    gate_rows = jnp.sum(gate_wide, axis=-1, keepdims=True)
    selector = chosen.astype(BF16)
    unit_selector = selector.reshape(devices, local_units, CAP, rows_here)
    unit_selector = [
        unit_selector[:, u].reshape(devices * CAP, rows_here) for u in range(local_units)
    ]
    selector = selector.reshape(units * CAP, rows_here)

    def exchange(rows):
        return lax.all_to_all(rows, "fsdp", split_axis=0, concat_axis=0, tiled=True)

    def exchange_unit(rows):
        return exchange(rows.reshape(devices, CAP, D)).reshape(devices * CAP, D)

    grads_out = (gate_rows * matmul(selector, out_grad)).astype(BF16)
    grad_rows = exchange(grads_out.reshape(devices, local_units * CAP, D))
    grad_rows = grad_rows.reshape(devices, local_units, CAP, D)
    grad_rows = [grad_rows[:, u].reshape(devices * CAP, D) for u in range(local_units)]

    allowed, cosine_table, sine_table = tables(doc_ids[0])
    cosine_lanes = jnp.concatenate([cosine_table] * 4, axis=1)
    sine_lanes = jnp.concatenate([-sine_table, sine_table] * 2, axis=1)
    (
        normed_two,
        mixed,
        normed_one,
        latent_norm,
        latent_in,
        latent_scale,
        queries,
        key_values,
        rope_key,
        probs,
        head_out,
        gain_rows,
        ups,
    ) = attention(hidden_in, allowed.astype(F32), cosine_lanes, sine_lanes, place, attention_weights, half, size)

    rows_out = [matmul(unit_selector[u], normed_two).astype(BF16) for u in range(local_units)]
    rows_in = []
    for rows in rows_out:
        rows_in.append(exchange_unit(rows))

    shared_rows = after(normed_two, rows_out[0])
    full_shared_in = gather_finish(gather_start(shared_in, devices, (0, 2, 1)), devices)
    full_shared_out = gather_finish(gather_start(shared_out, devices, (0, 1, 2)), devices)
    shared_pre = matmul(shared_rows, full_shared_in)
    shared_act = swiglu_forward(shared_pre)
    grad_shared_act = matmul(out_grad, full_shared_out)
    grad_shared_pre = swiglu_backward(shared_pre, grad_shared_act)
    middle = shared_out.shape[1]
    dpre_pair = (grad_shared_pre, swap_with(grad_shared_pre, devices, 1))
    act_pair = (shared_act, swap_with(shared_act, devices, 1))
    size_x, size_y = axes_of(devices)[2][1], axes_of(devices)[1][1]
    normed_left = [mine_and_other(normed_two, along) for along in (along_x, along_y)]
    cotangent_left = mine_and_other(out_grad, along_x)
    blocks_x = grads_of(
        (
            (middle, ((*normed_left[0], *dpre_pair, 0),)),
            (middle, ((*cotangent_left, *act_pair, 0),)),
        ),
        size_x,
    )
    blocks_y = grads_of(((middle, ((*normed_left[1], *dpre_pair, middle),)),), size_y)
    shared_blocks = (blocks_x, blocks_y)
    shared_y = product("tf,df->td", shared_act, full_shared_out)
    shared_dx = product("tf,df->td", grad_shared_pre, full_shared_in)

    back_dx, back_out, saved = [], [], []
    for u in range(local_units):
        dx_rows, y_rows, activation, grad_pre = experts(
            rows_in[u], grad_rows[u], expert_in, expert_out, u, pieces
        )
        back_dx.append(exchange_unit(dx_rows))
        back_out.append(y_rows.reshape(devices, CAP, D))
        saved.append((activation, grad_pre))
    back_out = jnp.concatenate(back_out, axis=1)
    for rows in back_dx:
        back_out = after(back_out, rows)
    back_out = exchange(back_out).reshape(units * CAP, D)

    grad_mixed, mixed_low, ffn_gain_grad = mixed_back(
        shared_dx, out_grad, mixed, gain_rows, unit_selector, back_dx
    )

    heads_pair = (head_out, swap_with(head_out, devices, 1))
    first_left = mine_and_other(normed_one, along_y)
    up_left = [mine_and_other(latent_in, side) for side in sides_x]
    output_left = mine_and_other(mixed_low, along_x)
    back, input_grad, other_gain_grads = attention_back(
        (
            hidden_in,
            grad_mixed,
            mixed_low,
            cosine_lanes,
            sine_lanes,
            latent_norm,
            latent_scale,
            queries,
            key_values,
            rope_key,
            probs,
            head_out,
            gain_rows,
            ups,
        ),
        place,
        attention_weights,
        size,
    )
    back_pair = (back, swap_with(back, devices, 1))
    gain_grads = jnp.concatenate(
        [other_gain_grads[:1], ffn_gain_grad[:1], jnp.zeros((6, D), F32)], axis=0
    ).astype(BF16)
    placed = matmul(gain_grads, along_y) + jnp.pad(
        matmul(other_gain_grads[1:7, :RANK].astype(BF16), sides_y[0]), ((2, 0), (0, 0))
    )
    placed = placed.astype(BF16)
    gain_left = (placed[:, : D // 2], swap_with(placed[:, D // 2 :], devices, 1))
    row = jnp.arange(8, dtype=jnp.int32)[:, None]
    lane = jnp.arange(output_at, dtype=jnp.int32)[None, :]
    gain_right = ((row < 3) & (lane == gain_at + row)).astype(BF16)
    blocks_y = grads_of(
        (
            (
                output_at,
                ((*first_left, *back_pair, 2 * UW), (*gain_left, gain_right, gain_right, 0)),
            ),
        ),
        size_y,
    )
    owned_first = scatter_sum(blocks_y, devices, (1, 2, 0))
    blocks_x = grads_of(
        (
            (output_width, ((*output_left, *heads_pair, 0),)),
            (UW, tuple((*up_left[i], *back_pair, i * UW) for i in range(2))),
        ),
        size_x,
    )
    gates_high = lax.reduce_precision(gate_wide, 8, 7)
    gates_low = (gate_wide - gates_high).astype(BF16)
    layer_out = combined(mixed, shared_y, gates_high.astype(BF16), gates_low, back_out)
    owned_second = scatter_sum(blocks_x, devices, (2, 1, 0))
    shared_late = ((blocks_x[0], blocks_y[0]),)
    owned_gate_out = scatter_sum(shared_blocks[0], devices, (2, 1, 0), shared_late)
    owned_up_in = scatter_sum(shared_blocks[1], devices, (1, 2, 0), shared_late)
    owned_output, owned_up = owned_second[:, :output_width], owned_second[:, output_width:]
    held = None
    for u in range(local_units):
        held = expert_grads(
            rows_in[u], grad_rows[u], *saved[u], per_device, u, blocks_x[-1] if u else None, held
        )
    owned_query = jnp.concatenate(
        [
            owned_first[:, : H * NOPE].reshape(own, H, NOPE),
            owned_first[:, H * NOPE : query_width].reshape(own, H, ROPE),
        ],
        axis=2,
    ).reshape(own, query_width)
    return (
        layer_out,
        input_grad,
        owned_first[:, gain_at],
        owned_query,
        owned_first[:, query_width:gain_at],
        owned_first[:half, gain_at + 2],
        jnp.concatenate([owned_up[:half], owned_up[half:]], axis=1),
        owned_output,
        owned_first[:, gain_at + 1],
        jnp.concatenate([owned_gate_out[:, :middle], owned_up_in], axis=1),
        owned_gate_out[:, middle:],
        held[0],
        held[1],
    )


def solution(mesh):
    rows = P("fsdp", None)
    flat = P("fsdp")
    cube = P("fsdp", None, None)
    in_specs = (rows,) * 5 + (flat, rows, rows, flat, rows, rows, flat, rows, rows, cube, cube)
    out_specs = (rows, rows, flat, rows, rows, flat, rows, rows, flat, rows, rows, cube, cube)
    return jax.shard_map(body, mesh=mesh, in_specs=in_specs, out_specs=out_specs, check_vma=False)
```

```python
import functools
import math

import jax
import jax.numpy as jnp
from jax import lax
from jax.experimental import pallas as pl
from jax.experimental.pallas import tpu as pltpu
from jax.sharding import PartitionSpec as P


D = 1024
H = 8
NOPE = 128
ROPE = 64
VDIM = 128
RANK = 512
EXPERTS = 64
CAP = 16
UW = H * (NOPE + VDIM) // 2
LW = RANK + ROPE

EPSILON = 1e-06
F32 = jnp.float32
BF16 = jnp.bfloat16


def matmul(left_side, right_side):
    return jnp.dot(left_side, right_side, preferred_element_type=F32)


def inverse_rms(values):
    return lax.rsqrt(jnp.mean(values * values, axis=-1, keepdims=True) + EPSILON)


def swiglu_parts(pre_act):
    middle = pre_act.shape[-1] // 2
    gate_pre = pre_act[..., :middle]
    up_pre = pre_act[..., middle:]
    return (gate_pre, up_pre, jax.nn.sigmoid(gate_pre))


def swiglu_forward(pre_act):
    gate_pre, up_pre, sigmoid_gate = swiglu_parts(pre_act)
    return (gate_pre * sigmoid_gate * up_pre).astype(BF16)


def swiglu_backward(pre_act, grad_act):
    gate_pre, up_pre, sigmoid_gate = swiglu_parts(pre_act)
    silu_value = gate_pre * sigmoid_gate
    slope = sigmoid_gate * (1.0 + gate_pre * (1.0 - sigmoid_gate))
    return jnp.concatenate([grad_act * up_pre * slope, grad_act * silu_value], axis=-1).astype(BF16)


def tables(documents):
    rows_here = documents.shape[0]
    indices = jnp.arange(rows_here, dtype=jnp.int32)
    same_doc = documents[:, None] == documents[None, :]
    starts = jnp.min(jnp.where(same_doc, indices[None, :], rows_here), axis=1)
    allowed = same_doc & (indices[None, :] <= indices[:, None])
    position = (indices - starts).astype(F32)
    frequency = jnp.exp(jnp.arange(ROPE // 2, dtype=F32) * (-2.0 * math.log(10000.0) / ROPE))
    angles = position[:, None] * frequency[None, :]
    return (allowed, jnp.cos(angles), jnp.sin(angles))


def nn(left_side, right_side):
    return lax.dot_general(
        left_side, right_side, (((1,), (0,)), ((), ())), preferred_element_type=F32
    )


def nt(left_side, right_side):
    return lax.dot_general(
        left_side, right_side, (((1,), (1,)), ((), ())), preferred_element_type=F32
    )


def tn(left_side, right_side):
    return lax.dot_general(
        left_side, right_side, (((0,), (0,)), ((), ())), preferred_element_type=F32
    )


def experts_kernel(rows, grads, w_in, w_out, dx, y, act, dpre, dx_sum, y_sum):
    piece = pl.program_id(0)
    block = rows.shape[0]
    here = pl.ds(pl.program_id(1) * block, block)
    middle = w_out.shape[1]
    pre_act = nn(rows[...], w_in[0])
    gate_pre = pre_act[:, :middle]
    up_pre = pre_act[:, middle:]
    sigmoid_gate = jax.nn.sigmoid(gate_pre)
    silu_value = gate_pre * sigmoid_gate
    act_low = (silu_value * up_pre).astype(BF16)
    act[0] = act_low
    grad_act = nt(grads[...], w_out[0])
    slope = sigmoid_gate * (1.0 + gate_pre * (1.0 - sigmoid_gate))
    dpre_low = jnp.concatenate([grad_act * up_pre * slope, grad_act * silu_value], axis=1).astype(BF16)
    dpre[0] = dpre_low
    dx_part = nt(dpre_low, w_in[0])
    y_part = nn(act_low, w_out[0])

    @pl.when(piece == 0)
    def _():
        dx_sum[here] = dx_part
        y_sum[here] = y_part

    @pl.when(piece > 0)
    def _():
        dx_sum[here] += dx_part
        y_sum[here] += y_part

    @pl.when(piece == pl.num_programs(0) - 1)
    def _():
        dx[...] = dx_sum[here].astype(BF16)
        y[...] = y_sum[here].astype(BF16)


def experts(rows, grads, w_in, w_out, unit, pieces):
    count, width = rows.shape
    first = unit * pieces
    double, middle = w_in.shape[2], w_out.shape[1]
    block = min(256, count)
    row_spec = pl.BlockSpec((block, width), lambda p, r: (r, 0))
    last_spec = pl.BlockSpec((block, width), lambda p, r: (jnp.where(p == pieces - 1, r, 0), 0))
    return pl.pallas_call(
        experts_kernel,
        grid=(pieces, count // block),
        in_specs=[
            row_spec,
            row_spec,
            pl.BlockSpec((1, width, double), lambda p, r: (first + p, 0, 0)),
            pl.BlockSpec((1, middle, width), lambda p, r: (first + p, 0, 0)),
        ],
        out_specs=[
            last_spec,
            last_spec,
            pl.BlockSpec((1, block, middle), lambda p, r: (p, r, 0)),
            pl.BlockSpec((1, block, double), lambda p, r: (p, r, 0)),
        ],
        out_shape=[
            jax.ShapeDtypeStruct((count, width), BF16),
            jax.ShapeDtypeStruct((count, width), BF16),
            jax.ShapeDtypeStruct((pieces, count, middle), BF16),
            jax.ShapeDtypeStruct((pieces, count, double), BF16),
        ],
        scratch_shapes=[pltpu.VMEM((count, width), F32), pltpu.VMEM((count, width), F32)],
        compiler_params=pltpu.CompilerParams(vmem_limit_bytes=60 * 2**20),
        cost_estimate=pl.CostEstimate(
            flops=2 * count * width * pieces * (2 * double + 2 * middle),
            bytes_accessed=pieces * (width + count) * (double + middle) * 2 + count * width * 8,
            transcendentals=count * middle * pieces,
        ),
        name="experts",
    )(rows, grads, w_in, w_out)


def expert_grads_kernel(rows, grads, act, dpre, *refs):
    grad_in, grad_out = refs[-2:]
    grad_in[0] = tn(rows[...], dpre[0])
    grad_out[0] = tn(act[0], grads[...])


def expert_grads(rows, grads, act, dpre, total, unit, late, held=None, chunk=256):
    count, width = rows.shape
    pieces, _, middle = act.shape
    first = unit * pieces
    double = dpre.shape[2]
    row_spec = pl.BlockSpec((count, chunk), lambda p, k: (0, k))
    operands = [rows, grads, act, dpre]
    in_specs = [
        row_spec,
        row_spec,
        pl.BlockSpec((1, count, middle), lambda p, k: (p, 0, 0)),
        pl.BlockSpec((1, count, double), lambda p, k: (p, 0, 0)),
    ]
    if late is not None:
        operands.append(late)
        in_specs.append(pl.BlockSpec(memory_space=pl.ANY))
    aliases = {}
    if held is not None:
        operands += list(held)
        in_specs += [pl.BlockSpec(memory_space=pl.ANY)] * 2
        aliases = {len(operands) - 2: 0, len(operands) - 1: 1}
    return pl.pallas_call(
        expert_grads_kernel,
        grid=(pieces, width // chunk),
        in_specs=in_specs,
        out_specs=[
            pl.BlockSpec((1, chunk, double), lambda p, k: (first + p, k, 0)),
            pl.BlockSpec((1, middle, chunk), lambda p, k: (first + p, 0, k)),
        ],
        out_shape=[
            jax.ShapeDtypeStruct((total, width, double), F32),
            jax.ShapeDtypeStruct((total, middle, width), F32),
        ],
        input_output_aliases=aliases,
        compiler_params=pltpu.CompilerParams(vmem_limit_bytes=60 * 2**20),
        cost_estimate=pl.CostEstimate(
            flops=2 * count * width * pieces * (double + middle),
            bytes_accessed=pieces * width * (double + middle) * 4 + count * width * 8,
            transcendentals=0,
        ),
        name="expert_grads",
    )(*operands)


def grads_kernel(*refs, plan, count):
    inputs, outs = refs[:-count], refs[-count:]
    rows = outs[0].shape[0]
    at = 0
    for width, starts in plan:
        left, right = [], []
        for start in starts:
            pair, inputs = inputs[:4], inputs[4:]
            left += [pair[0][...], pair[1][...]]
            right += [values[:, start : start + width] for values in pair[2:]]
        total = tn(jnp.concatenate(left, axis=0), jnp.concatenate(right, axis=0))
        for k, out in enumerate(outs):
            out[:, at : at + width] = total[k * rows : (k + 1) * rows].astype(BF16)
        at += width


def grads_of(segments, count):
    plan, operands, specs = [], [], []
    rows = segments[0][1][0][0].shape[1]

    def block(values, at, width):
        return pl.BlockSpec((values.shape[0], width), lambda _: (0, at // width))

    flops = 0
    for width, products in segments:
        starts = []
        for left_mine, left_other, right_mine, right_other, at in products:
            operands += [left_mine, left_other, right_mine, right_other]
            whole = at % width > 0
            starts.append(at if whole else 0)
            specs += [block(left_mine, 0, rows)] * 2
            specs += [block(right_mine, 0 if whole else at, right_mine.shape[1] if whole else width)] * 2
            flops += 4 * rows * width * left_mine.shape[0]
        plan.append((width, tuple(starts)))
    total = sum(width for width, _ in segments)
    return pl.pallas_call(
        functools.partial(grads_kernel, plan=tuple(plan), count=count),
        grid=(1,),
        in_specs=specs,
        out_specs=[pl.BlockSpec((rows // count, total), lambda _: (0, 0))] * count,
        out_shape=[jax.ShapeDtypeStruct((rows // count, total), BF16)] * count,
        compiler_params=pltpu.CompilerParams(vmem_limit_bytes=60 * 2**20),
        cost_estimate=pl.CostEstimate(
            flops=flops, bytes_accessed=4 * rows * total, transcendentals=0
        ),
    )(*operands)


def swap_halves(values):
    width = values.shape[1]
    lane = lax.broadcasted_iota(jnp.int32, values.shape, 1)
    return jnp.where(
        lane % ROPE < ROPE // 2,
        pltpu.roll(values, width - ROPE // 2, 1),
        pltpu.roll(values, ROPE // 2, 1),
    )


def repeated(table, times):
    return jnp.concatenate([table] * times, axis=1)


def upper_lanes(shape, head):
    return lax.broadcasted_iota(jnp.int32, shape, 1) // ROPE == head % 2


def lefts_and_rights(block, half, into):
    rows, width = block.shape
    if half % 16 == 0:
        cut = block.reshape(rows // (2 * half), 2 * half, width)
        return [
            cut[:, side * half : (side + 1) * half].reshape(rows // 2, width) for side in range(into)
        ]
    out = []
    for side in range(into):
        shape = (rows // 2, rows)
        row = lax.broadcasted_iota(jnp.int32, shape, 0)
        column = lax.broadcasted_iota(jnp.int32, shape, 1)
        wanted = row // half * (2 * half) + side * half + row % half
        out.append(nn((column == wanted).astype(BF16), block).astype(BF16))
    return out


def assemble(place, refs, targets, sems, size):
    if size is None:
        return [[pltpu.make_async_copy(ref, target, sems.at[i])] for i, (ref, target) in enumerate(zip(refs, targets))]
    core, spots = place[0], (place[1], place[2])
    out = []
    for i, target in enumerate(targets):
        copies = []
        for j in range(2 * size):
            spot = spots[i] ^ (j % size)
            here = core ^ (j // size)
            view = target.at[:, spot, :, here] if i == 0 else target.at[:, :, spot, here]
            at = 2 * size * i + j
            copies.append(pltpu.make_async_copy(refs[at], view, sems.at[at]))
        out.append(copies)
    return out


def flat(target):
    values = target[...]
    return values.reshape(D, values.shape[-1])


def attention_kernel(
    hidden,
    mask,
    cosine,
    sine,
    place,
    *refs,
    half,
    size,
):
    weights, refs = refs[:-16], refs[-16:]
    (
    normed_two,
    mixed_out,
    normed_one_out,
    latent_norm_out,
    latent_in_out,
    latent_scale_out,
    query_out,
    key_value_out,
    rope_key_out,
    probs_out,
    head_out,
    gains_out,
    ups_out,
    first_ref,
    second_ref,
    sems,
    ) = refs
    copies = assemble(place, weights, (first_ref, second_ref), sems, size)
    for copy in copies[0] + copies[1]:
        copy.start()
    hidden_wide = hidden[...].astype(F32)
    norm_one = hidden_wide * inverse_rms(hidden_wide)
    for copy in copies[0]:
        copy.wait()
    first = flat(first_ref)
    tail = first[:, first.shape[1] - 128 :]
    picked = lax.broadcasted_iota(jnp.int32, (16, 128), 1) == ROPE + lax.broadcasted_iota(
        jnp.int32, (16, 128), 0
    )
    picked = picked.astype(BF16)
    gains = nt(picked, tail)
    latent_gains = nt(picked, lefts_and_rights(tail, half, 1)[0])
    gains_out[...] = jnp.concatenate(
        [gains[:2], jnp.concatenate([latent_gains[2:3], jnp.zeros((1, D - RANK), F32)], axis=1),
         jnp.zeros((5, D), F32)], axis=0
    )
    normed_one = (norm_one * gains[0:1]).astype(BF16)
    normed_one_out[...] = normed_one
    projected = nn(normed_one, first)
    nope_width = H * NOPE
    query_width = H * (NOPE + ROPE)
    latent_part = projected[:, query_width : query_width + RANK]
    latent_scale = inverse_rms(latent_part)
    latent_norm = latent_part * latent_scale
    latent_in = (latent_norm * latent_gains[2:3]).astype(BF16)
    latent_norm_out[...] = latent_norm
    latent_in_out[...] = latent_in
    latent_scale_out[...] = jnp.broadcast_to(latent_scale, latent_scale_out.shape)
    cos, sin = cosine[...], sine[...]
    rope = projected[:, nope_width:query_width]
    rope = rope * repeated(cos, H // 2) + swap_halves(rope) * repeated(sin, H // 2)
    query_out[:, :nope_width] = projected[:, :nope_width].astype(BF16)
    query_out[:, nope_width:] = rope.astype(BF16)
    key = projected[:, query_width + RANK : query_width + RANK + 128]
    key = jnp.where(upper_lanes(key.shape, 0), key, 0.0)
    key = key + pltpu.roll(key, ROPE, 1)
    rope_key = (key * cos + swap_halves(key) * sin).astype(BF16)
    rope_key_out[...] = rope_key
    for copy in copies[1]:
        copy.wait()
    second = flat(second_ref)
    for side, part in enumerate(lefts_and_rights(second[:, H * VDIM :], half, 2)):
        ups_out[side] = part
        key_value_out[:, side * UW : (side + 1) * UW] = nn(latent_in, part).astype(BF16)
    scaling = (NOPE + ROPE) ** (-0.5)
    allowed = mask[...]
    for head in range(H):
        pair = query_out[:, nope_width + head // 2 * 128 : nope_width + head // 2 * 128 + 128]
        pair = jnp.where(upper_lanes(pair.shape, head), pair, jnp.zeros_like(pair))
        query = jnp.concatenate([query_out[:, head * NOPE : (head + 1) * NOPE], pair], axis=1)
        at = head * (NOPE + VDIM)
        keys = jnp.concatenate([key_value_out[:, at : at + NOPE], rope_key], axis=1)
        scores = nt(query, keys) * scaling
        raised = jnp.exp(scores) * allowed
        probs = raised / jnp.sum(raised, axis=-1, keepdims=True)
        probs_out[head] = probs
        head_out[:, head * VDIM : (head + 1) * VDIM] = nn(
            probs.astype(BF16), key_value_out[:, at + NOPE : at + NOPE + VDIM]
        ).astype(BF16)
    mixed = hidden_wide + nt(head_out[...], second[:, : H * VDIM])
    mixed_out[...] = mixed
    normed_two[...] = (mixed * inverse_rms(mixed) * gains[1:2]).astype(BF16)


def weight_scratch(weights, size):
    if size is None:
        return [pltpu.VMEM(values.shape, BF16) for values in weights] + [
            pltpu.SemaphoreType.DMA((len(weights),))
        ]
    out = []
    for i in range(2):
        part = weights[2 * size * i].shape
        shape = (part[0], size, part[1], 2) if i == 0 else (part[0], part[1], size, 2)
        out.append(pltpu.VMEM(shape + part[2:], BF16))
    return out + [pltpu.SemaphoreType.DMA((len(weights),))]


def attention(hidden, mask, cosine, sine, place, weights, half, size):
    rows, width = hidden.shape
    query_width = H * (NOPE + ROPE)
    first_width = query_width + RANK + 128
    vmem = pl.BlockSpec(memory_space=pltpu.VMEM)
    smem = pl.BlockSpec(memory_space=pltpu.SMEM)
    shapes = [
        ((rows, width), BF16),
        ((rows, width), F32),
        ((rows, width), BF16),
        ((rows, RANK), F32),
        ((rows, RANK), BF16),
        ((rows, 128), F32),
        ((rows, query_width), BF16),
        ((rows, 2 * UW), BF16),
        ((rows, 128), BF16),
        ((H, rows, rows), F32),
        ((rows, H * VDIM), BF16),
        ((8, width), F32),
        ((2, RANK, UW), BF16),
    ]
    return pl.pallas_call(
        functools.partial(attention_kernel, half=half, size=size),
        in_specs=[vmem] * 4 + [smem] + [pl.BlockSpec(memory_space=pl.ANY)] * len(weights),
        out_specs=[vmem] * len(shapes),
        out_shape=[jax.ShapeDtypeStruct(shape, dtype) for shape, dtype in shapes],
        scratch_shapes=weight_scratch(weights, size),
        compiler_params=pltpu.CompilerParams(vmem_limit_bytes=60 * 2**20),
        cost_estimate=pl.CostEstimate(
            flops=2 * rows * width * (first_width + 3 * width),
            bytes_accessed=2 * width * (first_width + 2 * width) + 8 * rows * width,
            transcendentals=H * rows * rows,
        ),
        name="attention",
    )(hidden, mask, cosine, sine, place, *weights)


def shared_kernel(normed, cotangent, place, *refs, size):
    weights, refs = refs[:-7], refs[-7:]
    dpre, act, shared_y, shared_dx, in_ref, out_ref, sems = refs
    copies = assemble(place, weights, (in_ref, out_ref), sems, size)
    for copy in copies[0] + copies[1]:
        copy.start()
    for copy in copies[0]:
        copy.wait()
    weight_in = flat(in_ref)
    pre_act = nn(normed[...], weight_in)
    for copy in copies[1]:
        copy.wait()
    weight_out = flat(out_ref)
    act[...] = swiglu_forward(pre_act)
    dpre[...] = swiglu_backward(pre_act, nn(cotangent[...], weight_out))
    shared_y[...] = nt(act[...], weight_out)
    shared_dx[...] = nt(dpre[...], weight_in)


def shared_expert(normed, cotangent, place, weights, size, middle):
    rows, width = normed.shape
    vmem = pl.BlockSpec(memory_space=pltpu.VMEM)
    return pl.pallas_call(
        functools.partial(shared_kernel, size=size),
        in_specs=[vmem] * 2
        + [pl.BlockSpec(memory_space=pltpu.SMEM)]
        + [pl.BlockSpec(memory_space=pl.ANY)] * len(weights),
        out_specs=[vmem] * 4,
        out_shape=[
            jax.ShapeDtypeStruct((rows, 2 * middle), BF16),
            jax.ShapeDtypeStruct((rows, middle), BF16),
            jax.ShapeDtypeStruct((rows, width), F32),
            jax.ShapeDtypeStruct((rows, width), F32),
        ],
        scratch_shapes=weight_scratch(weights, size),
        compiler_params=pltpu.CompilerParams(vmem_limit_bytes=60 * 2**20),
        cost_estimate=pl.CostEstimate(
            flops=12 * rows * width * middle,
            bytes_accessed=6 * width * middle,
            transcendentals=rows * middle,
        ),
        name="shared_expert",
    )(normed, cotangent, place, *weights)


def combined_kernel(mixed, shared_y, gates_high, gates_low, rows, out):
    routed = tn(gates_high[...], rows[...]) + tn(gates_low[...], rows[...])
    out[...] = (mixed[...] + shared_y[...] + routed).astype(BF16)


def combined(mixed, shared_y, gates_high, gates_low, rows):
    vmem = pl.BlockSpec(memory_space=pltpu.VMEM)
    return pl.pallas_call(
        combined_kernel,
        in_specs=[vmem] * 5,
        out_specs=vmem,
        out_shape=jax.ShapeDtypeStruct(mixed.shape, BF16),
        compiler_params=pltpu.CompilerParams(vmem_limit_bytes=60 * 2**20),
        cost_estimate=pl.CostEstimate(
            flops=4 * rows.size * mixed.shape[0], bytes_accessed=2 * rows.size, transcendentals=0
        ),
        name="combined",
    )(mixed, shared_y, gates_high, gates_low, rows)


def mixed_back_kernel(*refs):
    count = (len(refs) - 7) // 2
    shared_dx, out_grad, mixed, gains = refs[:4]
    selectors, back = refs[4 : 4 + count], refs[4 + count : 4 + 2 * count]
    grad_mixed_out, mixed_low, gain_out = refs[4 + 2 * count :]
    grad = shared_dx[...]
    for selector, rows in zip(selectors, back):
        grad = grad + tn(selector[...], rows[...])
    scale = inverse_rms(mixed[...])
    norm_two = mixed[...] * scale
    gain_out[...] = jnp.broadcast_to(jnp.sum(grad * norm_two, axis=0, keepdims=True), gain_out.shape)
    grad_norm = grad * gains[1:2]
    grad_mixed = out_grad[...].astype(F32) + scale * (
        grad_norm - norm_two * jnp.mean(grad_norm * norm_two, axis=-1, keepdims=True)
    )
    grad_mixed_out[...] = grad_mixed
    mixed_low[...] = grad_mixed.astype(BF16)


def mixed_back(shared_dx, out_grad, mixed, gains, selectors, back):
    rows, width = mixed.shape
    vmem = pl.BlockSpec(memory_space=pltpu.VMEM)
    total = sum(values.shape[0] for values in back)
    return pl.pallas_call(
        mixed_back_kernel,
        in_specs=[vmem] * (4 + 2 * len(back)),
        out_specs=[vmem] * 3,
        out_shape=[
            jax.ShapeDtypeStruct((rows, width), F32),
            jax.ShapeDtypeStruct((rows, width), BF16),
            jax.ShapeDtypeStruct((8, width), F32),
        ],
        compiler_params=pltpu.CompilerParams(vmem_limit_bytes=60 * 2**20),
        cost_estimate=pl.CostEstimate(
            flops=2 * rows * width * total, bytes_accessed=2 * total * width, transcendentals=0
        ),
        name="mixed_back",
    )(shared_dx, out_grad, mixed, gains, *selectors, *back)


def attention_back_kernel(
    hidden,
    grad_mixed,
    mixed_low,
    cosine,
    sine,
    latent_norm,
    latent_scale,
    query,
    key_value,
    rope_key,
    probs,
    head_out,
    gains,
    ups,
    place,
    *refs,
    size,
):
    weights, refs = refs[:-6], refs[-6:]
    back, input_grad, gain_out, first_ref, second_ref, sems = refs
    copies = assemble(place, weights, (first_ref, second_ref), sems, size)
    for copy in copies[1] + copies[0]:
        copy.start()
    grad_projected = back.at[:, 2 * UW :]
    grad_key_value = back.at[:, : 2 * UW]
    for copy in copies[1]:
        copy.wait()
    output = flat(second_ref)[:, : H * VDIM]
    rows = hidden.shape[0]
    nope_width = H * NOPE
    query_width = H * (NOPE + ROPE)
    scaling = (NOPE + ROPE) ** (-0.5)
    heads = nn(mixed_low[...], output).astype(BF16)
    rope_sum = jnp.zeros((rows, 128), F32)
    rope_grads = []
    for head in range(H):
        grad_head = heads[:, head * VDIM : (head + 1) * VDIM]
        at = head * (NOPE + VDIM)
        weights_here = probs[head]
        own_lanes = upper_lanes((rows, 128), head)
        pair = query[:, nope_width + head // 2 * 128 : nope_width + head // 2 * 128 + 128]
        pair = jnp.where(own_lanes, pair, jnp.zeros_like(pair))
        query_here = jnp.concatenate([query[:, head * NOPE : (head + 1) * NOPE], pair], axis=1)
        keys = jnp.concatenate([key_value[:, at : at + NOPE], rope_key[...]], axis=1)
        grad_probs = nt(grad_head, key_value[:, at + NOPE : at + NOPE + VDIM])
        delta = jnp.sum(
            grad_head.astype(F32) * head_out[:, head * VDIM : (head + 1) * VDIM].astype(F32),
            axis=-1,
            keepdims=True,
        )
        grad_scores = (weights_here * (grad_probs - delta) * scaling).astype(BF16)
        grad_query = nn(grad_scores, keys)
        grad_projected[:, head * NOPE : (head + 1) * NOPE] = grad_query[:, :NOPE].astype(BF16)
        rope_grads.append(jnp.where(own_lanes, grad_query[:, NOPE:], 0.0))
        grad_keys = tn(grad_scores, query_here)
        rope_sum = rope_sum + grad_keys[:, NOPE:]
        grad_key_value[:, at : at + NOPE] = grad_keys[:, :NOPE].astype(BF16)
        grad_key_value[:, at + NOPE : at + NOPE + VDIM] = tn(
            weights_here.astype(BF16), grad_head
        ).astype(BF16)
    cos, sin = cosine[...], sine[...]
    rope = jnp.concatenate(
        [rope_grads[2 * pair] + rope_grads[2 * pair + 1] for pair in range(H // 2)], axis=1
    )
    rope = rope * repeated(cos, H // 2) - swap_halves(rope) * repeated(sin, H // 2)
    grad_projected[:, nope_width:query_width] = rope.astype(BF16)
    key = rope_sum + pltpu.roll(rope_sum, ROPE, 1)
    key = key * cos - swap_halves(key) * sin
    key = jnp.where(upper_lanes(key.shape, 0), key, 0.0)
    grad_projected[:, query_width + RANK :] = key.astype(BF16)
    grad_latent_in = nt(grad_key_value[:, :UW], ups[0]) + nt(grad_key_value[:, UW:], ups[1])
    norm = latent_norm[...]
    latent_gain_grad = jnp.sum(grad_latent_in * norm, axis=0, keepdims=True)
    grad_norm = grad_latent_in * gains[2:3, :RANK]
    grad_latent = latent_scale[:, 0:1] * (
        grad_norm - norm * jnp.mean(grad_norm * norm, axis=-1, keepdims=True)
    )
    grad_projected[:, query_width : query_width + RANK] = grad_latent.astype(BF16)
    for copy in copies[0]:
        copy.wait()
    grad_normed = nt(grad_projected[...], flat(first_ref))
    hidden_wide = hidden[...].astype(F32)
    scale = inverse_rms(hidden_wide)
    norm_one = hidden_wide * scale
    gain_out[...] = jnp.concatenate(
        [
            jnp.sum(grad_normed * norm_one, axis=0, keepdims=True),
            jnp.concatenate([latent_gain_grad, jnp.zeros((1, D - RANK), F32)], axis=1),
            jnp.zeros((6, D), F32),
        ],
        axis=0,
    )
    grad_norm = grad_normed * gains[0:1]
    input_grad[...] = grad_mixed[...] + scale * (
        grad_norm - norm_one * jnp.mean(grad_norm * norm_one, axis=-1, keepdims=True)
    )


def attention_back(operands, place, weights, size):
    hidden = operands[0]
    rows, width = hidden.shape
    first_width = H * (NOPE + ROPE) + RANK + 128
    vmem = pl.BlockSpec(memory_space=pltpu.VMEM)
    return pl.pallas_call(
        functools.partial(attention_back_kernel, size=size),
        in_specs=[vmem] * len(operands)
        + [pl.BlockSpec(memory_space=pltpu.SMEM)]
        + [pl.BlockSpec(memory_space=pl.ANY)] * len(weights),
        out_specs=[vmem] * 3,
        out_shape=[
            jax.ShapeDtypeStruct((rows, first_width + 2 * UW), BF16),
            jax.ShapeDtypeStruct((rows, width), F32),
            jax.ShapeDtypeStruct((8, width), F32),
        ],
        scratch_shapes=weight_scratch(weights, size),
        compiler_params=pltpu.CompilerParams(vmem_limit_bytes=60 * 2**20),
        cost_estimate=pl.CostEstimate(
            flops=2 * rows * width * (first_width + 3 * width),
            bytes_accessed=2 * width * (first_width + 2 * width) + 8 * rows * width,
            transcendentals=0,
        ),
        name="attention_back",
    )(*operands, place, *weights)


def after_kernel(values, late, out):
    pass


def after(values, late):
    anywhere = pl.BlockSpec(memory_space=pl.ANY)
    return pl.pallas_call(
        after_kernel,
        in_specs=[anywhere, anywhere],
        out_specs=anywhere,
        out_shape=jax.ShapeDtypeStruct(values.shape, values.dtype),
        input_output_aliases={0: 0},
        cost_estimate=pl.CostEstimate(flops=0, bytes_accessed=0, transcendentals=0),
        name="after",
    )(values, late)


def axes_of(devices):
    return {32: ((8, 4), (4, 2), (2, 2)), 128: ((32, 4), (8, 4), (2, 4))}[devices]


def swap_with(values, devices, offset):
    return lax.ppermute(values, "fsdp", [(i, i ^ offset) for i in range(devices)])


def pick(values, index, axis):
    return lax.dynamic_index_in_dim(values, index, axis, keepdims=False)


def row_order(devices, axis, half=None):
    me = lax.axis_index("fsdp")
    own = D // devices
    axes = axes_of(devices)
    to = jnp.arange(D, dtype=jnp.int32)
    chip_row = to % (D // 2)
    stride, size = axes[axis]
    block = chip_row // (D // 2 // size)
    rest = chip_row % (D // 2 // size) // own
    device = (me % 2) ^ (to // (D // 2))
    device = device + (((me // stride) % size) ^ block) * stride
    for other in (2, 1, 0):
        if other != axis:
            device = device + rest % axes[other][1] * axes[other][0]
            rest = rest // axes[other][1]
    row = to % own
    if half is None:
        source = device * own + row
        return (jnp.arange(D, dtype=jnp.int32)[:, None] == source[None, :]).astype(BF16)
    source = device * half + row % half
    hit = jnp.arange(D // 2, dtype=jnp.int32)[:, None] == source[None, :]
    return [(hit & (row // half == side)[None, :]).astype(BF16) for side in range(2)]


def scatter_sum(blocks, devices, order, late=()):
    me = lax.axis_index("fsdp")
    axes = axes_of(devices)
    left = [0, 1, 2]
    values = None
    for axis in order:
        stride, size = axes[axis]
        at = left.index(axis)
        left.remove(axis)
        mine = (me // stride) % size
        if values is not None:
            blocks = [pick(values, mine ^ k, at) for k in range(size)]
        total = blocks[0]
        if late:
            for values in late[0]:
                total = after(total, values)
            late = late[1:]
        total = total.astype(F32)
        parts = [swap_with(blocks[k], devices, k * stride) for k in range(1, size)]
        for part in parts:
            total = total + part.astype(F32)
        values = total if not left else total.astype(BF16)
        if values.ndim == 2 and left:
            values = values.reshape(
                *(axes[other][1] for other in left), D // devices, values.shape[-1]
            )
    return values


def gather_start(shard, devices, order):
    me = lax.axis_index("fsdp")
    axes = axes_of(devices)
    have = []
    values = shard
    for axis in order:
        stride, size = axes[axis]
        mine = (me // stride) % size
        at = sum(other < axis for other in have)
        have.append(axis)
        parts = [values] + [swap_with(values, devices, k * stride) for k in range(1, size)]
        if len(have) < 3:
            values = placed_along(parts, mine, at)
    return (parts, mine, at)


def placed_along(parts, mine, at):
    if len(parts) == 2:
        return jnp.where(mine == 0, jnp.stack(parts, at), jnp.stack(parts[::-1], at))
    shape = parts[0].shape
    values = jnp.zeros(shape[:at] + (len(parts),) + shape[at:], parts[0].dtype)
    for k, part in enumerate(parts):
        values = lax.dynamic_update_index_in_dim(values, part, mine ^ k, at)
    return values


def gather_finish(started, devices):
    parts, mine, at = started
    values = placed_along(parts, mine, at)
    other = swap_with(values, devices, 1)
    first = lax.axis_index("fsdp") % 2 == 0
    pair = jnp.where(first, jnp.stack([values, other], 3), jnp.stack([other, values], 3))
    return pair.reshape(-1, values.shape[-1])


def body(
    hidden_in,
    out_grad,
    doc_ids,
    routes,
    gate_values,
    attn_gain,
    query_proj,
    latent_proj,
    latent_gain,
    latent_up,
    output_proj,
    ffn_gain,
    shared_in,
    shared_out,
    expert_in,
    expert_out,
):
    devices = lax.axis_size("fsdp")
    rows_here = hidden_in.shape[0]
    own = D // devices
    half = own // 2
    me = lax.axis_index("fsdp")

    along_x, along_y = row_order(devices, 2), row_order(devices, 1)
    sides_x, sides_y = row_order(devices, 2, half), row_order(devices, 1, half)

    def mine_and_other(columns, order):
        placed = matmul(columns, order).astype(BF16)
        return (placed[:, : D // 2], swap_with(placed[:, D // 2 :], devices, 1))

    spare = 128 - LW % 128
    query_width, output_width = query_proj.shape[1], output_proj.shape[1]
    gain_at = query_width + LW
    output_at = gain_at + spare
    by_head = query_proj.reshape(own, H, NOPE + ROPE)
    started = [
        gather_start(
            jnp.concatenate(
                [
                    by_head[:, :, :NOPE].reshape(own, H * NOPE),
                    by_head[:, :, NOPE:].reshape(own, H * ROPE),
                    latent_proj,
                    attn_gain[:, None],
                    ffn_gain[:, None],
                    jnp.concatenate([latent_gain, jnp.zeros_like(latent_gain)])[:, None],
                    jnp.zeros((own, spare - 3), BF16),
                ],
                axis=1,
            ),
            devices,
            (0, 2, 1),
        ),
        gather_start(
            jnp.concatenate(
                [output_proj, jnp.concatenate([latent_up[:, :UW], latent_up[:, UW:]], axis=0)],
                axis=1,
            ),
            devices,
            (0, 1, 2),
        ),
    ]
    place = jnp.stack([me % 2, started[0][1], started[1][1]]).astype(jnp.int32)
    size = len(started[0][0]) if own % 16 == 0 else None

    def gathered_parts(started):
        out = []
        for begun in started:
            if size is None:
                out.append(gather_finish(begun, devices))
            else:
                out += begun[0] + [swap_with(part, devices, 1) for part in begun[0]]
        return out

    attention_weights = gathered_parts(started)

    per_device = expert_in.shape[0]
    pieces = 2 if per_device % 2 == 0 else 1
    units = 2 * EXPERTS // pieces
    local_units = units // devices
    token = jnp.arange(rows_here, dtype=jnp.int32)
    earlier = (token[None, :] < token[:, None]).astype(BF16)

    def routing(names, values, base, count):
        unit_expert = (base + jnp.arange(count, dtype=jnp.int32)) // (2 // pieces)
        named = names[:, :, None] == unit_expert[None, None, :]
        hits = jnp.any(named, axis=1)
        gates = jnp.sum(jnp.where(named, values[:, :, None], 0.0), axis=1)
        slots = matmul(earlier, hits.astype(BF16)).astype(jnp.int32)
        return (jnp.where(hits, slots, CAP).T, gates.T)

    slots, gates = routing(routes, gate_values, 0, units)
    chosen = slots[:, None, :] == jnp.arange(CAP, dtype=jnp.int32)[None, :, None]
    gate_wide = jnp.where(chosen, gates[:, None, :], 0.0).reshape(units * CAP, rows_here)
    gate_rows = jnp.sum(gate_wide, axis=-1, keepdims=True)
    selector = chosen.astype(BF16)
    unit_selector = selector.reshape(devices, local_units, CAP, rows_here)
    unit_selector = [
        unit_selector[:, u].reshape(devices * CAP, rows_here) for u in range(local_units)
    ]
    selector = selector.reshape(units * CAP, rows_here)

    def exchange(rows):
        return lax.all_to_all(rows, "fsdp", split_axis=0, concat_axis=0, tiled=True)

    def exchange_unit(rows):
        return exchange(rows.reshape(devices, CAP, D)).reshape(devices * CAP, D)

    grads_out = (gate_rows * matmul(selector, out_grad)).astype(BF16)
    grad_rows = exchange(grads_out.reshape(devices, local_units * CAP, D))
    grad_rows = grad_rows.reshape(devices, local_units, CAP, D)
    grad_rows = [grad_rows[:, u].reshape(devices * CAP, D) for u in range(local_units)]

    allowed, cosine_table, sine_table = tables(doc_ids[0])
    cosine_lanes = jnp.concatenate([cosine_table] * 4, axis=1)
    sine_lanes = jnp.concatenate([-sine_table, sine_table] * 2, axis=1)
    (
        normed_two,
        mixed,
        normed_one,
        latent_norm,
        latent_in,
        latent_scale,
        queries,
        key_values,
        rope_key,
        probs,
        head_out,
        gain_rows,
        ups,
    ) = attention(hidden_in, allowed.astype(F32), cosine_lanes, sine_lanes, place, attention_weights, half, size)

    rows_out = [matmul(unit_selector[u], normed_two).astype(BF16) for u in range(local_units)]
    rows_in = []
    for rows in rows_out:
        rows_in.append(exchange_unit(rows))

    shared_rows = after(normed_two, rows_out[0])
    started = [
        gather_start(shared_in, devices, (0, 2, 1)), gather_start(shared_out, devices, (0, 1, 2))
    ]
    shared_weights = gathered_parts(started)
    middle = shared_out.shape[1]
    grad_shared_pre, shared_act, shared_y, shared_dx = shared_expert(
        shared_rows, out_grad, place, shared_weights, size, middle
    )
    middle = shared_out.shape[1]
    dpre_pair = (grad_shared_pre, swap_with(grad_shared_pre, devices, 1))
    act_pair = (shared_act, swap_with(shared_act, devices, 1))
    size_x, size_y = axes_of(devices)[2][1], axes_of(devices)[1][1]
    normed_left = [mine_and_other(normed_two, along) for along in (along_x, along_y)]
    cotangent_left = mine_and_other(out_grad, along_x)
    blocks_x = grads_of(
        (
            (middle, ((*normed_left[0], *dpre_pair, 0),)),
            (middle, ((*cotangent_left, *act_pair, 0),)),
        ),
        size_x,
    )
    blocks_y = grads_of(((middle, ((*normed_left[1], *dpre_pair, middle),)),), size_y)
    shared_blocks = (blocks_x, blocks_y)

    back_dx, back_out, saved = [], [], []
    for u in range(local_units):
        dx_rows, y_rows, activation, grad_pre = experts(
            rows_in[u], grad_rows[u], expert_in, expert_out, u, pieces
        )
        back_dx.append(exchange_unit(dx_rows))
        back_out.append(y_rows.reshape(devices, CAP, D))
        saved.append((activation, grad_pre))
    back_out = jnp.concatenate(back_out, axis=1)
    for rows in back_dx:
        back_out = after(back_out, rows)
    back_out = exchange(back_out).reshape(units * CAP, D)

    grad_mixed, mixed_low, ffn_gain_grad = mixed_back(
        shared_dx, out_grad, mixed, gain_rows, unit_selector, back_dx
    )

    heads_pair = (head_out, swap_with(head_out, devices, 1))
    first_left = mine_and_other(normed_one, along_y)
    up_left = [mine_and_other(latent_in, side) for side in sides_x]
    output_left = mine_and_other(mixed_low, along_x)
    back, input_grad, other_gain_grads = attention_back(
        (
            hidden_in,
            grad_mixed,
            mixed_low,
            cosine_lanes,
            sine_lanes,
            latent_norm,
            latent_scale,
            queries,
            key_values,
            rope_key,
            probs,
            head_out,
            gain_rows,
            ups,
        ),
        place,
        attention_weights,
        size,
    )
    back_pair = (back, swap_with(back, devices, 1))
    gain_grads = jnp.concatenate(
        [other_gain_grads[:1], ffn_gain_grad[:1], jnp.zeros((6, D), F32)], axis=0
    ).astype(BF16)
    placed = matmul(gain_grads, along_y) + jnp.pad(
        matmul(other_gain_grads[1:7, :RANK].astype(BF16), sides_y[0]), ((2, 0), (0, 0))
    )
    placed = placed.astype(BF16)
    gain_left = (placed[:, : D // 2], swap_with(placed[:, D // 2 :], devices, 1))
    row = jnp.arange(8, dtype=jnp.int32)[:, None]
    lane = jnp.arange(output_at, dtype=jnp.int32)[None, :]
    gain_right = ((row < 3) & (lane == gain_at + row)).astype(BF16)
    blocks_y = grads_of(
        (
            (
                output_at,
                ((*first_left, *back_pair, 2 * UW), (*gain_left, gain_right, gain_right, 0)),
            ),
        ),
        size_y,
    )
    owned_first = scatter_sum(blocks_y, devices, (1, 2, 0))
    blocks_x = grads_of(
        (
            (output_width, ((*output_left, *heads_pair, 0),)),
            (UW, tuple((*up_left[i], *back_pair, i * UW) for i in range(2))),
        ),
        size_x,
    )
    gates_high = lax.reduce_precision(gate_wide, 8, 7)
    gates_low = (gate_wide - gates_high).astype(BF16)
    layer_out = combined(mixed, shared_y, gates_high.astype(BF16), gates_low, back_out)
    owned_second = scatter_sum(blocks_x, devices, (2, 1, 0))
    shared_late = ((blocks_x[0], blocks_y[0]),)
    owned_gate_out = scatter_sum(shared_blocks[0], devices, (2, 1, 0), shared_late)
    owned_up_in = scatter_sum(shared_blocks[1], devices, (1, 2, 0), shared_late)
    owned_output, owned_up = owned_second[:, :output_width], owned_second[:, output_width:]
    held = None
    for u in range(local_units):
        held = expert_grads(
            rows_in[u], grad_rows[u], *saved[u], per_device, u, blocks_x[-1] if u else None, held
        )
    owned_query = jnp.concatenate(
        [
            owned_first[:, : H * NOPE].reshape(own, H, NOPE),
            owned_first[:, H * NOPE : query_width].reshape(own, H, ROPE),
        ],
        axis=2,
    ).reshape(own, query_width)
    return (
        layer_out,
        input_grad,
        owned_first[:, gain_at],
        owned_query,
        owned_first[:, query_width:gain_at],
        owned_first[:half, gain_at + 2],
        jnp.concatenate([owned_up[:half], owned_up[half:]], axis=1),
        owned_output,
        owned_first[:, gain_at + 1],
        jnp.concatenate([owned_gate_out[:, :middle], owned_up_in], axis=1),
        owned_gate_out[:, middle:],
        held[0],
        held[1],
    )


def solution(mesh):
    rows = P("fsdp", None)
    flat = P("fsdp")
    cube = P("fsdp", None, None)
    in_specs = (rows,) * 5 + (flat, rows, rows, flat, rows, rows, flat, rows, rows, cube, cube)
    out_specs = (rows, rows, flat, rows, rows, flat, rows, rows, flat, rows, rows, cube, cube)
    return jax.shard_map(body, mesh=mesh, in_specs=in_specs, out_specs=out_specs, check_vma=False)
```

```python
import functools
import math

import jax
import jax.numpy as jnp
from jax import lax
from jax.experimental import pallas as pl
from jax.experimental.pallas import tpu as pltpu
from jax.sharding import PartitionSpec as P


D = 1024
H = 8
NOPE = 128
ROPE = 64
VDIM = 128
RANK = 512
EXPERTS = 64
CAP = 16
UW = H * (NOPE + VDIM) // 2
LW = RANK + ROPE

EPSILON = 1e-06
F32 = jnp.float32
BF16 = jnp.bfloat16


def matmul(left_side, right_side):
    return jnp.dot(left_side, right_side, preferred_element_type=F32)


def inverse_rms(values):
    return lax.rsqrt(jnp.mean(values * values, axis=-1, keepdims=True) + EPSILON)


def swiglu_parts(pre_act):
    middle = pre_act.shape[-1] // 2
    gate_pre = pre_act[..., :middle]
    up_pre = pre_act[..., middle:]
    return (gate_pre, up_pre, jax.nn.sigmoid(gate_pre))


def swiglu_forward(pre_act):
    gate_pre, up_pre, sigmoid_gate = swiglu_parts(pre_act)
    return (gate_pre * sigmoid_gate * up_pre).astype(BF16)


def swiglu_backward(pre_act, grad_act):
    gate_pre, up_pre, sigmoid_gate = swiglu_parts(pre_act)
    silu_value = gate_pre * sigmoid_gate
    slope = sigmoid_gate * (1.0 + gate_pre * (1.0 - sigmoid_gate))
    return jnp.concatenate([grad_act * up_pre * slope, grad_act * silu_value], axis=-1).astype(BF16)


def tables(documents):
    rows_here = documents.shape[0]
    indices = jnp.arange(rows_here, dtype=jnp.int32)
    same_doc = documents[:, None] == documents[None, :]
    starts = jnp.min(jnp.where(same_doc, indices[None, :], rows_here), axis=1)
    allowed = same_doc & (indices[None, :] <= indices[:, None])
    position = (indices - starts).astype(F32)
    frequency = jnp.exp(jnp.arange(ROPE // 2, dtype=F32) * (-2.0 * math.log(10000.0) / ROPE))
    angles = position[:, None] * frequency[None, :]
    return (allowed, jnp.cos(angles), jnp.sin(angles))


def nn(left_side, right_side):
    return lax.dot_general(
        left_side, right_side, (((1,), (0,)), ((), ())), preferred_element_type=F32
    )


def nt(left_side, right_side):
    return lax.dot_general(
        left_side, right_side, (((1,), (1,)), ((), ())), preferred_element_type=F32
    )


def tn(left_side, right_side):
    return lax.dot_general(
        left_side, right_side, (((0,), (0,)), ((), ())), preferred_element_type=F32
    )


def experts_kernel(rows, grads, w_in, w_out, dx, y, act, dpre, dx_sum, y_sum):
    piece = pl.program_id(0)
    block = rows.shape[0]
    here = pl.ds(pl.program_id(1) * block, block)
    middle = w_out.shape[1]
    pre_act = nn(rows[...], w_in[0])
    gate_pre = pre_act[:, :middle]
    up_pre = pre_act[:, middle:]
    sigmoid_gate = jax.nn.sigmoid(gate_pre)
    silu_value = gate_pre * sigmoid_gate
    act_low = (silu_value * up_pre).astype(BF16)
    act[0] = act_low
    grad_act = nt(grads[...].reshape(rows.shape), w_out[0])
    slope = sigmoid_gate * (1.0 + gate_pre * (1.0 - sigmoid_gate))
    dpre_low = jnp.concatenate([grad_act * up_pre * slope, grad_act * silu_value], axis=1).astype(BF16)
    dpre[0] = dpre_low
    dx_part = nt(dpre_low, w_in[0])
    y_part = nn(act_low, w_out[0])

    @pl.when(piece == 0)
    def _():
        dx_sum[here] = dx_part
        y_sum[here] = y_part

    @pl.when(piece > 0)
    def _():
        dx_sum[here] += dx_part
        y_sum[here] += y_part

    @pl.when(piece == pl.num_programs(0) - 1)
    def _():
        dx[...] = dx_sum[here].astype(BF16)
        y[...] = y_sum[here].astype(BF16)


def experts(rows, grads, w_in, w_out, unit, pieces):
    count, width = rows.shape
    first = unit * pieces
    double, middle = w_in.shape[2], w_out.shape[1]
    block = min(256, count)
    row_spec = pl.BlockSpec((block, width), lambda p, r: (r, 0))
    last_spec = pl.BlockSpec((block, width), lambda p, r: (jnp.where(p == pieces - 1, r, 0), 0))
    return pl.pallas_call(
        experts_kernel,
        grid=(pieces, count // block),
        in_specs=[
            row_spec,
            pl.BlockSpec((block // CAP, 1, CAP, width), lambda p, r: (r, unit, 0, 0)),
            pl.BlockSpec((1, width, double), lambda p, r: (first + p, 0, 0)),
            pl.BlockSpec((1, middle, width), lambda p, r: (first + p, 0, 0)),
        ],
        out_specs=[
            last_spec,
            last_spec,
            pl.BlockSpec((1, block, middle), lambda p, r: (p, r, 0)),
            pl.BlockSpec((1, block, double), lambda p, r: (p, r, 0)),
        ],
        out_shape=[
            jax.ShapeDtypeStruct((count, width), BF16),
            jax.ShapeDtypeStruct((count, width), BF16),
            jax.ShapeDtypeStruct((pieces, count, middle), BF16),
            jax.ShapeDtypeStruct((pieces, count, double), BF16),
        ],
        scratch_shapes=[pltpu.VMEM((count, width), F32), pltpu.VMEM((count, width), F32)],
        compiler_params=pltpu.CompilerParams(vmem_limit_bytes=60 * 2**20),
        cost_estimate=pl.CostEstimate(
            flops=2 * count * width * pieces * (2 * double + 2 * middle),
            bytes_accessed=pieces * (width + count) * (double + middle) * 2 + count * width * 8,
            transcendentals=count * middle * pieces,
        ),
        name="experts",
    )(rows, grads, w_in, w_out)


def expert_grads_kernel(rows, grads, act, dpre, *refs):
    grad_in, grad_out = refs[-2:]
    grad_in[0] = tn(rows[...], dpre[0])
    grad_out[0] = tn(act[0], grads[...].reshape(rows.shape))


def expert_grads(rows, grads, act, dpre, total, unit, late, held=None, chunk=256):
    count, width = rows.shape
    pieces, _, middle = act.shape
    first = unit * pieces
    double = dpre.shape[2]
    row_spec = pl.BlockSpec((count, chunk), lambda p, k: (0, k))
    operands = [rows, grads, act, dpre]
    in_specs = [
        row_spec,
        pl.BlockSpec((count // CAP, 1, CAP, chunk), lambda p, k: (0, unit, 0, k)),
        pl.BlockSpec((1, count, middle), lambda p, k: (p, 0, 0)),
        pl.BlockSpec((1, count, double), lambda p, k: (p, 0, 0)),
    ]
    if late is not None:
        operands.append(late)
        in_specs.append(pl.BlockSpec(memory_space=pl.ANY))
    aliases = {}
    if held is not None:
        operands += list(held)
        in_specs += [pl.BlockSpec(memory_space=pl.ANY)] * 2
        aliases = {len(operands) - 2: 0, len(operands) - 1: 1}
    return pl.pallas_call(
        expert_grads_kernel,
        grid=(pieces, width // chunk),
        in_specs=in_specs,
        out_specs=[
            pl.BlockSpec((1, chunk, double), lambda p, k: (first + p, k, 0)),
            pl.BlockSpec((1, middle, chunk), lambda p, k: (first + p, 0, k)),
        ],
        out_shape=[
            jax.ShapeDtypeStruct((total, width, double), F32),
            jax.ShapeDtypeStruct((total, middle, width), F32),
        ],
        input_output_aliases=aliases,
        compiler_params=pltpu.CompilerParams(vmem_limit_bytes=60 * 2**20),
        cost_estimate=pl.CostEstimate(
            flops=2 * count * width * pieces * (double + middle),
            bytes_accessed=pieces * width * (double + middle) * 4 + count * width * 8,
            transcendentals=0,
        ),
        name="expert_grads",
    )(*operands)


def grads_kernel(*refs, plan, count):
    inputs, outs = refs[:-count], refs[-count:]
    rows = outs[0].shape[0]
    at = 0
    for width, starts in plan:
        left, right = [], []
        for start in starts:
            pair, inputs = inputs[:4], inputs[4:]
            left += [pair[0][...], pair[1][...]]
            right += [values[:, start : start + width] for values in pair[2:]]
        total = tn(jnp.concatenate(left, axis=0), jnp.concatenate(right, axis=0))
        for k, out in enumerate(outs):
            out[:, at : at + width] = total[k * rows : (k + 1) * rows].astype(BF16)
        at += width


def grads_of(segments, count):
    plan, operands, specs = [], [], []
    rows = segments[0][1][0][0].shape[1]

    def block(values, at, width):
        return pl.BlockSpec((values.shape[0], width), lambda _: (0, at // width))

    flops = 0
    for width, products in segments:
        starts = []
        for left_mine, left_other, right_mine, right_other, at in products:
            operands += [left_mine, left_other, right_mine, right_other]
            whole = at % width > 0
            starts.append(at if whole else 0)
            specs += [block(left_mine, 0, rows)] * 2
            specs += [block(right_mine, 0 if whole else at, right_mine.shape[1] if whole else width)] * 2
            flops += 4 * rows * width * left_mine.shape[0]
        plan.append((width, tuple(starts)))
    total = sum(width for width, _ in segments)
    return pl.pallas_call(
        functools.partial(grads_kernel, plan=tuple(plan), count=count),
        grid=(1,),
        in_specs=specs,
        out_specs=[pl.BlockSpec((rows // count, total), lambda _: (0, 0))] * count,
        out_shape=[jax.ShapeDtypeStruct((rows // count, total), BF16)] * count,
        compiler_params=pltpu.CompilerParams(vmem_limit_bytes=60 * 2**20),
        cost_estimate=pl.CostEstimate(
            flops=flops, bytes_accessed=4 * rows * total, transcendentals=0
        ),
    )(*operands)


def swap_halves(values):
    width = values.shape[1]
    lane = lax.broadcasted_iota(jnp.int32, values.shape, 1)
    return jnp.where(
        lane % ROPE < ROPE // 2,
        pltpu.roll(values, width - ROPE // 2, 1),
        pltpu.roll(values, ROPE // 2, 1),
    )


def repeated(table, times):
    return jnp.concatenate([table] * times, axis=1)


def upper_lanes(shape, head):
    return lax.broadcasted_iota(jnp.int32, shape, 1) // ROPE == head % 2


def lefts_and_rights(block, half, into):
    rows, width = block.shape
    if half % 16 == 0:
        cut = block.reshape(rows // (2 * half), 2 * half, width)
        return [
            cut[:, side * half : (side + 1) * half].reshape(rows // 2, width) for side in range(into)
        ]
    out = []
    for side in range(into):
        shape = (rows // 2, rows)
        row = lax.broadcasted_iota(jnp.int32, shape, 0)
        column = lax.broadcasted_iota(jnp.int32, shape, 1)
        wanted = row // half * (2 * half) + side * half + row % half
        out.append(nn((column == wanted).astype(BF16), block).astype(BF16))
    return out


def assemble(place, refs, targets, sems, size):
    if size is None:
        return [[pltpu.make_async_copy(ref, target, sems.at[i])] for i, (ref, target) in enumerate(zip(refs, targets))]
    core, spots = place[0], (place[1], place[2])
    out = []
    for i, target in enumerate(targets):
        copies = []
        for j in range(2 * size):
            spot = spots[i] ^ (j % size)
            here = core ^ (j // size)
            view = target.at[:, spot, :, here] if i == 0 else target.at[:, :, spot, here]
            at = 2 * size * i + j
            copies.append(pltpu.make_async_copy(refs[at], view, sems.at[at]))
        out.append(copies)
    return out


def flat(target):
    values = target[...]
    return values.reshape(D, values.shape[-1])


def attention_kernel(
    hidden,
    mask,
    cosine,
    sine,
    place,
    *refs,
    half,
    size,
):
    weights, refs = refs[:-16], refs[-16:]
    (
    normed_two,
    mixed_out,
    normed_one_out,
    latent_norm_out,
    latent_in_out,
    latent_scale_out,
    query_out,
    key_value_out,
    rope_key_out,
    probs_out,
    head_out,
    gains_out,
    ups_out,
    first_ref,
    second_ref,
    sems,
    ) = refs
    copies = assemble(place, weights, (first_ref, second_ref), sems, size)
    for copy in copies[0] + copies[1]:
        copy.start()
    hidden_wide = hidden[...].astype(F32)
    norm_one = hidden_wide * inverse_rms(hidden_wide)
    for copy in copies[0]:
        copy.wait()
    first = flat(first_ref)
    tail = first[:, first.shape[1] - 128 :]
    picked = lax.broadcasted_iota(jnp.int32, (16, 128), 1) == ROPE + lax.broadcasted_iota(
        jnp.int32, (16, 128), 0
    )
    picked = picked.astype(BF16)
    gains = nt(picked, tail)
    latent_gains = nt(picked, lefts_and_rights(tail, half, 1)[0])
    gains_out[...] = jnp.concatenate(
        [gains[:2], jnp.concatenate([latent_gains[2:3], jnp.zeros((1, D - RANK), F32)], axis=1),
         jnp.zeros((5, D), F32)], axis=0
    )
    normed_one = (norm_one * gains[0:1]).astype(BF16)
    normed_one_out[...] = normed_one
    projected = nn(normed_one, first)
    nope_width = H * NOPE
    query_width = H * (NOPE + ROPE)
    latent_part = projected[:, query_width : query_width + RANK]
    latent_scale = inverse_rms(latent_part)
    latent_norm = latent_part * latent_scale
    latent_in = (latent_norm * latent_gains[2:3]).astype(BF16)
    latent_norm_out[...] = latent_norm
    latent_in_out[...] = latent_in
    latent_scale_out[...] = jnp.broadcast_to(latent_scale, latent_scale_out.shape)
    cos, sin = cosine[...], sine[...]
    rope = projected[:, nope_width:query_width]
    rope = rope * repeated(cos, H // 2) + swap_halves(rope) * repeated(sin, H // 2)
    query_out[:, :nope_width] = projected[:, :nope_width].astype(BF16)
    query_out[:, nope_width:] = rope.astype(BF16)
    key = projected[:, query_width + RANK : query_width + RANK + 128]
    key = jnp.where(upper_lanes(key.shape, 0), key, 0.0)
    key = key + pltpu.roll(key, ROPE, 1)
    rope_key = (key * cos + swap_halves(key) * sin).astype(BF16)
    rope_key_out[...] = rope_key
    for copy in copies[1]:
        copy.wait()
    second = flat(second_ref)
    for side, part in enumerate(lefts_and_rights(second[:, H * VDIM :], half, 2)):
        ups_out[side] = part
        key_value_out[:, side * UW : (side + 1) * UW] = nn(latent_in, part).astype(BF16)
    scaling = (NOPE + ROPE) ** (-0.5)
    allowed = mask[...]
    for head in range(H):
        pair = query_out[:, nope_width + head // 2 * 128 : nope_width + head // 2 * 128 + 128]
        pair = jnp.where(upper_lanes(pair.shape, head), pair, jnp.zeros_like(pair))
        query = jnp.concatenate([query_out[:, head * NOPE : (head + 1) * NOPE], pair], axis=1)
        at = head * (NOPE + VDIM)
        keys = jnp.concatenate([key_value_out[:, at : at + NOPE], rope_key], axis=1)
        scores = nt(query, keys) * scaling
        raised = jnp.exp(scores) * allowed
        probs = raised / jnp.sum(raised, axis=-1, keepdims=True)
        probs_out[head] = probs
        head_out[:, head * VDIM : (head + 1) * VDIM] = nn(
            probs.astype(BF16), key_value_out[:, at + NOPE : at + NOPE + VDIM]
        ).astype(BF16)
    mixed = hidden_wide + nt(head_out[...], second[:, : H * VDIM])
    mixed_out[...] = mixed
    normed_two[...] = (mixed * inverse_rms(mixed) * gains[1:2]).astype(BF16)


def weight_scratch(weights, size):
    if size is None:
        return [pltpu.VMEM(values.shape, BF16) for values in weights] + [
            pltpu.SemaphoreType.DMA((len(weights),))
        ]
    out = []
    for i in range(2):
        part = weights[2 * size * i].shape
        shape = (part[0], size, part[1], 2) if i == 0 else (part[0], part[1], size, 2)
        out.append(pltpu.VMEM(shape + part[2:], BF16))
    return out + [pltpu.SemaphoreType.DMA((len(weights),))]


def attention(hidden, mask, cosine, sine, place, weights, half, size):
    rows, width = hidden.shape
    query_width = H * (NOPE + ROPE)
    first_width = query_width + RANK + 128
    vmem = pl.BlockSpec(memory_space=pltpu.VMEM)
    smem = pl.BlockSpec(memory_space=pltpu.SMEM)
    shapes = [
        ((rows, width), BF16),
        ((rows, width), F32),
        ((rows, width), BF16),
        ((rows, RANK), F32),
        ((rows, RANK), BF16),
        ((rows, 128), F32),
        ((rows, query_width), BF16),
        ((rows, 2 * UW), BF16),
        ((rows, 128), BF16),
        ((H, rows, rows), F32),
        ((rows, H * VDIM), BF16),
        ((8, width), F32),
        ((2, RANK, UW), BF16),
    ]
    return pl.pallas_call(
        functools.partial(attention_kernel, half=half, size=size),
        in_specs=[vmem] * 4 + [smem] + [pl.BlockSpec(memory_space=pl.ANY)] * len(weights),
        out_specs=[vmem] * len(shapes),
        out_shape=[jax.ShapeDtypeStruct(shape, dtype) for shape, dtype in shapes],
        scratch_shapes=weight_scratch(weights, size),
        compiler_params=pltpu.CompilerParams(vmem_limit_bytes=60 * 2**20),
        cost_estimate=pl.CostEstimate(
            flops=2 * rows * width * (first_width + 3 * width),
            bytes_accessed=2 * width * (first_width + 2 * width) + 8 * rows * width,
            transcendentals=H * rows * rows,
        ),
        name="attention",
    )(hidden, mask, cosine, sine, place, *weights)


def shared_kernel(normed, cotangent, place, *refs, size):
    weights, refs = refs[:-7], refs[-7:]
    dpre, act, shared_y, shared_dx, in_ref, out_ref, sems = refs
    copies = assemble(place, weights, (in_ref, out_ref), sems, size)
    for copy in copies[0] + copies[1]:
        copy.start()
    for copy in copies[0]:
        copy.wait()
    weight_in = flat(in_ref)
    pre_act = nn(normed[...], weight_in)
    for copy in copies[1]:
        copy.wait()
    weight_out = flat(out_ref)
    act[...] = swiglu_forward(pre_act)
    dpre[...] = swiglu_backward(pre_act, nn(cotangent[...], weight_out))
    shared_y[...] = nt(act[...], weight_out)
    shared_dx[...] = nt(dpre[...], weight_in)


def shared_expert(normed, cotangent, place, weights, size, middle):
    rows, width = normed.shape
    vmem = pl.BlockSpec(memory_space=pltpu.VMEM)
    return pl.pallas_call(
        functools.partial(shared_kernel, size=size),
        in_specs=[vmem] * 2
        + [pl.BlockSpec(memory_space=pltpu.SMEM)]
        + [pl.BlockSpec(memory_space=pl.ANY)] * len(weights),
        out_specs=[vmem] * 4,
        out_shape=[
            jax.ShapeDtypeStruct((rows, 2 * middle), BF16),
            jax.ShapeDtypeStruct((rows, middle), BF16),
            jax.ShapeDtypeStruct((rows, width), F32),
            jax.ShapeDtypeStruct((rows, width), F32),
        ],
        scratch_shapes=weight_scratch(weights, size),
        compiler_params=pltpu.CompilerParams(vmem_limit_bytes=60 * 2**20),
        cost_estimate=pl.CostEstimate(
            flops=12 * rows * width * middle,
            bytes_accessed=6 * width * middle,
            transcendentals=rows * middle,
        ),
        name="shared_expert",
    )(normed, cotangent, place, *weights)


def combined_kernel(mixed, shared_y, gates_high, gates_low, rows, out):
    routed = tn(gates_high[...], rows[...]) + tn(gates_low[...], rows[...])
    out[...] = (mixed[...] + shared_y[...] + routed).astype(BF16)


def combined(mixed, shared_y, gates_high, gates_low, rows):
    vmem = pl.BlockSpec(memory_space=pltpu.VMEM)
    return pl.pallas_call(
        combined_kernel,
        in_specs=[vmem] * 5,
        out_specs=vmem,
        out_shape=jax.ShapeDtypeStruct(mixed.shape, BF16),
        compiler_params=pltpu.CompilerParams(vmem_limit_bytes=60 * 2**20),
        cost_estimate=pl.CostEstimate(
            flops=4 * rows.size * mixed.shape[0], bytes_accessed=2 * rows.size, transcendentals=0
        ),
        name="combined",
    )(mixed, shared_y, gates_high, gates_low, rows)


def mixed_back_kernel(*refs):
    count = (len(refs) - 7) // 2
    shared_dx, out_grad, mixed, gains = refs[:4]
    selectors, back = refs[4 : 4 + count], refs[4 + count : 4 + 2 * count]
    grad_mixed_out, mixed_low, gain_out = refs[4 + 2 * count :]
    grad = shared_dx[...]
    for selector, rows in zip(selectors, back):
        grad = grad + tn(selector[...], rows[...])
    scale = inverse_rms(mixed[...])
    norm_two = mixed[...] * scale
    gain_out[...] = jnp.broadcast_to(jnp.sum(grad * norm_two, axis=0, keepdims=True), gain_out.shape)
    grad_norm = grad * gains[1:2]
    grad_mixed = out_grad[...].astype(F32) + scale * (
        grad_norm - norm_two * jnp.mean(grad_norm * norm_two, axis=-1, keepdims=True)
    )
    grad_mixed_out[...] = grad_mixed
    mixed_low[...] = grad_mixed.astype(BF16)


def mixed_back(shared_dx, out_grad, mixed, gains, selectors, back):
    rows, width = mixed.shape
    vmem = pl.BlockSpec(memory_space=pltpu.VMEM)
    total = sum(values.shape[0] for values in back)
    return pl.pallas_call(
        mixed_back_kernel,
        in_specs=[vmem] * (4 + 2 * len(back)),
        out_specs=[vmem] * 3,
        out_shape=[
            jax.ShapeDtypeStruct((rows, width), F32),
            jax.ShapeDtypeStruct((rows, width), BF16),
            jax.ShapeDtypeStruct((8, width), F32),
        ],
        compiler_params=pltpu.CompilerParams(vmem_limit_bytes=60 * 2**20),
        cost_estimate=pl.CostEstimate(
            flops=2 * rows * width * total, bytes_accessed=2 * total * width, transcendentals=0
        ),
        name="mixed_back",
    )(shared_dx, out_grad, mixed, gains, *selectors, *back)


def attention_back_kernel(
    hidden,
    grad_mixed,
    mixed_low,
    cosine,
    sine,
    latent_norm,
    latent_scale,
    query,
    key_value,
    rope_key,
    probs,
    head_out,
    gains,
    ups,
    place,
    *refs,
    size,
):
    weights, refs = refs[:-6], refs[-6:]
    back, input_grad, gain_out, first_ref, second_ref, sems = refs
    copies = assemble(place, weights, (first_ref, second_ref), sems, size)
    for copy in copies[1] + copies[0]:
        copy.start()
    grad_projected = back.at[:, 2 * UW :]
    grad_key_value = back.at[:, : 2 * UW]
    for copy in copies[1]:
        copy.wait()
    output = flat(second_ref)[:, : H * VDIM]
    rows = hidden.shape[0]
    nope_width = H * NOPE
    query_width = H * (NOPE + ROPE)
    scaling = (NOPE + ROPE) ** (-0.5)
    heads = nn(mixed_low[...], output).astype(BF16)
    rope_sum = jnp.zeros((rows, 128), F32)
    rope_grads = []
    for head in range(H):
        grad_head = heads[:, head * VDIM : (head + 1) * VDIM]
        at = head * (NOPE + VDIM)
        weights_here = probs[head]
        own_lanes = upper_lanes((rows, 128), head)
        pair = query[:, nope_width + head // 2 * 128 : nope_width + head // 2 * 128 + 128]
        pair = jnp.where(own_lanes, pair, jnp.zeros_like(pair))
        query_here = jnp.concatenate([query[:, head * NOPE : (head + 1) * NOPE], pair], axis=1)
        keys = jnp.concatenate([key_value[:, at : at + NOPE], rope_key[...]], axis=1)
        grad_probs = nt(grad_head, key_value[:, at + NOPE : at + NOPE + VDIM])
        delta = jnp.sum(
            grad_head.astype(F32) * head_out[:, head * VDIM : (head + 1) * VDIM].astype(F32),
            axis=-1,
            keepdims=True,
        )
        grad_scores = (weights_here * (grad_probs - delta) * scaling).astype(BF16)
        grad_query = nn(grad_scores, keys)
        grad_projected[:, head * NOPE : (head + 1) * NOPE] = grad_query[:, :NOPE].astype(BF16)
        rope_grads.append(jnp.where(own_lanes, grad_query[:, NOPE:], 0.0))
        grad_keys = tn(grad_scores, query_here)
        rope_sum = rope_sum + grad_keys[:, NOPE:]
        grad_key_value[:, at : at + NOPE] = grad_keys[:, :NOPE].astype(BF16)
        grad_key_value[:, at + NOPE : at + NOPE + VDIM] = tn(
            weights_here.astype(BF16), grad_head
        ).astype(BF16)
    cos, sin = cosine[...], sine[...]
    rope = jnp.concatenate(
        [rope_grads[2 * pair] + rope_grads[2 * pair + 1] for pair in range(H // 2)], axis=1
    )
    rope = rope * repeated(cos, H // 2) - swap_halves(rope) * repeated(sin, H // 2)
    grad_projected[:, nope_width:query_width] = rope.astype(BF16)
    key = rope_sum + pltpu.roll(rope_sum, ROPE, 1)
    key = key * cos - swap_halves(key) * sin
    key = jnp.where(upper_lanes(key.shape, 0), key, 0.0)
    grad_projected[:, query_width + RANK :] = key.astype(BF16)
    grad_latent_in = nt(grad_key_value[:, :UW], ups[0]) + nt(grad_key_value[:, UW:], ups[1])
    norm = latent_norm[...]
    latent_gain_grad = jnp.sum(grad_latent_in * norm, axis=0, keepdims=True)
    grad_norm = grad_latent_in * gains[2:3, :RANK]
    grad_latent = latent_scale[:, 0:1] * (
        grad_norm - norm * jnp.mean(grad_norm * norm, axis=-1, keepdims=True)
    )
    grad_projected[:, query_width : query_width + RANK] = grad_latent.astype(BF16)
    for copy in copies[0]:
        copy.wait()
    grad_normed = nt(grad_projected[...], flat(first_ref))
    hidden_wide = hidden[...].astype(F32)
    scale = inverse_rms(hidden_wide)
    norm_one = hidden_wide * scale
    gain_out[...] = jnp.concatenate(
        [
            jnp.sum(grad_normed * norm_one, axis=0, keepdims=True),
            jnp.concatenate([latent_gain_grad, jnp.zeros((1, D - RANK), F32)], axis=1),
            jnp.zeros((6, D), F32),
        ],
        axis=0,
    )
    grad_norm = grad_normed * gains[0:1]
    input_grad[...] = grad_mixed[...] + scale * (
        grad_norm - norm_one * jnp.mean(grad_norm * norm_one, axis=-1, keepdims=True)
    )


def attention_back(operands, place, weights, size):
    hidden = operands[0]
    rows, width = hidden.shape
    first_width = H * (NOPE + ROPE) + RANK + 128
    vmem = pl.BlockSpec(memory_space=pltpu.VMEM)
    return pl.pallas_call(
        functools.partial(attention_back_kernel, size=size),
        in_specs=[vmem] * len(operands)
        + [pl.BlockSpec(memory_space=pltpu.SMEM)]
        + [pl.BlockSpec(memory_space=pl.ANY)] * len(weights),
        out_specs=[vmem] * 3,
        out_shape=[
            jax.ShapeDtypeStruct((rows, first_width + 2 * UW), BF16),
            jax.ShapeDtypeStruct((rows, width), F32),
            jax.ShapeDtypeStruct((8, width), F32),
        ],
        scratch_shapes=weight_scratch(weights, size),
        compiler_params=pltpu.CompilerParams(vmem_limit_bytes=60 * 2**20),
        cost_estimate=pl.CostEstimate(
            flops=2 * rows * width * (first_width + 3 * width),
            bytes_accessed=2 * width * (first_width + 2 * width) + 8 * rows * width,
            transcendentals=0,
        ),
        name="attention_back",
    )(*operands, place, *weights)


def after_kernel(values, late, out):
    pass


def after(values, late):
    anywhere = pl.BlockSpec(memory_space=pl.ANY)
    return pl.pallas_call(
        after_kernel,
        in_specs=[anywhere, anywhere],
        out_specs=anywhere,
        out_shape=jax.ShapeDtypeStruct(values.shape, values.dtype),
        input_output_aliases={0: 0},
        cost_estimate=pl.CostEstimate(flops=0, bytes_accessed=0, transcendentals=0),
        name="after",
    )(values, late)


def axes_of(devices):
    return {32: ((8, 4), (4, 2), (2, 2)), 128: ((32, 4), (8, 4), (2, 4))}[devices]


def swap_with(values, devices, offset):
    return lax.ppermute(values, "fsdp", [(i, i ^ offset) for i in range(devices)])


def pick(values, index, axis):
    return lax.dynamic_index_in_dim(values, index, axis, keepdims=False)


def row_order(devices, axis, half=None):
    me = lax.axis_index("fsdp")
    own = D // devices
    axes = axes_of(devices)
    to = jnp.arange(D, dtype=jnp.int32)
    chip_row = to % (D // 2)
    stride, size = axes[axis]
    block = chip_row // (D // 2 // size)
    rest = chip_row % (D // 2 // size) // own
    device = (me % 2) ^ (to // (D // 2))
    device = device + (((me // stride) % size) ^ block) * stride
    for other in (2, 1, 0):
        if other != axis:
            device = device + rest % axes[other][1] * axes[other][0]
            rest = rest // axes[other][1]
    row = to % own
    if half is None:
        source = device * own + row
        return (jnp.arange(D, dtype=jnp.int32)[:, None] == source[None, :]).astype(BF16)
    source = device * half + row % half
    hit = jnp.arange(D // 2, dtype=jnp.int32)[:, None] == source[None, :]
    return [(hit & (row // half == side)[None, :]).astype(BF16) for side in range(2)]


def scatter_sum(blocks, devices, order, late=()):
    me = lax.axis_index("fsdp")
    axes = axes_of(devices)
    left = [0, 1, 2]
    values = None
    for axis in order:
        stride, size = axes[axis]
        at = left.index(axis)
        left.remove(axis)
        mine = (me // stride) % size
        if values is not None:
            blocks = [pick(values, mine ^ k, at) for k in range(size)]
        total = blocks[0]
        if late:
            for values in late[0]:
                total = after(total, values)
            late = late[1:]
        total = total.astype(F32)
        parts = [swap_with(blocks[k], devices, k * stride) for k in range(1, size)]
        for part in parts:
            total = total + part.astype(F32)
        values = total if not left else total.astype(BF16)
        if values.ndim == 2 and left:
            values = values.reshape(
                *(axes[other][1] for other in left), D // devices, values.shape[-1]
            )
    return values


def gather_start(shard, devices, order):
    me = lax.axis_index("fsdp")
    axes = axes_of(devices)
    have = []
    values = shard
    for axis in order:
        stride, size = axes[axis]
        mine = (me // stride) % size
        at = sum(other < axis for other in have)
        have.append(axis)
        parts = [values] + [swap_with(values, devices, k * stride) for k in range(1, size)]
        if len(have) < 3:
            values = placed_along(parts, mine, at)
    return (parts, mine, at)


def placed_along(parts, mine, at):
    if len(parts) == 2:
        return jnp.where(mine == 0, jnp.stack(parts, at), jnp.stack(parts[::-1], at))
    shape = parts[0].shape
    values = jnp.zeros(shape[:at] + (len(parts),) + shape[at:], parts[0].dtype)
    for k, part in enumerate(parts):
        values = lax.dynamic_update_index_in_dim(values, part, mine ^ k, at)
    return values


def gather_finish(started, devices):
    parts, mine, at = started
    values = placed_along(parts, mine, at)
    other = swap_with(values, devices, 1)
    first = lax.axis_index("fsdp") % 2 == 0
    pair = jnp.where(first, jnp.stack([values, other], 3), jnp.stack([other, values], 3))
    return pair.reshape(-1, values.shape[-1])


def body(
    hidden_in,
    out_grad,
    doc_ids,
    routes,
    gate_values,
    attn_gain,
    query_proj,
    latent_proj,
    latent_gain,
    latent_up,
    output_proj,
    ffn_gain,
    shared_in,
    shared_out,
    expert_in,
    expert_out,
):
    devices = lax.axis_size("fsdp")
    rows_here = hidden_in.shape[0]
    own = D // devices
    half = own // 2
    me = lax.axis_index("fsdp")

    along_x, along_y = row_order(devices, 2), row_order(devices, 1)
    sides_x, sides_y = row_order(devices, 2, half), row_order(devices, 1, half)

    def mine_and_other(columns, order):
        placed = matmul(columns, order).astype(BF16)
        return (placed[:, : D // 2], swap_with(placed[:, D // 2 :], devices, 1))

    spare = 128 - LW % 128
    query_width, output_width = query_proj.shape[1], output_proj.shape[1]
    gain_at = query_width + LW
    output_at = gain_at + spare
    by_head = query_proj.reshape(own, H, NOPE + ROPE)
    started = [
        gather_start(
            jnp.concatenate(
                [
                    by_head[:, :, :NOPE].reshape(own, H * NOPE),
                    by_head[:, :, NOPE:].reshape(own, H * ROPE),
                    latent_proj,
                    attn_gain[:, None],
                    ffn_gain[:, None],
                    jnp.concatenate([latent_gain, jnp.zeros_like(latent_gain)])[:, None],
                    jnp.zeros((own, spare - 3), BF16),
                ],
                axis=1,
            ),
            devices,
            (0, 2, 1),
        ),
        gather_start(
            jnp.concatenate(
                [output_proj, jnp.concatenate([latent_up[:, :UW], latent_up[:, UW:]], axis=0)],
                axis=1,
            ),
            devices,
            (0, 1, 2),
        ),
    ]
    place = jnp.stack([me % 2, started[0][1], started[1][1]]).astype(jnp.int32)
    size = len(started[0][0]) if own % 16 == 0 else None

    def gathered_parts(started):
        out = []
        for begun in started:
            if size is None:
                out.append(gather_finish(begun, devices))
            else:
                out += begun[0] + [swap_with(part, devices, 1) for part in begun[0]]
        return out

    attention_weights = gathered_parts(started)

    per_device = expert_in.shape[0]
    pieces = 2 if per_device % 2 == 0 else 1
    units = 2 * EXPERTS // pieces
    local_units = units // devices
    token = jnp.arange(rows_here, dtype=jnp.int32)
    earlier = (token[None, :] < token[:, None]).astype(BF16)

    def routing(names, values, base, count):
        unit_expert = (base + jnp.arange(count, dtype=jnp.int32)) // (2 // pieces)
        named = names[:, :, None] == unit_expert[None, None, :]
        hits = jnp.any(named, axis=1)
        gates = jnp.sum(jnp.where(named, values[:, :, None], 0.0), axis=1)
        slots = matmul(earlier, hits.astype(BF16)).astype(jnp.int32)
        return (jnp.where(hits, slots, CAP).T, gates.T)

    slots, gates = routing(routes, gate_values, 0, units)
    chosen = slots[:, None, :] == jnp.arange(CAP, dtype=jnp.int32)[None, :, None]
    gate_wide = jnp.where(chosen, gates[:, None, :], 0.0).reshape(units * CAP, rows_here)
    gate_rows = jnp.sum(gate_wide, axis=-1, keepdims=True)
    selector = chosen.astype(BF16)
    unit_selector = selector.reshape(devices, local_units, CAP, rows_here)
    unit_selector = [
        unit_selector[:, u].reshape(devices * CAP, rows_here) for u in range(local_units)
    ]
    selector = selector.reshape(units * CAP, rows_here)

    def exchange(rows):
        return lax.all_to_all(rows, "fsdp", split_axis=0, concat_axis=0, tiled=True)

    def exchange_unit(rows):
        return exchange(rows.reshape(devices, CAP, D)).reshape(devices * CAP, D)

    grads_out = (gate_rows * matmul(selector, out_grad)).astype(BF16)
    grad_rows = exchange(grads_out.reshape(devices, local_units * CAP, D))
    grad_rows = grad_rows.reshape(devices, local_units, CAP, D)

    allowed, cosine_table, sine_table = tables(doc_ids[0])
    cosine_lanes = jnp.concatenate([cosine_table] * 4, axis=1)
    sine_lanes = jnp.concatenate([-sine_table, sine_table] * 2, axis=1)
    (
        normed_two,
        mixed,
        normed_one,
        latent_norm,
        latent_in,
        latent_scale,
        queries,
        key_values,
        rope_key,
        probs,
        head_out,
        gain_rows,
        ups,
    ) = attention(hidden_in, allowed.astype(F32), cosine_lanes, sine_lanes, place, attention_weights, half, size)

    rows_out = [matmul(unit_selector[u], normed_two).astype(BF16) for u in range(local_units)]
    rows_in = []
    for rows in rows_out:
        rows_in.append(exchange_unit(rows))

    shared_rows = after(normed_two, rows_out[0])
    started = [
        gather_start(shared_in, devices, (0, 2, 1)), gather_start(shared_out, devices, (0, 1, 2))
    ]
    shared_weights = gathered_parts(started)
    middle = shared_out.shape[1]
    grad_shared_pre, shared_act, shared_y, shared_dx = shared_expert(
        shared_rows, out_grad, place, shared_weights, size, middle
    )
    middle = shared_out.shape[1]
    dpre_pair = (grad_shared_pre, swap_with(grad_shared_pre, devices, 1))
    act_pair = (shared_act, swap_with(shared_act, devices, 1))
    size_x, size_y = axes_of(devices)[2][1], axes_of(devices)[1][1]
    normed_left = [mine_and_other(normed_two, along) for along in (along_x, along_y)]
    cotangent_left = mine_and_other(out_grad, along_x)
    blocks_x = grads_of(
        (
            (middle, ((*normed_left[0], *dpre_pair, 0),)),
            (middle, ((*cotangent_left, *act_pair, 0),)),
        ),
        size_x,
    )
    blocks_y = grads_of(((middle, ((*normed_left[1], *dpre_pair, middle),)),), size_y)
    shared_blocks = (blocks_x, blocks_y)

    back_dx, back_out, saved = [], [], []
    for u in range(local_units):
        dx_rows, y_rows, activation, grad_pre = experts(
            rows_in[u], grad_rows, expert_in, expert_out, u, pieces
        )
        back_dx.append(exchange_unit(dx_rows))
        back_out.append(y_rows.reshape(devices, CAP, D))
        saved.append((activation, grad_pre))
    back_out = jnp.concatenate(back_out, axis=1)
    for rows in back_dx:
        back_out = after(back_out, rows)
    back_out = exchange(back_out).reshape(units * CAP, D)

    grad_mixed, mixed_low, ffn_gain_grad = mixed_back(
        shared_dx, out_grad, mixed, gain_rows, unit_selector, back_dx
    )

    heads_pair = (head_out, swap_with(head_out, devices, 1))
    first_left = mine_and_other(normed_one, along_y)
    up_left = [mine_and_other(latent_in, side) for side in sides_x]
    output_left = mine_and_other(mixed_low, along_x)
    back, input_grad, other_gain_grads = attention_back(
        (
            hidden_in,
            grad_mixed,
            mixed_low,
            cosine_lanes,
            sine_lanes,
            latent_norm,
            latent_scale,
            queries,
            key_values,
            rope_key,
            probs,
            head_out,
            gain_rows,
            ups,
        ),
        place,
        attention_weights,
        size,
    )
    back_pair = (back, swap_with(back, devices, 1))
    gain_grads = jnp.concatenate(
        [other_gain_grads[:1], ffn_gain_grad[:1], jnp.zeros((6, D), F32)], axis=0
    ).astype(BF16)
    placed = matmul(gain_grads, along_y) + jnp.pad(
        matmul(other_gain_grads[1:7, :RANK].astype(BF16), sides_y[0]), ((2, 0), (0, 0))
    )
    placed = placed.astype(BF16)
    gain_left = (placed[:, : D // 2], swap_with(placed[:, D // 2 :], devices, 1))
    row = jnp.arange(8, dtype=jnp.int32)[:, None]
    lane = jnp.arange(output_at, dtype=jnp.int32)[None, :]
    gain_right = ((row < 3) & (lane == gain_at + row)).astype(BF16)
    blocks_y = grads_of(
        (
            (
                output_at,
                ((*first_left, *back_pair, 2 * UW), (*gain_left, gain_right, gain_right, 0)),
            ),
        ),
        size_y,
    )
    owned_first = scatter_sum(blocks_y, devices, (1, 2, 0))
    blocks_x = grads_of(
        (
            (output_width, ((*output_left, *heads_pair, 0),)),
            (UW, tuple((*up_left[i], *back_pair, i * UW) for i in range(2))),
        ),
        size_x,
    )
    gates_high = lax.reduce_precision(gate_wide, 8, 7)
    gates_low = (gate_wide - gates_high).astype(BF16)
    layer_out = combined(mixed, shared_y, gates_high.astype(BF16), gates_low, back_out)
    owned_second = scatter_sum(blocks_x, devices, (2, 1, 0))
    shared_late = ((blocks_x[0], blocks_y[0]),)
    owned_gate_out = scatter_sum(shared_blocks[0], devices, (2, 1, 0), shared_late)
    owned_up_in = scatter_sum(shared_blocks[1], devices, (1, 2, 0), shared_late)
    owned_output, owned_up = owned_second[:, :output_width], owned_second[:, output_width:]
    held = None
    for u in range(local_units):
        held = expert_grads(
            rows_in[u], grad_rows, *saved[u], per_device, u, blocks_x[-1] if u else None, held
        )
    owned_query = jnp.concatenate(
        [
            owned_first[:, : H * NOPE].reshape(own, H, NOPE),
            owned_first[:, H * NOPE : query_width].reshape(own, H, ROPE),
        ],
        axis=2,
    ).reshape(own, query_width)
    return (
        layer_out,
        input_grad,
        owned_first[:, gain_at],
        owned_query,
        owned_first[:, query_width:gain_at],
        owned_first[:half, gain_at + 2],
        jnp.concatenate([owned_up[:half], owned_up[half:]], axis=1),
        owned_output,
        owned_first[:, gain_at + 1],
        jnp.concatenate([owned_gate_out[:, :middle], owned_up_in], axis=1),
        owned_gate_out[:, middle:],
        held[0],
        held[1],
    )


def solution(mesh):
    rows = P("fsdp", None)
    flat = P("fsdp")
    cube = P("fsdp", None, None)
    in_specs = (rows,) * 5 + (flat, rows, rows, flat, rows, rows, flat, rows, rows, cube, cube)
    out_specs = (rows, rows, flat, rows, rows, flat, rows, rows, flat, rows, rows, cube, cube)
    return jax.shard_map(body, mesh=mesh, in_specs=in_specs, out_specs=out_specs, check_vma=False)
```
